512 devices in a mesh: dp: 8 (over z_hi, core), tensor: 64 (over z_lo, y, x).
Axes of the slice: x: 4, y: 8, z: 8 (z_hi: 4, z_lo: 2; z = z_hi * 2 + z_lo), core: 2. Of those that a mesh axis runs over, the one named last changes fastest.
Arguments:
- tokens: bfloat16 [2048, 4096], P(('dp', 'tensor')), may hold values from -6 to 6
- cotangent: bfloat16 [2048, 4096], P(('dp', 'tensor')), may hold values from -3 to 3
- gate_weight: bfloat16 [4096, 16384], P(None, 'tensor'), may hold values from -0.09375 to 0.09375
- up_weight: bfloat16 [4096, 16384], P(None, 'tensor'), may hold values from -0.09375 to 0.09375
- down_weight: bfloat16 [16384, 4096], P('tensor', 'dp'), may hold values from -0.75 to 0.75
Outputs:
- input_grad: bfloat16 [2048, 4096], P(('dp', 'tensor'))
- down_grad: float32 [16384, 4096], P('tensor', 'dp')
The draws below stay inside these ranges and needn't reach their ends.
All inputs are finite; a program needn't handle non-finite values.
Results may differ from the reference program's by a relative error of at most 0.015.
Values may be sent and summed in bfloat16 or wider, within the bound.
No kernel may reach another device: no remote copies, remote signals or barrier semaphores. Data moves between devices by JAX's collectives and lax.ppermute only.
A program may use at most 64 MiB of HBM per device.

```python
import jax
import jax.numpy as jnp
from jax import lax

D = 4096
FF = 16384
GROUP_ROWS = 256
TOKENS = 2048
N_DP = 8


def raised(result, rng, source, target, shards_of, factor):
    def block_of(dim):
        return (jnp.arange(result.shape[dim]) // (result.shape[dim] // shards_of)).reshape((-1,) + (1,) * (result.ndim - 1 - dim))

    first = jax.random.permutation(rng, shards_of)[block_of(target)]
    far = (block_of(target) + shards_of // 2) % shards_of
    return jnp.where((block_of(source) == first) | (block_of(source) == far), factor * result, result)


def block_levels(stream_key, shape, pieces, low, largest):
    def one(position, shards_of):
        heights = jax.random.uniform(jax.random.fold_in(jax.random.fold_in(stream_key, 6), position), (shards_of,), jnp.float32, low / len(pieces), largest / len(pieces))
        return jnp.repeat(jnp.exp(heights), shape[position] // shards_of).reshape((-1,) + (1,) * (len(shape) - position - 1))

    gain = one(*pieces[0])
    for cut in pieces[1:]:
        gain = gain * one(*cut)
    return gain


def gaussian(rng, shape, width, reach, cuts=(), kind=jnp.bfloat16):
    entries = width * jax.random.normal(rng, shape, jnp.float32)
    if cuts:
        entries = entries * block_levels(rng, shape, cuts, -0.22, 0.18)
    return jnp.clip(entries, -reach, reach).astype(kind)


def heavy_noise(key, extent, spread, bound, cuts, heavy, kind=jnp.bfloat16):
    values = spread * jax.random.normal(key, extent, jnp.float32)
    if cuts:
        values = values * block_levels(key, extent, cuts, -0.22, 0.18)
    return jnp.clip(raised(values, jax.random.fold_in(key, 3), *heavy), -bound, bound).astype(kind)


def setup_inputs(seed: int = 0) -> dict:
    key_list = jax.random.split(jax.random.key(seed), 6)
    return {
        "tokens": gaussian(key_list[0], (TOKENS, D), 1.0, 6.0, ((0, 512),)),
        "cotangent": heavy_noise(key_list[1], (TOKENS, D), 0.125, 3.0, ((0, 512),), (0, 1, 512, 6.0)),
        "gate_weight": gaussian(key_list[2], (D, FF), D ** -0.5, 0.09375, ((1, 64),)),
        "up_weight": gaussian(key_list[3], (D, FF), D ** -0.5, 0.09375, ((1, 64),)),
        "down_weight": gaussian(key_list[4], (FF, D), (D // 64) ** -0.5, 0.75, ((0, 64), (1, 8))),
    }


def reference(tokens, cotangent, gate_weight, up_weight, down_weight):
    gate_pre = jnp.dot(tokens, gate_weight, preferred_element_type=jnp.float32)
    up_pre = jnp.dot(tokens, up_weight, preferred_element_type=jnp.float32)
    d_hidden = lax.dot_general(cotangent, down_weight, (((1,), (1,)), ((), ())), preferred_element_type=jnp.float32)
    sigma = jax.nn.sigmoid(gate_pre)
    silu_val = gate_pre * sigma
    hidden = (silu_val * up_pre).astype(jnp.bfloat16)
    d_up = (d_hidden * silu_val).astype(jnp.bfloat16)
    d_gate = (d_hidden * up_pre * sigma * (1.0 + gate_pre * (1.0 - sigma))).astype(jnp.bfloat16)
    input_grad = lax.dot_general(d_gate, gate_weight, (((1,), (1,)), ((), ())), preferred_element_type=jnp.float32)
    input_grad = input_grad + lax.dot_general(d_up, up_weight, (((1,), (1,)), ((), ())), preferred_element_type=jnp.float32)
    input_grad = input_grad.astype(jnp.bfloat16)
    group_rows = GROUP_ROWS
    down_grad = jnp.zeros((FF, D), jnp.float32)
    for group in range(N_DP):
        hid_rows = hidden[group * group_rows:(group + 1) * group_rows]
        cot_rows = cotangent[group * group_rows:(group + 1) * group_rows]
        partial_value = jnp.dot(hid_rows.T, cot_rows, preferred_element_type=jnp.float32)
        rounded = lax.optimization_barrier(partial_value.astype(jnp.bfloat16))
        down_grad = down_grad + rounded.astype(jnp.float32)
    return input_grad, down_grad
```

```python
import jax
import jax.numpy as jnp
from jax import lax
from jax.sharding import PartitionSpec as P


def contract(a, b, ca, cb):
    return lax.dot_general(a, b, (((ca,), (cb,)), ((), ())), preferred_element_type=jnp.float32)


def on_device(tokens, cotangent, gate_weight, up_weight, down_weight):
    n = lax.axis_size("tensor")
    rows, d = tokens.shape
    down_rows = lax.all_gather(down_weight, "dp", axis=1, tiled=True)
    both = jnp.concatenate([tokens, cotangent], axis=0)
    sent = jnp.broadcast_to(both[None], (n, 2 * rows, d))
    got = lax.all_to_all(sent, "tensor", 0, 0)
    input_piece = got[:, :rows].reshape(n * rows, d)
    cot_piece = got[:, rows:].reshape(n * rows, d)
    gate_piece = contract(input_piece, gate_weight, 1, 0)
    up_piece = contract(input_piece, up_weight, 1, 0)
    sigma = jax.nn.sigmoid(gate_piece)
    silu_val = gate_piece * sigma
    hidden = (silu_val * up_piece).astype(jnp.bfloat16)
    partial_value = contract(hidden, cot_piece, 0, 0)
    down_grad = lax.psum_scatter(
        partial_value.astype(jnp.bfloat16), "dp", scatter_dimension=1, tiled=True
    ).astype(jnp.float32)
    d_hidden = contract(cot_piece, down_rows, 1, 1)
    d_up = (d_hidden * silu_val).astype(jnp.bfloat16)
    d_gate = (d_hidden * up_piece * sigma * (1.0 + gate_piece * (1.0 - sigma))).astype(jnp.bfloat16)
    term = contract(d_gate, gate_weight, 1, 1) + contract(d_up, up_weight, 1, 1)
    parts = lax.all_to_all(term.astype(jnp.bfloat16).reshape(n, rows, d), "tensor", 0, 0)
    input_grad = jnp.sum(parts.astype(jnp.float32), axis=0).astype(jnp.bfloat16)
    return (input_grad, down_grad)


def solution(mesh):
    placed = (
        P(("dp", "tensor"), None),
        P(("dp", "tensor"), None),
        P(None, "tensor"),
        P(None, "tensor"),
        P("tensor", "dp"),
    )
    return jax.shard_map(
        on_device,
        mesh=mesh,
        in_specs=placed,
        out_specs=(P(("dp", "tensor"), None), P("tensor", "dp")),
        check_vma=False,
    )
```

```python
import jax
import jax.numpy as jnp
from jax import lax
from jax.sharding import Mesh, PartitionSpec as P

BF16 = jnp.bfloat16
F32 = jnp.float32
DP = ("zh", "c")
PLANE = ("y", "x")
TENSOR = ("zl", "y", "x")


def contract(a, b, ca, cb):
    return lax.dot_general(a, b, (((ca,), (cb,)), ((), ())), preferred_element_type=F32)


def swap(value, axis):
    return lax.ppermute(value, axis, [(0, 1), (1, 0)])


def spread(block, axis):
    n = lax.axis_size(axis)
    return lax.all_to_all(jnp.broadcast_to(block[None], (n, *block.shape)), axis, 0, 0)


def on_device(tokens, cotangent, gate_weight, up_weight, down_weight):
    n_dp, n_plane = lax.axis_size(DP), lax.axis_size(PLANE)
    rows, d = tokens.shape
    feats = d // n_dp
    hid = gate_weight.shape[1]
    half = n_plane * rows
    first = lax.axis_index("c") == 0

    mine = swap(jnp.where(first, gate_weight, up_weight), "zl")
    other = swap(mine, "c")
    down_pair = jnp.concatenate([down_weight, swap(down_weight, "zl")], axis=0)

    cot = cotangent.reshape(rows, n_dp, feats).swapaxes(0, 1)
    cot = lax.all_to_all(cot, DP, 0, 0)
    cot = spread(cot.reshape(n_dp * rows, feats), PLANE)
    cot = cot.reshape(n_plane, n_dp, rows, feats).swapaxes(0, 1).reshape(n_dp * half, feats)

    part = contract(cot, down_pair, 1, 1).astype(BF16)
    part = part.reshape(lax.axis_size("zh"), 2, half, 2 * hid).swapaxes(0, 1)
    part = lax.all_to_all(part, "c", 0, 0)
    part = (part[0].astype(F32) + part[1].astype(F32)).astype(BF16)
    part = lax.all_to_all(part, "zh", 0, 0)
    d_hidden = jnp.sum(part.astype(F32), axis=0)

    tok = spread(tokens, PLANE).reshape(half, d)
    pre_mine = contract(tok, mine, 1, 0)
    pre_other = contract(tok, other, 1, 0)
    gate = jnp.concatenate(
        [contract(tok, gate_weight, 1, 0), jnp.where(first, pre_mine, pre_other)], axis=1
    )
    up = jnp.concatenate(
        [contract(tok, up_weight, 1, 0), jnp.where(first, pre_other, pre_mine)], axis=1
    )
    sigma = jax.nn.sigmoid(gate)
    silu = gate * sigma
    hidden = (silu * up).astype(BF16)
    d_up = (d_hidden * silu).astype(BF16)
    d_gate = (d_hidden * up * sigma * (1.0 + gate * (1.0 - sigma))).astype(BF16)

    hidden_all = spread(hidden, "zh")
    hidden_all = spread(hidden_all, "c").swapaxes(0, 1).reshape(n_dp * half, 2 * hid)

    dg, du = d_gate[:, hid:], d_up[:, hid:]
    term = (
        contract(d_gate[:, :hid], gate_weight, 1, 1)
        + contract(d_up[:, :hid], up_weight, 1, 1)
        + contract(jnp.where(first, dg, du), mine, 1, 1)
        + contract(jnp.where(first, du, dg), other, 1, 1)
    )
    parts = lax.all_to_all(term.astype(BF16).reshape(n_plane, rows, d), PLANE, 0, 0)
    input_grad = jnp.sum(parts.astype(F32), axis=0).astype(BF16)

    grads = contract(hidden_all, cot, 0, 0)
    down_grad = grads[:hid] + swap(grads[hid:].astype(BF16), "zl").astype(F32)
    return (input_grad, down_grad)


def solution(mesh):
    fine = Mesh(mesh.devices.reshape(4, 2, 2, 8, 4), ("zh", "c", "zl", "y", "x"))
    placed = (
        P((*DP, *TENSOR), None),
        P((*DP, *TENSOR), None),
        P(None, TENSOR),
        P(None, TENSOR),
        P(TENSOR, DP),
    )
    return jax.shard_map(
        on_device,
        mesh=fine,
        in_specs=placed,
        out_specs=(P((*DP, *TENSOR), None), P(TENSOR, DP)),
        check_vma=False,
    )
```

```python
import jax
import jax.numpy as jnp
from jax import lax
from jax.sharding import Mesh, PartitionSpec as P

BF16 = jnp.bfloat16
F32 = jnp.float32
DP = ("zh", "c")
TENSOR = ("zl", "y", "x")


def contract(a, b, ca, cb):
    return lax.dot_general(a, b, (((ca,), (cb,)), ((), ())), preferred_element_type=F32)


def swap(value, axis):
    return lax.ppermute(value, axis, [(0, 1), (1, 0)])


def shift(value, axis, k):
    n = lax.axis_size(axis)
    return lax.ppermute(value, axis, [(i, (i + k) % n) for i in range(n)])


def spread(block, axis):
    n = lax.axis_size(axis)
    return lax.all_to_all(jnp.broadcast_to(block[None], (n, *block.shape)), axis, 0, 0)


def on_device(tokens, cotangent, gate_weight, up_weight, down_weight):
    nz, ny, nx = lax.axis_size("zh"), lax.axis_size("y"), lax.axis_size("x")
    rows, d = tokens.shape
    feats = d // (2 * nz)
    wide = d // 2
    hid = gate_weight.shape[1]
    half = nx * ny * rows
    first = lax.axis_index("c") == 0
    low = lax.axis_index("zl") == 0

    mine = swap(jnp.where(first, gate_weight, up_weight), "zl")
    down_rows = lax.all_gather(down_weight, ("zh", "zl"), axis=0).reshape(nz, 2 * hid, feats)

    cot = cotangent.reshape(rows, nz, 2, feats)
    cot_0, cot_1 = cot[:, :, 0].reshape(rows, wide), cot[:, :, 1].reshape(rows, wide)
    cot_own = jnp.where(first, cot_0, cot_1)
    cot_far = swap(jnp.where(first, cot_1, cot_0), "c")
    block = spread(jnp.concatenate([tokens, cot_own, cot_far], axis=1), "y")
    blocks = [block] + [shift(block, "x", k) for k in (1, 2, 3)]
    plane = jnp.stack(blocks).reshape(half, 2 * d)
    other = swap(mine, "c")
    tok, cot_own, cot_far = plane[:, :d], plane[:, d : d + wide], plane[:, d + wide :]

    def down(cot):
        return sum(contract(cot[:, z * feats : (z + 1) * feats], down_rows[z], 1, 1) for z in range(nz))

    d_hidden = down(cot_own) + swap(down(cot_far), "c")
    d_low, d_high = d_hidden[:, :hid], d_hidden[:, hid:]
    d_hidden = jnp.concatenate([jnp.where(low, d_low, d_high), jnp.where(low, d_high, d_low)], axis=1)

    pre_mine = contract(tok, mine, 1, 0)
    pre_other = contract(tok, other, 1, 0)
    gate = jnp.concatenate(
        [contract(tok, gate_weight, 1, 0), jnp.where(first, pre_mine, pre_other)], axis=1
    )
    up = jnp.concatenate(
        [contract(tok, up_weight, 1, 0), jnp.where(first, pre_other, pre_mine)], axis=1
    )
    sigma = jax.nn.sigmoid(gate)
    silu = gate * sigma
    hidden = (silu * up).astype(BF16)
    d_up = (d_hidden * silu).astype(BF16)
    d_gate = (d_hidden * up * sigma * (1.0 + gate * (1.0 - sigma))).astype(BF16)

    dg, du = d_gate[:, hid:], d_up[:, hid:]
    term = (
        contract(d_gate[:, :hid], gate_weight, 1, 1)
        + contract(d_up[:, :hid], up_weight, 1, 1)
        + contract(jnp.where(first, dg, du), mine, 1, 1)
        + contract(jnp.where(first, du, dg), other, 1, 1)
    ).astype(BF16)
    term = term.reshape(nx, ny * rows, d)
    total = term[0].astype(F32)
    for k in (1, 2, 3):
        total = total + shift(term[k], "x", -k).astype(F32)
    parts = lax.all_to_all(total.astype(BF16).reshape(ny, rows, d), "y", 0, 0)
    input_grad = jnp.sum(parts.astype(F32), axis=0).astype(BF16)

    both = jnp.stack([cot_own, cot_far]).reshape(2, half, nz, feats)
    both = lax.all_to_all(jnp.moveaxis(both, 2, 0), "zh", 0, 0)
    hid_own = spread(hidden, "zh")
    hid_far = swap(hid_own, "c")
    grads = contract(hid_own.reshape(nz * half, 2 * hid), both[:, 0].reshape(nz * half, feats), 0, 0)
    grads = grads + contract(
        hid_far.reshape(nz * half, 2 * hid), both[:, 1].reshape(nz * half, feats), 0, 0
    )
    down_grad = grads[:hid] + swap(grads[hid:].astype(BF16), "zl").astype(F32)
    return (input_grad, down_grad)


def solution(mesh):
    fine = Mesh(mesh.devices.reshape(4, 2, 2, 8, 4), ("zh", "c", "zl", "y", "x"))
    placed = (
        P((*DP, *TENSOR), None),
        P((*DP, *TENSOR), None),
        P(None, TENSOR),
        P(None, TENSOR),
        P(TENSOR, DP),
    )
    return jax.shard_map(
        on_device,
        mesh=fine,
        in_specs=placed,
        out_specs=(P((*DP, *TENSOR), None), P(TENSOR, DP)),
        check_vma=False,
    )
```

```python
import functools

import jax
import jax.numpy as jnp
import numpy as np
from jax import lax
from jax.experimental import pallas as pl
from jax.experimental.pallas import tpu as pltpu
from jax.sharding import Mesh, PartitionSpec as P

BF16 = jnp.bfloat16
F32 = jnp.float32
DP = ("zh", "c")
TENSOR = ("zl", "y", "x")
NZ, NY, NX = 4, 8, 4
ROWS = 4
HALF = NX * NY * ROWS
D = 4096
HID = 256
FEATS = 512
STEPS = D // FEATS
PIECE = 2 * NY * ROWS


def contract(a, b, ca, cb):
    return lax.dot_general(a, b, (((ca,), (cb,)), ((), ())), preferred_element_type=F32)


def swap(value, axis):
    return lax.ppermute(value, axis, [(0, 1), (1, 0)])


def shift(value, axis, k):
    n = lax.axis_size(axis)
    return lax.ppermute(value, axis, [(i, (i + k) % n) for i in range(n)])


def forward_body(where, pick, r0, r1, r2, r3, gw, uw, mw, ow, dn, df, exch, dd, tok, cot, acc, dacc):
    step = pl.program_id(0)
    zh, far = step // 2, step % 2

    @pl.when(step == 0)
    def _():
        acc[...] = jnp.zeros_like(acc)
        dacc[...] = jnp.zeros_like(dacc)

    n = NY * ROWS
    for i, piece in enumerate((r0, r1, r2, r3)):
        rows = contract(pick[...], piece[...], 1, 0).astype(BF16)
        tok[i * n : (i + 1) * n] = rows[:n]
        cot[i * n : (i + 1) * n] = rows[n:]
    t = tok[...]
    for i, w in enumerate((gw, uw, mw, ow)):
        acc[:, i * HID : (i + 1) * HID] += contract(t, w[...], 1, 0)
    exch[zh, far] = cot[...]

    @pl.when(far == 0)
    def _():
        dacc[...] += contract(cot[...], dn[0], 1, 1)

    @pl.when(far == 1)
    def _():
        dacc[...] += contract(cot[...], df[0], 1, 1)

    @pl.when(step == STEPS - 1)
    def _():
        first, low = where[0] == 0, where[1] == 0
        pm, po = acc[:, 2 * HID : 3 * HID], acc[:, 3 * HID :]
        dl, dh = dacc[:, :HID], dacc[:, HID:]
        sides = (
            (acc[:, :HID], acc[:, HID : 2 * HID], jnp.where(low, dl, dh)),
            (jnp.where(first, pm, po), jnp.where(first, po, pm), jnp.where(low, dh, dl)),
        )
        for i, (gate, up, d_hidden) in enumerate(sides):
            sigma = jax.nn.sigmoid(gate)
            silu = gate * sigma
            hidden = (silu * up).astype(BF16)
            for z in range(NZ):
                exch[z, 2, :, i * HID : (i + 1) * HID] = hidden
            d_up = d_hidden * silu
            d_gate = d_hidden * up * sigma * (1.0 + gate * (1.0 - sigma))
            if i == 1:
                d_gate, d_up = jnp.where(first, d_gate, d_up), jnp.where(first, d_up, d_gate)
            dd[:, 2 * i * HID : (2 * i + 1) * HID] = d_gate.astype(BF16)
            dd[:, (2 * i + 1) * HID : (2 * i + 2) * HID] = d_up.astype(BF16)


def forward(where, pick, pieces, gw, uw, mw, ow, dn, df):
    def column(j, s):
        far = j % 2
        return (j // 2) * 2 + far + s[0] - 2 * far * s[0]

    whole = lambda *shape: pl.BlockSpec(shape, lambda j, s: (0,) * len(shape))
    piece = pl.BlockSpec((PIECE, FEATS), lambda j, s: (0, column(j, s)))
    weight = pl.BlockSpec((FEATS, HID), lambda j, s: (column(j, s), 0))
    down = pl.BlockSpec((1, 2 * HID, FEATS), lambda j, s: (j // 2, 0, 0))
    return pl.pallas_call(
        forward_body,
        grid_spec=pltpu.PrefetchScalarGridSpec(
            num_scalar_prefetch=1,
            grid=(STEPS,),
            in_specs=[whole(PIECE, PIECE)] + [piece] * 4 + [weight] * 4 + [down] * 2,
            out_specs=[whole(NZ, 3, HALF, FEATS), whole(HALF, 4 * HID)],
            scratch_shapes=[
                pltpu.VMEM((HALF, FEATS), BF16),
                pltpu.VMEM((HALF, FEATS), BF16),
                pltpu.VMEM((HALF, 4 * HID), F32),
                pltpu.VMEM((HALF, 2 * HID), F32),
            ],
        ),
        out_shape=[
            jax.ShapeDtypeStruct((NZ, 3, HALF, FEATS), BF16),
            jax.ShapeDtypeStruct((HALF, 4 * HID), BF16),
        ],
        compiler_params=pltpu.CompilerParams(vmem_limit_bytes=32 * 2**20),
        name="forward",
    )(where, pick, *pieces, gw, uw, mw, ow, dn, df)


def term_body(dd, gw, uw, mw, ow, o0, o1, o2, o3):
    total = contract(dd[:, :HID], gw[...], 1, 1)
    for i, w in ((1, uw), (2, mw), (3, ow)):
        total += contract(dd[:, i * HID : (i + 1) * HID], w[...], 1, 1)
    n = NY * ROWS
    for i, o in enumerate((o0, o1, o2, o3)):
        o[...] = total[i * n : (i + 1) * n].astype(BF16)


def term(dd, gw, uw, mw, ow):
    weight = pl.BlockSpec((FEATS, HID), lambda j: (j, 0))
    out = pl.BlockSpec((NY * ROWS, FEATS), lambda j: (0, j))
    return pl.pallas_call(
        term_body,
        grid=(STEPS,),
        in_specs=[pl.BlockSpec((HALF, 4 * HID), lambda j: (0, 0))] + [weight] * 4,
        out_specs=[out] * 4,
        out_shape=[jax.ShapeDtypeStruct((NY * ROWS, D), BF16)] * 4,
        compiler_params=pltpu.CompilerParams(vmem_limit_bytes=32 * 2**20),
        name="term",
    )(dd, gw, uw, mw, ow)


def grads_body(near, far, keep, send, acc):
    step = pl.program_id(0)

    @pl.when(step == 0)
    def _():
        acc[...] = jnp.zeros_like(acc)

    acc[...] += contract(near[0, 2], near[0, 0], 0, 0) + contract(far[0, 1], far[0, 0], 0, 0)

    @pl.when(step == NZ - 1)
    def _():
        keep[...] = acc[:HID]
        send[...] = acc[HID:].astype(BF16)


def grads(near, far):
    return pl.pallas_call(
        grads_body,
        grid=(NZ,),
        in_specs=[
            pl.BlockSpec((1, 3, HALF, FEATS), lambda j: (j, 0, 0, 0)),
            pl.BlockSpec((1, 2, HALF, FEATS), lambda j: (j, 0, 0, 0)),
        ],
        out_specs=[pl.BlockSpec((HID, FEATS), lambda j: (0, 0))] * 2,
        out_shape=[
            jax.ShapeDtypeStruct((HID, FEATS), F32),
            jax.ShapeDtypeStruct((HID, FEATS), BF16),
        ],
        scratch_shapes=[pltpu.VMEM((2 * HID, FEATS), F32)],
        compiler_params=pltpu.CompilerParams(vmem_limit_bytes=32 * 2**20),
        name="grads",
    )(near, far)


def pick_matrix():
    out = np.zeros((PIECE, PIECE), np.float32)
    for y in range(NY):
        for t in range(ROWS):
            out[y * ROWS + t, 2 * y * ROWS + t] = 1
            out[NY * ROWS + y * ROWS + t, (2 * y + 1) * ROWS + t] = 1
    return jnp.asarray(out, BF16)


def on_device(tokens, cotangent, gate_weight, up_weight, down_weight):
    core, zl = lax.axis_index("c"), lax.axis_index("zl")
    where = jnp.stack([core, zl]).astype(jnp.int32)

    picked = jnp.where(core == 0, gate_weight, up_weight)
    picked, tokens = lax.optimization_barrier((picked, tokens))
    mine = swap(picked, "zl")
    down_near = lax.all_gather(down_weight, ("zh", "zl"), axis=0).reshape(NZ, 2 * HID, FEATS)
    down_far = swap(down_near, "c")

    block = jnp.concatenate([tokens, cotangent], axis=0)
    block = jnp.broadcast_to(block[None], (NY, 2 * ROWS, D))
    block = lax.all_to_all(block, "y", 0, 0).reshape(PIECE, D)
    near_1, near_3 = shift(block, "x", 1), shift(block, "x", 3)
    late, mine = lax.optimization_barrier((block, mine))
    other = swap(mine, "c")
    pieces = (block, near_1, shift(late, "x", 2), near_3)

    exch, dd = forward(where, pick_matrix(), pieces, gate_weight, up_weight, mine, other, down_near, down_far)

    exch = lax.all_to_all(exch, "zh", 0, 0)
    parts = term(dd, gate_weight, up_weight, mine, other)
    total = parts[0].astype(F32)
    for k in (1, 2, 3):
        total = total + shift(parts[k], "x", -k).astype(F32)
    total = lax.all_to_all(total.astype(BF16).reshape(NY, ROWS, D), "y", 0, 0)
    input_grad = jnp.sum(total.astype(F32), axis=0).astype(BF16)

    keep, send = grads(exch, swap(exch[:, 1:], "c"))
    down_grad = keep + swap(send, "zl").astype(F32)
    return (input_grad, down_grad)


def solution(mesh):
    fine = Mesh(mesh.devices.reshape(NZ, 2, 2, NY, NX), ("zh", "c", "zl", "y", "x"))
    placed = (
        P((*DP, *TENSOR), None),
        P((*DP, *TENSOR), None),
        P(None, TENSOR),
        P(None, TENSOR),
        P(TENSOR, DP),
    )
    return jax.shard_map(
        on_device,
        mesh=fine,
        in_specs=placed,
        out_specs=(P((*DP, *TENSOR), None), P(TENSOR, DP)),
        check_vma=False,
    )
```

```python
import functools

import jax
import jax.numpy as jnp
import numpy as np
from jax import lax
from jax.experimental import pallas as pl
from jax.experimental.pallas import tpu as pltpu
from jax.sharding import Mesh, PartitionSpec as P

BF16 = jnp.bfloat16
F32 = jnp.float32
DP = ("zh", "c")
TENSOR = ("zl", "y", "x")
NZ, NY, NX = 4, 8, 4
ROWS = 4
HALF = NX * NY * ROWS
D = 4096
HID = 256
FEATS = 512
STEPS = D // FEATS
PIECE = 2 * NY * ROWS


def contract(a, b, ca, cb):
    return lax.dot_general(a, b, (((ca,), (cb,)), ((), ())), preferred_element_type=F32)


def swap(value, axis):
    return lax.ppermute(value, axis, [(0, 1), (1, 0)])


def shift(value, axis, k):
    n = lax.axis_size(axis)
    return lax.ppermute(value, axis, [(i, (i + k) % n) for i in range(n)])


def neighbours(value):
    at = lambda zh, c, zl: ((zh % NZ) * 2 + c) * 2 + zl
    pairs = []
    for zh in range(NZ):
        pairs += [(at(zh, 0, 0), at(zh, 0, 1)), (at(zh, 0, 1), at(zh, 0, 0))]
        pairs += [(at(zh, 1, 1), at(zh + 1, 1, 0)), (at(zh + 1, 1, 0), at(zh, 1, 1))]
    return lax.ppermute(value, ("zh", "c", "zl"), pairs)


def split_body(where, pick, r0, r1, r2, r3, tok, cot):
    step = pl.program_id(0)
    n = NY * ROWS
    for i, piece in enumerate((r0, r1, r2, r3)):
        rows = contract(pick[...], piece[...], 1, 0).astype(BF16)
        tok[i * n : (i + 1) * n] = rows[:n]
        cot[0, 0, i * n : (i + 1) * n] = rows[n:]


def split(where, pick, pieces):
    piece = pl.BlockSpec((PIECE, FEATS), lambda j, s: (0, j))
    return pl.pallas_call(
        split_body,
        grid_spec=pltpu.PrefetchScalarGridSpec(
            num_scalar_prefetch=1,
            grid=(STEPS,),
            in_specs=[pl.BlockSpec((PIECE, PIECE), lambda j, s: (0, 0))] + [piece] * 4,
            out_specs=[
                pl.BlockSpec((HALF, FEATS), lambda j, s: (0, j)),
                pl.BlockSpec((1, 1, HALF, FEATS), lambda j, s: (j // 2, flip(j % 2, s[0]), 0, 0)),
            ],
        ),
        out_shape=[
            jax.ShapeDtypeStruct((HALF, D), BF16),
            jax.ShapeDtypeStruct((NZ, 2, HALF, FEATS), BF16),
        ],
        compiler_params=pltpu.CompilerParams(vmem_limit_bytes=32 * 2**20),
        name="split",
    )(where, pick, *pieces)


def flip(a, b):
    return a + b - 2 * a * b


def forward_body(where, tok, cot, gw, uw, mw, ow, dn, df, hid, dd, acc, dacc):
    step = pl.program_id(0)
    far = step % 2

    @pl.when(step == 0)
    def _():
        acc[...] = jnp.zeros_like(acc)
        dacc[...] = jnp.zeros_like(dacc)

    t = tok[...]
    for i, w in enumerate((gw, uw, mw, ow)):
        acc[:, i * HID : (i + 1) * HID] += contract(t, w[...], 1, 0)

    @pl.when(far == 0)
    def _():
        dacc[...] += contract(cot[0, 0], dn[0], 1, 1)

    @pl.when(far == 1)
    def _():
        dacc[...] += contract(cot[0, 0], df[0], 1, 1)

    @pl.when(step == STEPS - 1)
    def _():
        first, low = where[0] == 0, where[1] == 0
        pm, po = acc[:, 2 * HID : 3 * HID], acc[:, 3 * HID :]
        dl, dh = dacc[:, :HID], dacc[:, HID:]
        sides = (
            (acc[:, :HID], acc[:, HID : 2 * HID], jnp.where(low, dl, dh)),
            (jnp.where(first, pm, po), jnp.where(first, po, pm), jnp.where(low, dh, dl)),
        )
        for i, (gate, up, d_hidden) in enumerate(sides):
            sigma = jax.nn.sigmoid(gate)
            silu = gate * sigma
            hid[:, i * HID : (i + 1) * HID] = (silu * up).astype(BF16)
            d_up = d_hidden * silu
            d_gate = d_hidden * up * sigma * (1.0 + gate * (1.0 - sigma))
            if i == 1:
                d_gate, d_up = jnp.where(first, d_gate, d_up), jnp.where(first, d_up, d_gate)
            dd[:, 2 * i * HID : (2 * i + 1) * HID] = d_gate.astype(BF16)
            dd[:, (2 * i + 1) * HID : (2 * i + 2) * HID] = d_up.astype(BF16)


def forward(where, tok, cot, gw, uw, mw, ow, dn, df):
    def column(j, s):
        return (j // 2) * 2 + flip(j % 2, s[0])

    weight = pl.BlockSpec((FEATS, HID), lambda j, s: (column(j, s), 0))
    down = pl.BlockSpec((1, 2 * HID, FEATS), lambda j, s: (j // 2, 0, 0))
    return pl.pallas_call(
        forward_body,
        grid_spec=pltpu.PrefetchScalarGridSpec(
            num_scalar_prefetch=1,
            grid=(STEPS,),
            in_specs=[
                pl.BlockSpec((HALF, FEATS), lambda j, s: (0, column(j, s))),
                pl.BlockSpec((1, 1, HALF, FEATS), lambda j, s: (j // 2, j % 2, 0, 0)),
            ]
            + [weight] * 4
            + [down] * 2,
            out_specs=[
                pl.BlockSpec((HALF, 2 * HID), lambda j, s: (0, 0)),
                pl.BlockSpec((HALF, 4 * HID), lambda j, s: (0, 0)),
            ],
            scratch_shapes=[
                pltpu.VMEM((HALF, 4 * HID), F32),
                pltpu.VMEM((HALF, 2 * HID), F32),
            ],
        ),
        out_shape=[
            jax.ShapeDtypeStruct((HALF, 2 * HID), BF16),
            jax.ShapeDtypeStruct((HALF, 4 * HID), BF16),
        ],
        compiler_params=pltpu.CompilerParams(vmem_limit_bytes=32 * 2**20),
        name="forward",
    )(where, tok, cot, gw, uw, mw, ow, dn, df)


def term_body(dd, gw, uw, mw, ow, o0, o1, o2, o3):
    total = contract(dd[:, :HID], gw[...], 1, 1)
    for i, w in ((1, uw), (2, mw), (3, ow)):
        total += contract(dd[:, i * HID : (i + 1) * HID], w[...], 1, 1)
    n = NY * ROWS
    for i, o in enumerate((o0, o1, o2, o3)):
        o[...] = total[i * n : (i + 1) * n].astype(BF16)


def term(dd, gw, uw, mw, ow):
    weight = pl.BlockSpec((FEATS, HID), lambda j: (j, 0))
    out = pl.BlockSpec((NY * ROWS, FEATS), lambda j: (0, j))
    return pl.pallas_call(
        term_body,
        grid=(STEPS,),
        in_specs=[pl.BlockSpec((HALF, 4 * HID), lambda j: (0, 0))] + [weight] * 4,
        out_specs=[out] * 4,
        out_shape=[jax.ShapeDtypeStruct((NY * ROWS, D), BF16)] * 4,
        compiler_params=pltpu.CompilerParams(vmem_limit_bytes=32 * 2**20),
        name="term",
    )(dd, gw, uw, mw, ow)


def grads_body(hn, cn, hf, cf, keep, send, acc):
    step = pl.program_id(0)

    @pl.when(step == 0)
    def _():
        acc[...] = jnp.zeros_like(acc)

    acc[...] += contract(hn[0], cn[0, 0], 0, 0) + contract(hf[0], cf[0], 0, 0)

    @pl.when(step == NZ - 1)
    def _():
        keep[...] = acc[:HID]
        send[...] = acc[HID:].astype(BF16)


def grads(hid_near, cot_near, hid_far, cot_far):
    plain = pl.BlockSpec((1, HALF, FEATS), lambda j: (j, 0, 0))
    return pl.pallas_call(
        grads_body,
        grid=(NZ,),
        in_specs=[plain, pl.BlockSpec((1, 1, HALF, FEATS), lambda j: (j, 0, 0, 0)), plain, plain],
        out_specs=[pl.BlockSpec((HID, FEATS), lambda j: (0, 0))] * 2,
        out_shape=[
            jax.ShapeDtypeStruct((HID, FEATS), F32),
            jax.ShapeDtypeStruct((HID, FEATS), BF16),
        ],
        scratch_shapes=[pltpu.VMEM((2 * HID, FEATS), F32)],
        compiler_params=pltpu.CompilerParams(vmem_limit_bytes=32 * 2**20),
        name="grads",
    )(hid_near, cot_near, hid_far, cot_far)


def pick_matrix():
    out = np.zeros((PIECE, PIECE), np.float32)
    for y in range(NY):
        for t in range(ROWS):
            out[y * ROWS + t, 2 * y * ROWS + t] = 1
            out[NY * ROWS + y * ROWS + t, (2 * y + 1) * ROWS + t] = 1
    return jnp.asarray(out, BF16)


def on_device(tokens, cotangent, gate_weight, up_weight, down_weight):
    core, zl = lax.axis_index("c"), lax.axis_index("zl")
    where = jnp.stack([core, zl]).astype(jnp.int32)

    picked = jnp.where(core == 0, gate_weight, up_weight)
    picked, tokens = lax.optimization_barrier((picked, tokens))
    mine = neighbours(picked)
    down_near = lax.all_gather(down_weight, ("zh", "zl"), axis=0).reshape(NZ, 2 * HID, FEATS)
    down_far = swap(down_near, "c")

    block = jnp.concatenate([tokens, cotangent], axis=0)
    block = jnp.broadcast_to(block[None], (NY, 2 * ROWS, D))
    block = lax.all_to_all(block, "y", 0, 0).reshape(PIECE, D)
    near_1, near_3 = shift(block, "x", 1), shift(block, "x", 3)
    late, mine = lax.optimization_barrier((block, mine))
    other = swap(mine, "c")
    pieces = (block, near_1, shift(late, "x", 2), near_3)

    tok, cot = split(where, pick_matrix(), pieces)
    cot_x = lax.all_to_all(cot, "zh", 0, 0)
    cot_far = swap(cot_x[:, 1], "c")
    hidden, dd = forward(where, tok, cot, gate_weight, up_weight, mine, other, down_near, down_far)

    hid_near = lax.all_to_all(jnp.broadcast_to(hidden[None], (NZ, *hidden.shape)), "zh", 0, 0)
    parts = term(dd, gate_weight, up_weight, mine, other)
    total = parts[0].astype(F32)
    for k in (1, 2, 3):
        total = total + shift(parts[k], "x", -k).astype(F32)
    total = lax.all_to_all(total.astype(BF16).reshape(NY, ROWS, D), "y", 0, 0)
    input_grad = jnp.sum(total.astype(F32), axis=0).astype(BF16)

    keep, send = grads(hid_near, cot_x, swap(hid_near, "c"), cot_far)
    down_grad = keep + swap(send, "zl").astype(F32)
    return (input_grad, down_grad)


def solution(mesh):
    fine = Mesh(mesh.devices.reshape(NZ, 2, 2, NY, NX), ("zh", "c", "zl", "y", "x"))
    placed = (
        P((*DP, *TENSOR), None),
        P((*DP, *TENSOR), None),
        P(None, TENSOR),
        P(None, TENSOR),
        P(TENSOR, DP),
    )
    return jax.shard_map(
        on_device,
        mesh=fine,
        in_specs=placed,
        out_specs=(P((*DP, *TENSOR), None), P(TENSOR, DP)),
        check_vma=False,
    )
```

```python
import functools

import jax
import jax.numpy as jnp
import numpy as np
from jax import lax
from jax.experimental import pallas as pl
from jax.experimental.pallas import tpu as pltpu
from jax.sharding import Mesh, PartitionSpec as P

BF16 = jnp.bfloat16
F32 = jnp.float32
DP = ("zh", "c")
TENSOR = ("zl", "y", "x")
NZ, NY, NX = 4, 8, 4
ROWS = 4
HALF = NX * NY * ROWS
D = 4096
HID = 256
FEATS = 512
STEPS = D // FEATS
PIECE = 2 * NY * ROWS


def contract(a, b, ca, cb):
    return lax.dot_general(a, b, (((ca,), (cb,)), ((), ())), preferred_element_type=F32)


def swap(value, axis):
    return lax.ppermute(value, axis, [(0, 1), (1, 0)])


def shift(value, axis, k):
    n = lax.axis_size(axis)
    return lax.ppermute(value, axis, [(i, (i + k) % n) for i in range(n)])


def neighbours(value):
    at = lambda zh, c, zl: ((zh % NZ) * 2 + c) * 2 + zl
    pairs = []
    for zh in range(NZ):
        pairs += [(at(zh, 0, 0), at(zh, 0, 1)), (at(zh, 0, 1), at(zh, 0, 0))]
        pairs += [(at(zh, 1, 1), at(zh + 1, 1, 0)), (at(zh + 1, 1, 0), at(zh, 1, 1))]
    return lax.ppermute(value, ("zh", "c", "zl"), pairs)


def split_body(where, pick, r0, r1, r2, r3, tok, cot):
    step = pl.program_id(0)
    n = NY * ROWS
    for i, piece in enumerate((r0, r1, r2, r3)):
        rows = contract(pick[...], piece[...], 1, 0).astype(BF16)
        tok[i * n : (i + 1) * n] = rows[:n]
        cot[0, 0, i * n : (i + 1) * n] = rows[n:]


def split(where, pick, pieces):
    piece = pl.BlockSpec((PIECE, FEATS), lambda j, s: (0, j))
    return pl.pallas_call(
        split_body,
        grid_spec=pltpu.PrefetchScalarGridSpec(
            num_scalar_prefetch=1,
            grid=(STEPS,),
            in_specs=[pl.BlockSpec((PIECE, PIECE), lambda j, s: (0, 0))] + [piece] * 4,
            out_specs=[
                pl.BlockSpec((HALF, FEATS), lambda j, s: (0, j)),
                pl.BlockSpec((1, 1, HALF, FEATS), lambda j, s: (j // 2, flip(j % 2, s[0]), 0, 0)),
            ],
        ),
        out_shape=[
            hbm((HALF, D), BF16),
            hbm((NZ, 2, HALF, FEATS), BF16),
        ],
        compiler_params=pltpu.CompilerParams(vmem_limit_bytes=32 * 2**20),
        name="split",
    )(where, pick, *pieces)


def hbm(shape, dtype):
    return pltpu.MemorySpace.HBM(shape, dtype)


def pinned(*values):
    return [pltpu.with_memory_space_constraint(v, pltpu.MemorySpace.HBM) for v in values]


def flip(a, b):
    return a + b - 2 * a * b


def forward_body(where, tok, cot, gw, uw, mw, ow, dn, df, hid, dd, acc, dacc):
    step = pl.program_id(0)
    far = step % 2

    @pl.when(step == 0)
    def _():
        acc[...] = jnp.zeros_like(acc)
        dacc[...] = jnp.zeros_like(dacc)

    t = tok[...]
    for i, w in enumerate((gw, uw, mw, ow)):
        acc[:, i * HID : (i + 1) * HID] += contract(t, w[...], 1, 0)

    @pl.when(far == 0)
    def _():
        dacc[...] += contract(cot[0, 0], dn[0], 1, 1)

    @pl.when(far == 1)
    def _():
        dacc[...] += contract(cot[0, 0], df[0], 1, 1)

    @pl.when(step == STEPS - 1)
    def _():
        first, low = where[0] == 0, where[1] == 0
        pm, po = acc[:, 2 * HID : 3 * HID], acc[:, 3 * HID :]
        dl, dh = dacc[:, :HID], dacc[:, HID:]
        sides = (
            (acc[:, :HID], acc[:, HID : 2 * HID], jnp.where(low, dl, dh)),
            (jnp.where(first, pm, po), jnp.where(first, po, pm), jnp.where(low, dh, dl)),
        )
        for i, (gate, up, d_hidden) in enumerate(sides):
            sigma = jax.nn.sigmoid(gate)
            silu = gate * sigma
            hid[:, i * HID : (i + 1) * HID] = (silu * up).astype(BF16)
            d_up = d_hidden * silu
            d_gate = d_hidden * up * sigma * (1.0 + gate * (1.0 - sigma))
            if i == 1:
                d_gate, d_up = jnp.where(first, d_gate, d_up), jnp.where(first, d_up, d_gate)
            dd[:, 2 * i * HID : (2 * i + 1) * HID] = d_gate.astype(BF16)
            dd[:, (2 * i + 1) * HID : (2 * i + 2) * HID] = d_up.astype(BF16)


def forward(where, tok, cot, gw, uw, mw, ow, dn, df):
    def column(j, s):
        return (j // 2) * 2 + flip(j % 2, s[0])

    weight = pl.BlockSpec((FEATS, HID), lambda j, s: (column(j, s), 0))
    down = pl.BlockSpec((1, 2 * HID, FEATS), lambda j, s: (j // 2, 0, 0))
    return pl.pallas_call(
        forward_body,
        grid_spec=pltpu.PrefetchScalarGridSpec(
            num_scalar_prefetch=1,
            grid=(STEPS,),
            in_specs=[
                pl.BlockSpec((HALF, FEATS), lambda j, s: (0, column(j, s))),
                pl.BlockSpec((1, 1, HALF, FEATS), lambda j, s: (j // 2, j % 2, 0, 0)),
            ]
            + [weight] * 4
            + [down] * 2,
            out_specs=[
                pl.BlockSpec((HALF, 2 * HID), lambda j, s: (0, 0)),
                pl.BlockSpec((HALF, 4 * HID), lambda j, s: (0, 0)),
            ],
            scratch_shapes=[
                pltpu.VMEM((HALF, 4 * HID), F32),
                pltpu.VMEM((HALF, 2 * HID), F32),
            ],
        ),
        out_shape=[
            jax.ShapeDtypeStruct((HALF, 2 * HID), BF16),
            jax.ShapeDtypeStruct((HALF, 4 * HID), BF16),
        ],
        compiler_params=pltpu.CompilerParams(vmem_limit_bytes=32 * 2**20),
        name="forward",
    )(where, *pinned(tok, cot, gw, uw, mw), ow, *pinned(dn), df)


def term_body(where, dd, gw, uw, mw, ow, out):
    total = contract(dd[:, :HID], gw[...], 1, 1)
    for i, w in ((1, uw), (2, mw), (3, ow)):
        total += contract(dd[:, i * HID : (i + 1) * HID], w[...], 1, 1)
    n = NY * ROWS
    for i in range(NX):
        out[(where[2] + NX - i) % NX] = total[i * n : (i + 1) * n].astype(BF16)


def term(where, dd, gw, uw, mw, ow):
    weight = pl.BlockSpec((FEATS, HID), lambda j, s: (j, 0))
    return pl.pallas_call(
        term_body,
        grid_spec=pltpu.PrefetchScalarGridSpec(
            num_scalar_prefetch=1,
            grid=(STEPS,),
            in_specs=[pl.BlockSpec((HALF, 4 * HID), lambda j, s: (0, 0))] + [weight] * 4,
            out_specs=pl.BlockSpec((NX, NY * ROWS, FEATS), lambda j, s: (0, 0, j)),
        ),
        out_shape=jax.ShapeDtypeStruct((NX, NY * ROWS, D), BF16),
        compiler_params=pltpu.CompilerParams(vmem_limit_bytes=32 * 2**20),
        name="term",
    )(where, dd, *pinned(gw, uw, mw), ow)


def grads_body(h, cn, cf, keep, send, acc):
    step = pl.program_id(0)

    @pl.when(step == 0)
    def _():
        acc[...] = jnp.zeros_like(acc)

    acc[...] += contract(h[0, 0], cn[0, 0], 0, 0) + contract(h[0, 1], cf[0], 0, 0)

    @pl.when(step == NZ - 1)
    def _():
        keep[...] = acc[:HID]
        send[...] = acc[HID:].astype(BF16)


def grads(hidden, cot_near, cot_far):
    return pl.pallas_call(
        grads_body,
        grid=(NZ,),
        in_specs=[
            pl.BlockSpec((1, 2, HALF, 2 * HID), lambda j: (j, 0, 0, 0)),
            pl.BlockSpec((1, 1, HALF, FEATS), lambda j: (j, 0, 0, 0)),
            pl.BlockSpec((1, HALF, FEATS), lambda j: (j, 0, 0)),
        ],
        out_specs=[pl.BlockSpec((HID, FEATS), lambda j: (0, 0))] * 2,
        out_shape=[
            jax.ShapeDtypeStruct((HID, FEATS), F32),
            jax.ShapeDtypeStruct((HID, FEATS), BF16),
        ],
        scratch_shapes=[pltpu.VMEM((2 * HID, FEATS), F32)],
        compiler_params=pltpu.CompilerParams(vmem_limit_bytes=32 * 2**20),
        name="grads",
    )(hidden, cot_near, cot_far)


def pick_matrix():
    out = np.zeros((PIECE, PIECE), np.float32)
    for y in range(NY):
        for t in range(ROWS):
            out[y * ROWS + t, 2 * y * ROWS + t] = 1
            out[NY * ROWS + y * ROWS + t, (2 * y + 1) * ROWS + t] = 1
    return jnp.asarray(out, BF16)


def on_device(tokens, cotangent, gate_weight, up_weight, down_weight):
    core = lax.axis_index("c")
    where = jnp.stack([core, lax.axis_index("zl"), lax.axis_index("x")]).astype(jnp.int32)

    picked = jnp.where(core == 0, gate_weight, up_weight)
    picked, tokens = lax.optimization_barrier((picked, tokens))
    mine = neighbours(picked)
    down_near = lax.all_gather(down_weight, ("zh", "zl"), axis=0).reshape(NZ, 2 * HID, FEATS)

    block = jnp.concatenate([tokens, cotangent], axis=0)
    block = jnp.broadcast_to(block[None], (NY, 2 * ROWS, D))
    block = lax.all_to_all(block, "y", 0, 0).reshape(PIECE, D)
    pieces = [block] + [shift(block, "x", k) for k in (1, 2, 3)]
    tok, cot = split(where, pick_matrix(), pieces)
    cot_x = lax.all_to_all(cot, "zh", 0, 0)
    tok, mine, down_near = lax.optimization_barrier((tok, mine, down_near))
    other, down_far = swap(mine, "c"), swap(down_near, "c")
    cot_far = swap(cot_x[:, 1], "c")
    hidden, dd = forward(where, tok, cot, gate_weight, up_weight, mine, other, down_near, down_far)

    hidden = lax.all_gather(jnp.stack([hidden, swap(hidden, "c")]), "zh", axis=0)
    parts = term(where, dd, gate_weight, up_weight, mine, other)
    parts = lax.all_to_all(parts.reshape(NX * NY, ROWS, D), ("x", "y"), 0, 0)
    input_grad = jnp.sum(parts.astype(F32), axis=0).astype(BF16)

    keep, send = grads(hidden, cot_x, cot_far)
    down_grad = keep + swap(send, "zl").astype(F32)
    return (input_grad, down_grad)


def solution(mesh):
    fine = Mesh(mesh.devices.reshape(NZ, 2, 2, NY, NX), ("zh", "c", "zl", "y", "x"))
    placed = (
        P((*DP, *TENSOR), None),
        P((*DP, *TENSOR), None),
        P(None, TENSOR),
        P(None, TENSOR),
        P(TENSOR, DP),
    )
    return jax.shard_map(
        on_device,
        mesh=fine,
        in_specs=placed,
        out_specs=(P((*DP, *TENSOR), None), P(TENSOR, DP)),
        check_vma=False,
    )
```

```python
import functools

import jax
import jax.numpy as jnp
import numpy as np
from jax import lax
from jax.experimental import pallas as pl
from jax.experimental.pallas import tpu as pltpu
from jax.sharding import Mesh, PartitionSpec as P

BF16 = jnp.bfloat16
F32 = jnp.float32
DP = ("zh", "c")
TENSOR = ("zl", "y", "x")
NZ, NY, NX = 4, 8, 4
ROWS = 4
HALF = NX * NY * ROWS
D = 4096
HID = 256
FEATS = 512
STEPS = D // FEATS
PIECE = 2 * NY * ROWS


def contract(a, b, ca, cb):
    return lax.dot_general(a, b, (((ca,), (cb,)), ((), ())), preferred_element_type=F32)


def swap(value, axis):
    return lax.ppermute(value, axis, [(0, 1), (1, 0)])


def shift(value, axis, k):
    n = lax.axis_size(axis)
    return lax.ppermute(value, axis, [(i, (i + k) % n) for i in range(n)])


def neighbours(value):
    at = lambda zh, c, zl: ((zh % NZ) * 2 + c) * 2 + zl
    pairs = []
    for zh in range(NZ):
        pairs += [(at(zh, 0, 0), at(zh, 0, 1)), (at(zh, 0, 1), at(zh, 0, 0))]
        pairs += [(at(zh, 1, 1), at(zh + 1, 1, 0)), (at(zh + 1, 1, 0), at(zh, 1, 1))]
    return lax.ppermute(value, ("zh", "c", "zl"), pairs)


def split_body(where, pick_tok, pick_cot, t0, t1, t2, t3, c, tok, cot):
    n = NY * ROWS
    for i, piece in enumerate((t0, t1, t2, t3)):
        rows = contract(pick_tok[...], piece[...], 1, 0).astype(BF16)
        tok[0, i * n : (i + 1) * n] = rows[:n]
        tok[1, i * n : (i + 1) * n] = rows[n:]
    rows = contract(pick_cot[...], c[...], 1, 0).astype(BF16)
    cot[0, 0, 0] = rows[:HALF]
    cot[1, 0, 0] = rows[HALF:]


def split(where, pieces, cot):
    whole = lambda n: pl.BlockSpec((n, n), lambda j, s: (0, 0))
    return pl.pallas_call(
        split_body,
        grid_spec=pltpu.PrefetchScalarGridSpec(
            num_scalar_prefetch=1,
            grid=(STEPS // 2,),
            in_specs=[whole(PIECE), whole(2 * HALF)]
            + [pl.BlockSpec((PIECE, FEATS), lambda j, s: (0, j))] * 4
            + [pl.BlockSpec((2 * HALF, FEATS), lambda j, s: (0, j))],
            out_specs=[
                pl.BlockSpec((2, HALF, FEATS), lambda j, s: (0, 0, j)),
                pl.BlockSpec((2, 1, 1, HALF, FEATS), lambda j, s: (0, j // 2, flip(j % 2, s[0]), 0, 0)),
            ],
        ),
        out_shape=[
            hbm((2, HALF, D // 2), BF16),
            hbm((2, NZ // 2, 2, HALF, FEATS), BF16),
        ],
        compiler_params=pltpu.CompilerParams(vmem_limit_bytes=32 * 2**20),
        name="split",
    )(where, *picks(), *pieces, cot)


def hbm(shape, dtype):
    return pltpu.MemorySpace.HBM(shape, dtype)


def pinned(*values):
    return [pltpu.with_memory_space_constraint(v, pltpu.MemorySpace.HBM) for v in values]


def flip(a, b):
    return a + b - 2 * a * b


def gates_body(where, tok, gw, uw, mw, ow, hid, fac, acc):
    step = pl.program_id(0)

    @pl.when(step == 0)
    def _():
        acc[...] = jnp.zeros_like(acc)

    t = tok[0]
    for i, w in enumerate((gw, uw, mw, ow)):
        acc[:, i * HID : (i + 1) * HID] += contract(t, w[...], 1, 0)

    @pl.when(step == STEPS - 1)
    def _():
        first = where[0] == 0
        pm, po = acc[:, 2 * HID : 3 * HID], acc[:, 3 * HID :]
        sides = (
            (acc[:, :HID], acc[:, HID : 2 * HID]),
            (jnp.where(first, pm, po), jnp.where(first, po, pm)),
        )
        for i, (gate, up) in enumerate(sides):
            sigma = jax.nn.sigmoid(gate)
            silu = gate * sigma
            hid[:, i * HID : (i + 1) * HID] = (silu * up).astype(BF16)
            slope = up * sigma * (1.0 + gate * (1.0 - sigma))
            if i == 1:
                slope, silu = jnp.where(first, slope, silu), jnp.where(first, silu, slope)
            fac[:, 2 * i * HID : (2 * i + 1) * HID] = slope
            fac[:, (2 * i + 1) * HID : (2 * i + 2) * HID] = silu


def gates(where, tok, gw, uw, mw, ow):
    weight = pl.BlockSpec((FEATS, HID), lambda j, s: (j, 0))
    return pl.pallas_call(
        gates_body,
        grid_spec=pltpu.PrefetchScalarGridSpec(
            num_scalar_prefetch=1,
            grid=(STEPS,),
            in_specs=[pl.BlockSpec((1, HALF, FEATS), lambda j, s: (j // NZ, 0, j % NZ))] + [weight] * 4,
            out_specs=[
                pl.BlockSpec((HALF, 2 * HID), lambda j, s: (0, 0)),
                pl.BlockSpec((HALF, 4 * HID), lambda j, s: (0, 0)),
            ],
            scratch_shapes=[pltpu.VMEM((HALF, 4 * HID), F32)],
        ),
        out_shape=[
            jax.ShapeDtypeStruct((HALF, 2 * HID), BF16),
            jax.ShapeDtypeStruct((HALF, 4 * HID), F32),
        ],
        compiler_params=pltpu.CompilerParams(vmem_limit_bytes=32 * 2**20),
        name="gates",
    )(where, *pinned(tok, gw, uw, mw), ow)


def down_body(where, cot, dn, df, fac, dd, acc):
    step = pl.program_id(0)

    @pl.when(step == 0)
    def _():
        acc[...] = jnp.zeros_like(acc)

    acc[...] += contract(cot[0, 0], dn[0], 1, 1) + contract(cot[0, 1], df[0], 1, 1)

    @pl.when(step == NZ - 1)
    def _():
        low = where[1] == 0
        dl, dh = acc[:, :HID], acc[:, HID:]
        for i, d_hidden in enumerate((jnp.where(low, dl, dh), jnp.where(low, dh, dl))):
            for k in (2 * i, 2 * i + 1):
                dd[:, k * HID : (k + 1) * HID] = (d_hidden * fac[:, k * HID : (k + 1) * HID]).astype(BF16)


def down(where, cot, dn, df, fac):
    plane = pl.BlockSpec((1, 2 * HID, FEATS), lambda j, s: (j, 0, 0))
    block = pl.BlockSpec((HALF, 4 * HID), lambda j, s: (0, 0))
    return pl.pallas_call(
        down_body,
        grid_spec=pltpu.PrefetchScalarGridSpec(
            num_scalar_prefetch=1,
            grid=(NZ,),
            in_specs=[pl.BlockSpec((1, 2, HALF, FEATS), lambda j, s: (j, 0, 0, 0)), plane, plane, block],
            out_specs=block,
            scratch_shapes=[pltpu.VMEM((HALF, 2 * HID), F32)],
        ),
        out_shape=jax.ShapeDtypeStruct((HALF, 4 * HID), BF16),
        compiler_params=pltpu.CompilerParams(vmem_limit_bytes=32 * 2**20),
        name="down",
    )(where, *pinned(cot, dn), df, fac)


def term_body(where, pick, dd, *refs):
    weights, out = refs[:-1], refs[-1]
    halves = []
    for h in range(2):
        total = None
        for i, w in enumerate(weights[h::2]):
            part = contract(dd[:, i * HID : (i + 1) * HID], w[...], 1, 1)
            total = part if total is None else total + part
        halves.append(total.astype(BF16))
    rows = contract(pick[...], jnp.concatenate(halves, axis=0), 1, 0).astype(BF16)
    for i in range(NX):
        out[(where[2] + NX - i) % NX] = rows[i * PIECE : (i + 1) * PIECE]


def term(where, dd, gw, uw, mw, ow):
    low = pl.BlockSpec((FEATS, HID), lambda j, s: (j, 0))
    high = pl.BlockSpec((FEATS, HID), lambda j, s: (j + NZ, 0))
    gw, uw, mw = pinned(gw, uw, mw)
    return pl.pallas_call(
        term_body,
        grid_spec=pltpu.PrefetchScalarGridSpec(
            num_scalar_prefetch=1,
            grid=(STEPS // 2,),
            in_specs=[
                pl.BlockSpec((2 * HALF, 2 * HALF), lambda j, s: (0, 0)),
                pl.BlockSpec((HALF, 4 * HID), lambda j, s: (0, 0)),
            ]
            + [low, high] * 4,
            out_specs=pl.BlockSpec((NX, PIECE, FEATS), lambda j, s: (0, 0, j)),
        ),
        out_shape=hbm((NX, PIECE, D // 2), BF16),
        compiler_params=pltpu.CompilerParams(vmem_limit_bytes=32 * 2**20),
        name="term",
    )(where, merge(), dd, gw, gw, uw, uw, mw, mw, ow, ow)


def grads_body(h, cn, cf, keep, send, acc):
    step = pl.program_id(0)

    @pl.when(step == 0)
    def _():
        acc[...] = jnp.zeros_like(acc)

    acc[...] += contract(h[0, 0], cn[0, 0], 0, 0) + contract(h[0, 1], cf[0], 0, 0)

    @pl.when(step == NZ - 1)
    def _():
        keep[...] = acc[:HID]
        send[...] = acc[HID:].astype(BF16)


def grads(hidden, cot_near, cot_far):
    return pl.pallas_call(
        grads_body,
        grid=(NZ,),
        in_specs=[
            pl.BlockSpec((1, 2, HALF, 2 * HID), lambda j: (j, 0, 0, 0)),
            pl.BlockSpec((1, 1, HALF, FEATS), lambda j: (j, 0, 0, 0)),
            pl.BlockSpec((1, HALF, FEATS), lambda j: (j, 0, 0)),
        ],
        out_specs=[pl.BlockSpec((HID, FEATS), lambda j: (0, 0))] * 2,
        out_shape=[
            jax.ShapeDtypeStruct((HID, FEATS), F32),
            jax.ShapeDtypeStruct((HID, FEATS), BF16),
        ],
        scratch_shapes=[pltpu.VMEM((2 * HID, FEATS), F32)],
        compiler_params=pltpu.CompilerParams(vmem_limit_bytes=32 * 2**20),
        name="grads",
    )(hidden, cot_near, cot_far)


def selection(shape, order):
    source = np.arange(np.prod(shape)).reshape(shape).transpose(order).reshape(-1)
    return jnp.asarray(np.eye(source.size, dtype=np.float32)[source], BF16)


def picks():
    return selection((NY, 2, ROWS), (1, 0, 2)), selection((NY, NX, 2, ROWS), (2, 1, 0, 3))


def merge():
    return selection((2, NX, NY, ROWS), (1, 2, 0, 3))


def folded(rows):
    return jnp.concatenate([rows[:, : D // 2], rows[:, D // 2 :]], axis=0)


def spread(block, axis):
    n = lax.axis_size(axis)
    return lax.all_to_all(jnp.broadcast_to(block[None], (n, *block.shape)), axis, 0, 0)


def on_device(tokens, cotangent, gate_weight, up_weight, down_weight):
    core = lax.axis_index("c")
    where = jnp.stack([core, lax.axis_index("zl"), lax.axis_index("x")]).astype(jnp.int32)

    picked = jnp.where(core == 0, gate_weight, up_weight)
    picked, tokens = lax.optimization_barrier((picked, tokens))
    mine = neighbours(picked)
    down_near = lax.all_gather(down_weight, ("zh", "zl"), axis=0).reshape(NZ, 2 * HID, FEATS)

    tok = spread(folded(tokens), "y").reshape(PIECE, D // 2)
    cot = folded(cotangent)
    cot = jnp.concatenate([cot] + [shift(cot, "x", k) for k in (1, 2, 3)], axis=0)
    cot = spread(cot, "y").reshape(2 * HALF, D // 2)
    tok = [tok] + [shift(tok, "x", k) for k in (1, 2, 3)]

    tok, cot = split(where, tok, cot)
    cot = cot.reshape(NZ, 2, HALF, FEATS)
    cot_x = lax.all_to_all(cot, "zh", 0, 0)
    cot_far = swap(cot_x[:, 1], "c")
    tok, mine, down_near = lax.optimization_barrier((tok, mine, down_near))
    other, down_far = swap(mine, "c"), swap(down_near, "c")
    hidden, factors = gates(where, tok, gate_weight, up_weight, mine, other)
    hidden = lax.all_gather(jnp.stack([hidden, swap(hidden, "c")]), "zh", axis=0)
    dd = down(where, cot, down_near, down_far, factors)

    parts = term(where, dd, gate_weight, up_weight, mine, other)
    parts = lax.all_to_all(parts.reshape(NX * NY, 2 * ROWS, D // 2), ("x", "y"), 0, 0)
    total = jnp.sum(parts.astype(F32), axis=0).astype(BF16)
    input_grad = jnp.concatenate([total[:ROWS], total[ROWS:]], axis=1)

    keep, send = grads(hidden, cot_x, cot_far)
    down_grad = keep + swap(send, "zl").astype(F32)
    return (input_grad, down_grad)


def solution(mesh):
    fine = Mesh(mesh.devices.reshape(NZ, 2, 2, NY, NX), ("zh", "c", "zl", "y", "x"))
    placed = (
        P((*DP, *TENSOR), None),
        P((*DP, *TENSOR), None),
        P(None, TENSOR),
        P(None, TENSOR),
        P(TENSOR, DP),
    )
    return jax.shard_map(
        on_device,
        mesh=fine,
        in_specs=placed,
        out_specs=(P((*DP, *TENSOR), None), P(TENSOR, DP)),
        check_vma=False,
    )
```

```python
import functools

import jax
import jax.numpy as jnp
import numpy as np
from jax import lax
from jax.experimental import pallas as pl
from jax.experimental.pallas import tpu as pltpu
from jax.sharding import Mesh, PartitionSpec as P

BF16 = jnp.bfloat16
F32 = jnp.float32
DP = ("zh", "c")
TENSOR = ("zl", "y", "x")
NZ, NY, NX = 4, 8, 4
ROWS = 4
HALF = NX * NY * ROWS
D = 4096
HID = 256
FEATS = 512
STEPS = D // FEATS
PIECE = 2 * NY * ROWS


def contract(a, b, ca, cb):
    return lax.dot_general(a, b, (((ca,), (cb,)), ((), ())), preferred_element_type=F32)


def swap(value, axis):
    return lax.ppermute(value, axis, [(0, 1), (1, 0)])


def shift(value, axis, k):
    n = lax.axis_size(axis)
    return lax.ppermute(value, axis, [(i, (i + k) % n) for i in range(n)])


def neighbours(value):
    at = lambda zh, c, zl: ((zh % NZ) * 2 + c) * 2 + zl
    pairs = []
    for zh in range(NZ):
        pairs += [(at(zh, 0, 0), at(zh, 0, 1)), (at(zh, 0, 1), at(zh, 0, 0))]
        pairs += [(at(zh, 1, 1), at(zh + 1, 1, 0)), (at(zh + 1, 1, 0), at(zh, 1, 1))]
    return lax.ppermute(value, ("zh", "c", "zl"), pairs)


def split_body(where, pick, r0, r1, r2, r3, tok, cot):
    n = NY * ROWS
    for i, piece in enumerate((r0, r1, r2, r3)):
        rows = contract(pick[...], piece[...], 1, 0).astype(BF16)
        tok[i * n : (i + 1) * n] = rows[:n]
        cot[0, 0, i * n : (i + 1) * n] = rows[n:]


def split(where, pieces):
    piece = pl.BlockSpec((PIECE, FEATS), lambda j, s: (0, j))
    return pl.pallas_call(
        split_body,
        grid_spec=pltpu.PrefetchScalarGridSpec(
            num_scalar_prefetch=1,
            grid=(STEPS,),
            in_specs=[pl.BlockSpec((PIECE, PIECE), lambda j, s: (0, 0))] + [piece] * 4,
            out_specs=[
                pl.BlockSpec((HALF, FEATS), lambda j, s: (0, j)),
                pl.BlockSpec((1, 1, HALF, FEATS), lambda j, s: (j // 2, flip(j % 2, s[0]), 0, 0)),
            ],
        ),
        out_shape=[
            hbm((HALF, D), BF16),
            hbm((NZ, 2, HALF, FEATS), BF16),
        ],
        compiler_params=pltpu.CompilerParams(vmem_limit_bytes=32 * 2**20),
        name="split",
    )(where, selection((NY, 2, ROWS), (1, 0, 2)), *pieces)


def hbm(shape, dtype):
    return pltpu.MemorySpace.HBM(shape, dtype)


def pinned(*values):
    return [pltpu.with_memory_space_constraint(v, pltpu.MemorySpace.HBM) for v in values]


def flip(a, b):
    return a + b - 2 * a * b


def gates_body(where, tok, gw, uw, mw, ow, hid, fac, acc):
    step = pl.program_id(0)

    @pl.when(step == 0)
    def _():
        acc[...] = jnp.zeros_like(acc)

    t = tok[...]
    for i, w in enumerate((gw, uw, mw, ow)):
        acc[:, i * HID : (i + 1) * HID] += contract(t, w[...], 1, 0)

    @pl.when(step == STEPS - 1)
    def _():
        first = where[0] == 0
        pm, po = acc[:, 2 * HID : 3 * HID], acc[:, 3 * HID :]
        sides = (
            (acc[:, :HID], acc[:, HID : 2 * HID]),
            (jnp.where(first, pm, po), jnp.where(first, po, pm)),
        )
        for i, (gate, up) in enumerate(sides):
            sigma = jax.nn.sigmoid(gate)
            silu = gate * sigma
            hid[:, i * HID : (i + 1) * HID] = (silu * up).astype(BF16)
            slope = up * sigma * (1.0 + gate * (1.0 - sigma))
            if i == 1:
                slope, silu = jnp.where(first, slope, silu), jnp.where(first, silu, slope)
            fac[:, 2 * i * HID : (2 * i + 1) * HID] = slope
            fac[:, (2 * i + 1) * HID : (2 * i + 2) * HID] = silu


def gates(where, tok, gw, uw, mw, ow):
    weight = pl.BlockSpec((FEATS, HID), lambda j, s: (j, 0))
    return pl.pallas_call(
        gates_body,
        grid_spec=pltpu.PrefetchScalarGridSpec(
            num_scalar_prefetch=1,
            grid=(STEPS,),
            in_specs=[pl.BlockSpec((HALF, FEATS), lambda j, s: (0, j))] + [weight] * 4,
            out_specs=[
                pl.BlockSpec((HALF, 2 * HID), lambda j, s: (0, 0)),
                pl.BlockSpec((HALF, 4 * HID), lambda j, s: (0, 0)),
            ],
            scratch_shapes=[pltpu.VMEM((HALF, 4 * HID), F32)],
        ),
        out_shape=[
            jax.ShapeDtypeStruct((HALF, 2 * HID), BF16),
            jax.ShapeDtypeStruct((HALF, 4 * HID), F32),
        ],
        compiler_params=pltpu.CompilerParams(vmem_limit_bytes=32 * 2**20),
        name="gates",
    )(where, *pinned(tok, gw, uw, mw), ow)


def down_body(where, cot, dn, df, fac, dd, acc):
    step = pl.program_id(0)

    @pl.when(step == 0)
    def _():
        acc[...] = jnp.zeros_like(acc)

    acc[...] += contract(cot[0, 0], dn[0], 1, 1) + contract(cot[0, 1], df[0], 1, 1)

    @pl.when(step == NZ - 1)
    def _():
        low = where[1] == 0
        dl, dh = acc[:, :HID], acc[:, HID:]
        for i, d_hidden in enumerate((jnp.where(low, dl, dh), jnp.where(low, dh, dl))):
            for k in (2 * i, 2 * i + 1):
                dd[:, k * HID : (k + 1) * HID] = (d_hidden * fac[:, k * HID : (k + 1) * HID]).astype(BF16)


def down(where, cot, dn, df, fac):
    plane = pl.BlockSpec((1, 2 * HID, FEATS), lambda j, s: (j, 0, 0))
    block = pl.BlockSpec((HALF, 4 * HID), lambda j, s: (0, 0))
    return pl.pallas_call(
        down_body,
        grid_spec=pltpu.PrefetchScalarGridSpec(
            num_scalar_prefetch=1,
            grid=(NZ,),
            in_specs=[pl.BlockSpec((1, 2, HALF, FEATS), lambda j, s: (j, 0, 0, 0)), plane, plane, block],
            out_specs=block,
            scratch_shapes=[pltpu.VMEM((HALF, 2 * HID), F32)],
        ),
        out_shape=jax.ShapeDtypeStruct((HALF, 4 * HID), BF16),
        compiler_params=pltpu.CompilerParams(vmem_limit_bytes=32 * 2**20),
        name="down",
    )(where, *pinned(cot, dn), df, fac)


def term_body(where, pick, dd, *refs):
    weights, out = refs[:-1], refs[-1]
    halves = []
    for h in range(2):
        total = None
        for i, w in enumerate(weights[h::2]):
            part = contract(dd[:, i * HID : (i + 1) * HID], w[...], 1, 1)
            total = part if total is None else total + part
        halves.append(total.astype(BF16))
    rows = contract(pick[...], jnp.concatenate(halves, axis=0), 1, 0).astype(BF16)
    for i in range(NX):
        out[(where[2] + NX - i) % NX] = rows[i * PIECE : (i + 1) * PIECE]


def term(where, dd, gw, uw, mw, ow):
    low = pl.BlockSpec((FEATS, HID), lambda j, s: (j, 0))
    high = pl.BlockSpec((FEATS, HID), lambda j, s: (j + NZ, 0))
    gw, uw, mw = pinned(gw, uw, mw)
    return pl.pallas_call(
        term_body,
        grid_spec=pltpu.PrefetchScalarGridSpec(
            num_scalar_prefetch=1,
            grid=(STEPS // 2,),
            in_specs=[
                pl.BlockSpec((2 * HALF, 2 * HALF), lambda j, s: (0, 0)),
                pl.BlockSpec((HALF, 4 * HID), lambda j, s: (0, 0)),
            ]
            + [low, high] * 4,
            out_specs=pl.BlockSpec((NX, PIECE, FEATS), lambda j, s: (0, 0, j)),
        ),
        out_shape=hbm((NX, PIECE, D // 2), BF16),
        compiler_params=pltpu.CompilerParams(vmem_limit_bytes=32 * 2**20),
        name="term",
    )(where, merge(), dd, gw, gw, uw, uw, mw, mw, ow, ow)


def grads_body(where, h, n0, n1, n2, n3, far, keep, send):
    total = None
    for j, near in enumerate((n0, n1, n2, n3)):
        z = (where[3] + NZ - j) % NZ
        part = contract(h[z, 0], near[0], 0, 0) + contract(h[z, 1], far[j], 0, 0)
        total = part if total is None else total + part
    keep[...] = total[:HID]
    send[...] = total[HID:].astype(BF16)


def grads(where, hidden, near, far):
    vmem = pl.BlockSpec(memory_space=pltpu.MemorySpace.VMEM)
    return pl.pallas_call(
        grads_body,
        in_specs=[pl.BlockSpec(memory_space=pltpu.MemorySpace.SMEM)] + [vmem] * 6,
        out_specs=[vmem] * 2,
        out_shape=[
            jax.ShapeDtypeStruct((HID, FEATS), F32),
            jax.ShapeDtypeStruct((HID, FEATS), BF16),
        ],
        compiler_params=pltpu.CompilerParams(vmem_limit_bytes=32 * 2**20),
        name="grads",
    )(where, hidden.reshape(NZ, 2, HALF, 2 * HID), *near, far)


def selection(shape, order):
    source = np.arange(np.prod(shape)).reshape(shape).transpose(order).reshape(-1)
    return jnp.asarray(np.eye(source.size, dtype=np.float32)[source], BF16)


def merge():
    return selection((2, NX, NY, ROWS), (1, 2, 0, 3))


def spread(block, axis):
    n = lax.axis_size(axis)
    return lax.all_to_all(jnp.broadcast_to(block[None], (n, *block.shape)), axis, 0, 0)


def on_device(tokens, cotangent, gate_weight, up_weight, down_weight):
    core = lax.axis_index("c")
    where = [core, lax.axis_index("zl"), lax.axis_index("x"), lax.axis_index("zh")]
    where = jnp.stack(where).astype(jnp.int32)

    picked = jnp.where(core == 0, gate_weight, up_weight)
    picked, tokens = lax.optimization_barrier((picked, tokens))
    mine = neighbours(picked)
    down_near = lax.all_gather(down_weight, ("zh", "zl"), axis=0).reshape(NZ, 2 * HID, FEATS)

    block = spread(jnp.concatenate([tokens, cotangent], axis=0), "y").reshape(PIECE, D)
    pieces = [block] + [shift(block, "x", k) for k in (1, 2, 3)]

    tok, cot = split(where, pieces)
    tok, mine, down_near = lax.optimization_barrier((tok, mine, down_near))
    other, down_far = swap(mine, "c"), swap(down_near, "c")
    hidden, factors = gates(where, tok, gate_weight, up_weight, mine, other)
    hidden = lax.all_gather(jnp.stack([hidden, swap(hidden, "c")]), "zh", axis=0)
    dd = down(where, cot, down_near, down_far, factors)

    parts = term(where, dd, gate_weight, up_weight, mine, other)
    parts, cot = lax.optimization_barrier((parts, cot))
    parts = lax.all_to_all(parts.reshape(NX * NY, 2 * ROWS, D // 2), ("x", "y"), 0, 0)
    total = jnp.sum(parts.astype(F32), axis=0).astype(BF16)
    input_grad = jnp.concatenate([total[:ROWS], total[ROWS:]], axis=1)

    at = lambda k: lax.dynamic_index_in_dim(cot, (lax.axis_index("zh") + k) % NZ, 0, keepdims=False)
    near = [at(0)] + [shift(at(k), "zh", k) for k in (1, 2, 3)]
    far = swap(jnp.stack([n[1] for n in near]), "c")
    keep, send = grads(where, hidden, near, far)
    down_grad = keep + swap(send, "zl").astype(F32)
    return (input_grad, down_grad)


def solution(mesh):
    fine = Mesh(mesh.devices.reshape(NZ, 2, 2, NY, NX), ("zh", "c", "zl", "y", "x"))
    placed = (
        P((*DP, *TENSOR), None),
        P((*DP, *TENSOR), None),
        P(None, TENSOR),
        P(None, TENSOR),
        P(TENSOR, DP),
    )
    return jax.shard_map(
        on_device,
        mesh=fine,
        in_specs=placed,
        out_specs=(P((*DP, *TENSOR), None), P(TENSOR, DP)),
        check_vma=False,
    )
```

```python
import functools

import jax
import jax.numpy as jnp
import numpy as np
from jax import lax
from jax.experimental import pallas as pl
from jax.experimental.pallas import tpu as pltpu
from jax.sharding import Mesh, PartitionSpec as P

BF16 = jnp.bfloat16
F32 = jnp.float32
DP = ("zh", "c")
TENSOR = ("zl", "y", "x")
NZ, NY, NX = 4, 8, 4
ROWS = 4
HALF = NX * NY * ROWS
D = 4096
HID = 256
FEATS = 512
STEPS = D // FEATS
PIECE = 2 * NY * ROWS


def contract(a, b, ca, cb):
    return lax.dot_general(a, b, (((ca,), (cb,)), ((), ())), preferred_element_type=F32)


def swap(value, axis):
    return lax.ppermute(value, axis, [(0, 1), (1, 0)])


def shift(value, axis, k):
    n = lax.axis_size(axis)
    return lax.ppermute(value, axis, [(i, (i + k) % n) for i in range(n)])


def neighbours(value):
    at = lambda zh, c, zl: ((zh % NZ) * 2 + c) * 2 + zl
    pairs = []
    for zh in range(NZ):
        pairs += [(at(zh, 0, 0), at(zh, 0, 1)), (at(zh, 0, 1), at(zh, 0, 0))]
        pairs += [(at(zh, 1, 1), at(zh + 1, 1, 0)), (at(zh + 1, 1, 0), at(zh, 1, 1))]
    return lax.ppermute(value, ("zh", "c", "zl"), pairs)


def split_body(where, pick, r0, r1, r2a, r2b, r3, tok, cot):
    n = NY * ROWS
    r2 = jnp.concatenate([r2a[...], r2b[...]], axis=0)
    for i, piece in enumerate((r0[...], r1[...], r2, r3[...])):
        rows = contract(pick[...], piece, 1, 0).astype(BF16)
        tok[i * n : (i + 1) * n] = rows[:n]
        cot[0, 0, i * n : (i + 1) * n] = rows[n:]


def split(where, pieces):
    piece = pl.BlockSpec((PIECE, FEATS), lambda j, s: (0, j))
    part = pl.BlockSpec((PIECE // 2, FEATS), lambda j, s: (0, j))
    return pl.pallas_call(
        split_body,
        grid_spec=pltpu.PrefetchScalarGridSpec(
            num_scalar_prefetch=1,
            grid=(STEPS,),
            in_specs=[pl.BlockSpec((PIECE, PIECE), lambda j, s: (0, 0)), piece, piece, part, part, piece],
            out_specs=[
                pl.BlockSpec((HALF, FEATS), lambda j, s: (0, j)),
                pl.BlockSpec((1, 1, HALF, FEATS), lambda j, s: (j // 2, flip(j % 2, s[0]), 0, 0)),
            ],
        ),
        out_shape=[
            hbm((HALF, D), BF16),
            hbm((NZ, 2, HALF, FEATS), BF16),
        ],
        compiler_params=pltpu.CompilerParams(vmem_limit_bytes=32 * 2**20),
        name="split",
    )(where, selection((NY, 2, ROWS), (1, 0, 2)), *pieces)


def hbm(shape, dtype):
    return pltpu.MemorySpace.HBM(shape, dtype)


def pinned(*values):
    return [pltpu.with_memory_space_constraint(v, pltpu.MemorySpace.HBM) for v in values]


def flip(a, b):
    return a + b - 2 * a * b


def gates_body(where, tok, gw, uw, mw, ow, hid, fac, acc):
    step = pl.program_id(0)

    @pl.when(step == 0)
    def _():
        acc[...] = jnp.zeros_like(acc)

    t = tok[...]
    for i, w in enumerate((gw, uw, mw, ow)):
        acc[:, i * HID : (i + 1) * HID] += contract(t, w[...], 1, 0)

    @pl.when(step == STEPS - 1)
    def _():
        first = where[0] == 0
        pm, po = acc[:, 2 * HID : 3 * HID], acc[:, 3 * HID :]
        sides = (
            (acc[:, :HID], acc[:, HID : 2 * HID]),
            (jnp.where(first, pm, po), jnp.where(first, po, pm)),
        )
        for i, (gate, up) in enumerate(sides):
            sigma = jax.nn.sigmoid(gate)
            silu = gate * sigma
            hid[:, i * HID : (i + 1) * HID] = (silu * up).astype(BF16)
            slope = up * sigma * (1.0 + gate * (1.0 - sigma))
            if i == 1:
                slope, silu = jnp.where(first, slope, silu), jnp.where(first, silu, slope)
            fac[:, 2 * i * HID : (2 * i + 1) * HID] = slope
            fac[:, (2 * i + 1) * HID : (2 * i + 2) * HID] = silu


def gates(where, tok, gw, uw, mw, ow):
    weight = pl.BlockSpec((FEATS, HID), lambda j, s: (j, 0))
    return pl.pallas_call(
        gates_body,
        grid_spec=pltpu.PrefetchScalarGridSpec(
            num_scalar_prefetch=1,
            grid=(STEPS,),
            in_specs=[pl.BlockSpec((HALF, FEATS), lambda j, s: (0, j))] + [weight] * 4,
            out_specs=[
                pl.BlockSpec((HALF, 2 * HID), lambda j, s: (0, 0)),
                pl.BlockSpec((HALF, 4 * HID), lambda j, s: (0, 0)),
            ],
            scratch_shapes=[pltpu.VMEM((HALF, 4 * HID), F32)],
        ),
        out_shape=[
            jax.ShapeDtypeStruct((HALF, 2 * HID), BF16),
            jax.ShapeDtypeStruct((HALF, 4 * HID), F32),
        ],
        compiler_params=pltpu.CompilerParams(vmem_limit_bytes=32 * 2**20),
        name="gates",
    )(where, *pinned(tok, gw, uw, mw), ow)


def down_body(where, cot, dn, df, fac, dd, acc):
    step = pl.program_id(0)

    @pl.when(step == 0)
    def _():
        acc[...] = jnp.zeros_like(acc)

    acc[...] += contract(cot[0, 0], dn[0], 1, 1) + contract(cot[0, 1], df[0], 1, 1)

    @pl.when(step == NZ - 1)
    def _():
        low = where[1] == 0
        dl, dh = acc[:, :HID], acc[:, HID:]
        for i, d_hidden in enumerate((jnp.where(low, dl, dh), jnp.where(low, dh, dl))):
            for k in (2 * i, 2 * i + 1):
                dd[:, k * HID : (k + 1) * HID] = (d_hidden * fac[:, k * HID : (k + 1) * HID]).astype(BF16)


def down(where, cot, dn, df, fac):
    plane = pl.BlockSpec((1, 2 * HID, FEATS), lambda j, s: (j, 0, 0))
    block = pl.BlockSpec((HALF, 4 * HID), lambda j, s: (0, 0))
    return pl.pallas_call(
        down_body,
        grid_spec=pltpu.PrefetchScalarGridSpec(
            num_scalar_prefetch=1,
            grid=(NZ,),
            in_specs=[pl.BlockSpec((1, 2, HALF, FEATS), lambda j, s: (j, 0, 0, 0)), plane, plane, block],
            out_specs=block,
            scratch_shapes=[pltpu.VMEM((HALF, 2 * HID), F32)],
        ),
        out_shape=jax.ShapeDtypeStruct((HALF, 4 * HID), BF16),
        compiler_params=pltpu.CompilerParams(vmem_limit_bytes=32 * 2**20),
        name="down",
    )(where, *pinned(cot, dn), df, fac)


def term_body(where, pick, dd, *refs):
    weights, out = refs[:-1], refs[-1]
    halves = []
    for h in range(2):
        total = None
        for i, w in enumerate(weights[h::2]):
            part = contract(dd[:, i * HID : (i + 1) * HID], w[...], 1, 1)
            total = part if total is None else total + part
        halves.append(total.astype(BF16))
    rows = contract(pick[...], jnp.concatenate(halves, axis=0), 1, 0).astype(BF16)
    for i in range(NX):
        out[(where[2] + NX - i) % NX] = rows[i * PIECE : (i + 1) * PIECE]


def term(where, dd, gw, uw, mw, ow):
    low = pl.BlockSpec((FEATS, HID), lambda j, s: (j, 0))
    high = pl.BlockSpec((FEATS, HID), lambda j, s: (j + NZ, 0))
    gw, uw, mw = pinned(gw, uw, mw)
    return pl.pallas_call(
        term_body,
        grid_spec=pltpu.PrefetchScalarGridSpec(
            num_scalar_prefetch=1,
            grid=(STEPS // 2,),
            in_specs=[
                pl.BlockSpec((2 * HALF, 2 * HALF), lambda j, s: (0, 0)),
                pl.BlockSpec((HALF, 4 * HID), lambda j, s: (0, 0)),
            ]
            + [low, high] * 4,
            out_specs=pl.BlockSpec((NX, PIECE, FEATS), lambda j, s: (0, 0, j)),
        ),
        out_shape=hbm((NX, PIECE, D // 2), BF16),
        compiler_params=pltpu.CompilerParams(vmem_limit_bytes=32 * 2**20),
        name="term",
    )(where, merge(), dd, gw, gw, uw, uw, mw, mw, ow, ow)


def grads_body(hn, hf, cn, cf, keep, send):
    total = None
    for z in range(NZ):
        part = contract(hn[z], cn[z, 0], 0, 0) + contract(hf[z], cf[z], 0, 0)
        total = part if total is None else total + part
    keep[...] = total[:HID]
    send[...] = total[HID:].astype(BF16)


def grads(hid_near, hid_far, cot_near, cot_far):
    vmem = pl.BlockSpec(memory_space=pltpu.MemorySpace.VMEM)
    return pl.pallas_call(
        grads_body,
        in_specs=[vmem] * 4,
        out_specs=[vmem] * 2,
        out_shape=[
            jax.ShapeDtypeStruct((HID, FEATS), F32),
            jax.ShapeDtypeStruct((HID, FEATS), BF16),
        ],
        compiler_params=pltpu.CompilerParams(vmem_limit_bytes=32 * 2**20),
        name="grads",
    )(hid_near, hid_far, cot_near, cot_far)


def selection(shape, order):
    source = np.arange(np.prod(shape)).reshape(shape).transpose(order).reshape(-1)
    return jnp.asarray(np.eye(source.size, dtype=np.float32)[source], BF16)


def merge():
    return selection((2, NX, NY, ROWS), (1, 2, 0, 3))


def spread(block, axis):
    n = lax.axis_size(axis)
    return lax.all_to_all(jnp.broadcast_to(block[None], (n, *block.shape)), axis, 0, 0)


def on_device(tokens, cotangent, gate_weight, up_weight, down_weight):
    core = lax.axis_index("c")
    where = jnp.stack([core, lax.axis_index("zl"), lax.axis_index("x")]).astype(jnp.int32)

    picked = jnp.where(core == 0, gate_weight, up_weight)
    picked, tokens = lax.optimization_barrier((picked, tokens))
    mine = neighbours(picked)
    down_near = lax.all_gather(down_weight, ("zh", "zl"), axis=0).reshape(NZ, 2 * HID, FEATS)

    block = spread(jnp.concatenate([tokens, cotangent], axis=0), "y").reshape(PIECE, D)
    left, right = shift(block, "x", 1), shift(block, "x", -1)
    n = PIECE // 2
    pieces = (block, left, shift(left[:n], "x", 1), shift(right[n:], "x", -1), right)

    tok, cot = split(where, pieces)
    cot_near = lax.all_to_all(cot, "zh", 0, 0)
    cot_far = swap(cot_near[:, 1], "c")
    tok, mine, down_near = lax.optimization_barrier((tok, mine, down_near))
    other, down_far = swap(mine, "c"), swap(down_near, "c")
    hidden, factors = gates(where, tok, gate_weight, up_weight, mine, other)
    dd = down(where, cot, down_near, down_far, factors)

    parts = term(where, dd, gate_weight, up_weight, mine, other)
    parts, hidden = lax.optimization_barrier((parts, hidden))
    parts = lax.all_to_all(parts.reshape(NX * NY, 2 * ROWS, D // 2), ("x", "y"), 0, 0)
    total = jnp.sum(parts.astype(F32), axis=0).astype(BF16)
    input_grad = jnp.concatenate([total[:ROWS], total[ROWS:]], axis=1)

    hid_near = lax.all_gather(hidden, "zh", axis=0)
    keep, send = grads(hid_near, swap(hid_near, "c"), cot_near, cot_far)
    down_grad = keep + swap(send, "zl").astype(F32)
    return (input_grad, down_grad)


def solution(mesh):
    fine = Mesh(mesh.devices.reshape(NZ, 2, 2, NY, NX), ("zh", "c", "zl", "y", "x"))
    placed = (
        P((*DP, *TENSOR), None),
        P((*DP, *TENSOR), None),
        P(None, TENSOR),
        P(None, TENSOR),
        P(TENSOR, DP),
    )
    return jax.shard_map(
        on_device,
        mesh=fine,
        in_specs=placed,
        out_specs=(P((*DP, *TENSOR), None), P(TENSOR, DP)),
        check_vma=False,
    )
```

```python
import functools

import jax
import jax.numpy as jnp
import numpy as np
from jax import lax
from jax.experimental import pallas as pl
from jax.experimental.pallas import tpu as pltpu
from jax.sharding import Mesh, PartitionSpec as P

BF16 = jnp.bfloat16
F32 = jnp.float32
DP = ("zh", "c")
TENSOR = ("zl", "y", "x")
NZ, NY, NX = 4, 8, 4
ROWS = 4
HALF = NX * NY * ROWS
D = 4096
HID = 256
FEATS = 512
STEPS = D // FEATS
PIECE = 2 * NY * ROWS


def contract(a, b, ca, cb):
    return lax.dot_general(a, b, (((ca,), (cb,)), ((), ())), preferred_element_type=F32)


def swap(value, axis):
    return lax.ppermute(value, axis, [(0, 1), (1, 0)])


def shift(value, axis, k):
    n = lax.axis_size(axis)
    return lax.ppermute(value, axis, [(i, (i + k) % n) for i in range(n)])


def neighbours(value):
    at = lambda zh, c, zl: ((zh % NZ) * 2 + c) * 2 + zl
    pairs = []
    for zh in range(NZ):
        pairs += [(at(zh, 0, 0), at(zh, 0, 1)), (at(zh, 0, 1), at(zh, 0, 0))]
        pairs += [(at(zh, 1, 1), at(zh + 1, 1, 0)), (at(zh + 1, 1, 0), at(zh, 1, 1))]
    return lax.ppermute(value, ("zh", "c", "zl"), pairs)


def split_body(where, pick, r0, r1, r2a, r2b, r3, tok, cot):
    n = NY * ROWS
    r2 = jnp.concatenate([r2a[...], r2b[...]], axis=0)
    for i, piece in enumerate((r0[...], r1[...], r2, r3[...])):
        rows = contract(pick[...], piece, 1, 0).astype(BF16)
        tok[i * n : (i + 1) * n] = rows[:n]
        cot[0, 0, i * n : (i + 1) * n] = rows[n:]


def split(where, pieces):
    piece = pl.BlockSpec((PIECE, FEATS), lambda j, s: (0, j))
    part = pl.BlockSpec((PIECE // 2, FEATS), lambda j, s: (0, j))
    return pl.pallas_call(
        split_body,
        grid_spec=pltpu.PrefetchScalarGridSpec(
            num_scalar_prefetch=1,
            grid=(STEPS,),
            in_specs=[pl.BlockSpec((PIECE, PIECE), lambda j, s: (0, 0)), piece, piece, part, part, piece],
            out_specs=[
                pl.BlockSpec((HALF, FEATS), lambda j, s: (0, j)),
                pl.BlockSpec((1, 1, HALF, FEATS), lambda j, s: (j // 2, flip(j % 2, s[0]), 0, 0)),
            ],
        ),
        out_shape=[
            hbm((HALF, D), BF16),
            hbm((NZ, 2, HALF, FEATS), BF16),
        ],
        compiler_params=pltpu.CompilerParams(vmem_limit_bytes=32 * 2**20),
        name="split",
    )(where, selection((NY, 2, ROWS), (1, 0, 2)), *pieces)


def hbm(shape, dtype):
    return pltpu.MemorySpace.HBM(shape, dtype)


def pinned(*values):
    return [pltpu.with_memory_space_constraint(v, pltpu.MemorySpace.HBM) for v in values]


def flip(a, b):
    return a + b - 2 * a * b


def gates_body(where, tok, gw, uw, mw, ow, hid, fac, acc):
    step = pl.program_id(0)

    @pl.when(step == 0)
    def _():
        acc[...] = jnp.zeros_like(acc)

    t = tok[...]
    for i, w in enumerate((gw, uw, mw, ow)):
        acc[:, i * HID : (i + 1) * HID] += contract(t, w[...], 1, 0)

    @pl.when(step == STEPS - 1)
    def _():
        first = where[0] == 0
        pm, po = acc[:, 2 * HID : 3 * HID], acc[:, 3 * HID :]
        sides = (
            (acc[:, :HID], acc[:, HID : 2 * HID]),
            (jnp.where(first, pm, po), jnp.where(first, po, pm)),
        )
        for i, (gate, up) in enumerate(sides):
            sigma = jax.nn.sigmoid(gate)
            silu = gate * sigma
            hid[:, i * HID : (i + 1) * HID] = (silu * up).astype(BF16)
            slope = up * sigma * (1.0 + gate * (1.0 - sigma))
            if i == 1:
                slope, silu = jnp.where(first, slope, silu), jnp.where(first, silu, slope)
            fac[:, 2 * i * HID : (2 * i + 1) * HID] = slope
            fac[:, (2 * i + 1) * HID : (2 * i + 2) * HID] = silu


def gates(where, tok, gw, uw, mw, ow):
    weight = pl.BlockSpec((FEATS, HID), lambda j, s: (j, 0))
    return pl.pallas_call(
        gates_body,
        grid_spec=pltpu.PrefetchScalarGridSpec(
            num_scalar_prefetch=1,
            grid=(STEPS,),
            in_specs=[pl.BlockSpec((HALF, FEATS), lambda j, s: (0, j))] + [weight] * 4,
            out_specs=[
                pl.BlockSpec((HALF, 2 * HID), lambda j, s: (0, 0)),
                pl.BlockSpec((HALF, 4 * HID), lambda j, s: (0, 0)),
            ],
            scratch_shapes=[pltpu.VMEM((HALF, 4 * HID), F32)],
        ),
        out_shape=[
            jax.ShapeDtypeStruct((HALF, 2 * HID), BF16),
            jax.ShapeDtypeStruct((HALF, 4 * HID), F32),
        ],
        compiler_params=pltpu.CompilerParams(vmem_limit_bytes=32 * 2**20),
        name="gates",
    )(where, *pinned(tok, gw, uw, mw), ow)


def down_body(where, cot, dn, df, fac, dd, acc):
    step = pl.program_id(0)

    @pl.when(step == 0)
    def _():
        acc[...] = jnp.zeros_like(acc)

    acc[...] += contract(cot[0, 0], dn[0], 1, 1) + contract(cot[0, 1], df[0], 1, 1)

    @pl.when(step == NZ - 1)
    def _():
        low = where[1] == 0
        dl, dh = acc[:, :HID], acc[:, HID:]
        for i, d_hidden in enumerate((jnp.where(low, dl, dh), jnp.where(low, dh, dl))):
            for k in (2 * i, 2 * i + 1):
                dd[:, k * HID : (k + 1) * HID] = (d_hidden * fac[:, k * HID : (k + 1) * HID]).astype(BF16)


def down(where, cot, dn, df, fac):
    plane = pl.BlockSpec((1, 2 * HID, FEATS), lambda j, s: (j, 0, 0))
    block = pl.BlockSpec((HALF, 4 * HID), lambda j, s: (0, 0))
    return pl.pallas_call(
        down_body,
        grid_spec=pltpu.PrefetchScalarGridSpec(
            num_scalar_prefetch=1,
            grid=(NZ,),
            in_specs=[pl.BlockSpec((1, 2, HALF, FEATS), lambda j, s: (j, 0, 0, 0)), plane, plane, block],
            out_specs=block,
            scratch_shapes=[pltpu.VMEM((HALF, 2 * HID), F32)],
        ),
        out_shape=jax.ShapeDtypeStruct((HALF, 4 * HID), BF16),
        compiler_params=pltpu.CompilerParams(vmem_limit_bytes=32 * 2**20),
        name="down",
    )(where, *pinned(cot, dn), df, fac)


def term_body(where, pick, dd, *refs):
    weights, out = refs[:-1], refs[-1]
    halves = []
    for h in range(2):
        total = None
        for i, w in enumerate(weights[h::2]):
            part = contract(dd[:, i * HID : (i + 1) * HID], w[...], 1, 1)
            total = part if total is None else total + part
        halves.append(total.astype(BF16))
    rows = contract(pick[...], jnp.concatenate(halves, axis=0), 1, 0).astype(BF16)
    for i in range(NX):
        out[(where[2] + NX - i) % NX] = rows[i * PIECE : (i + 1) * PIECE]


def term(where, dd, gw, uw, mw, ow):
    low = pl.BlockSpec((FEATS, HID), lambda j, s: (j, 0))
    high = pl.BlockSpec((FEATS, HID), lambda j, s: (j + NZ, 0))
    gw, uw, mw = pinned(gw, uw, mw)
    return pl.pallas_call(
        term_body,
        grid_spec=pltpu.PrefetchScalarGridSpec(
            num_scalar_prefetch=1,
            grid=(STEPS // 2,),
            in_specs=[
                pl.BlockSpec((2 * HALF, 2 * HALF), lambda j, s: (0, 0)),
                pl.BlockSpec((HALF, 4 * HID), lambda j, s: (0, 0)),
            ]
            + [low, high] * 4,
            out_specs=pl.BlockSpec((NX, PIECE, FEATS), lambda j, s: (0, 0, j)),
        ),
        out_shape=hbm((NX, PIECE, D // 2), BF16),
        compiler_params=pltpu.CompilerParams(vmem_limit_bytes=32 * 2**20),
        name="term",
    )(where, merge(), dd, gw, gw, uw, uw, mw, mw, ow, ow)


def grads_body(where, h0, h1, h2, h3, cot, *outs):
    for far in range(2):
        total = None
        for j, h in enumerate((h0, h1, h2, h3)):
            part = contract(h[...], cot[(where[3] + NZ - j) % NZ, far], 0, 0)
            total = part if total is None else total + part
        for side, out in enumerate(outs[far::2]):
            out[...] = total[side * HID : (side + 1) * HID].astype(out.dtype)


def grads(where, hid, cot):
    vmem = pl.BlockSpec(memory_space=pltpu.MemorySpace.VMEM)
    return pl.pallas_call(
        grads_body,
        in_specs=[pl.BlockSpec(memory_space=pltpu.MemorySpace.SMEM)] + [vmem] * 5,
        out_specs=[vmem] * 4,
        out_shape=[jax.ShapeDtypeStruct((HID, FEATS), F32)] + [jax.ShapeDtypeStruct((HID, FEATS), BF16)] * 3,
        compiler_params=pltpu.CompilerParams(vmem_limit_bytes=32 * 2**20),
        name="grads",
    )(where, *hid, cot)


def selection(shape, order):
    source = np.arange(np.prod(shape)).reshape(shape).transpose(order).reshape(-1)
    return jnp.asarray(np.eye(source.size, dtype=np.float32)[source], BF16)


def merge():
    return selection((2, NX, NY, ROWS), (1, 2, 0, 3))


def spread(block, axis):
    n = lax.axis_size(axis)
    return lax.all_to_all(jnp.broadcast_to(block[None], (n, *block.shape)), axis, 0, 0)


def on_device(tokens, cotangent, gate_weight, up_weight, down_weight):
    core = lax.axis_index("c")
    where = [core, lax.axis_index("zl"), lax.axis_index("x"), lax.axis_index("zh")]
    where = jnp.stack(where).astype(jnp.int32)

    picked = jnp.where(core == 0, gate_weight, up_weight)
    picked, tokens = lax.optimization_barrier((picked, tokens))
    mine = neighbours(picked)
    down_near = lax.all_gather(down_weight, ("zh", "zl"), axis=0).reshape(NZ, 2 * HID, FEATS)

    block = spread(jnp.concatenate([tokens, cotangent], axis=0), "y").reshape(PIECE, D)
    left, right = shift(block, "x", 1), shift(block, "x", -1)
    n = PIECE // 2
    pieces = (block, left, shift(left[:n], "x", 1), shift(right[n:], "x", -1), right)

    tok, cot = split(where, pieces)
    cot_near = lax.all_to_all(cot, "zh", 0, 0)
    tok, mine, down_near = lax.optimization_barrier((tok, mine, down_near))
    other, down_far = swap(mine, "c"), swap(down_near, "c")
    hidden, factors = gates(where, tok, gate_weight, up_weight, mine, other)
    dd = down(where, cot, down_near, down_far, factors)

    parts = term(where, dd, gate_weight, up_weight, mine, other)
    parts, hidden = lax.optimization_barrier((parts, hidden))
    parts = lax.all_to_all(parts.reshape(NX * NY, 2 * ROWS, D // 2), ("x", "y"), 0, 0)
    total = jnp.sum(parts.astype(F32), axis=0).astype(BF16)
    input_grad = jnp.concatenate([total[:ROWS], total[ROWS:]], axis=1)

    hid = [hidden] + [shift(hidden, "zh", k) for k in (1, 2, 3)]
    keep, core_part, zl_part, both_part = grads(where, hid, cot_near)
    down_grad = (
        keep
        + swap(core_part, "c").astype(F32)
        + swap(zl_part, "zl").astype(F32)
        + lax.ppermute(both_part, ("c", "zl"), [(0, 3), (3, 0), (1, 2), (2, 1)]).astype(F32)
    )
    return (input_grad, down_grad)


def solution(mesh):
    fine = Mesh(mesh.devices.reshape(NZ, 2, 2, NY, NX), ("zh", "c", "zl", "y", "x"))
    placed = (
        P((*DP, *TENSOR), None),
        P((*DP, *TENSOR), None),
        P(None, TENSOR),
        P(None, TENSOR),
        P(TENSOR, DP),
    )
    return jax.shard_map(
        on_device,
        mesh=fine,
        in_specs=placed,
        out_specs=(P((*DP, *TENSOR), None), P(TENSOR, DP)),
        check_vma=False,
    )
```

```python
import functools

import jax
import jax.numpy as jnp
import numpy as np
from jax import lax
from jax.experimental import pallas as pl
from jax.experimental.pallas import tpu as pltpu
from jax.sharding import Mesh, PartitionSpec as P

BF16 = jnp.bfloat16
F32 = jnp.float32
DP = ("zh", "c")
TENSOR = ("zl", "y", "x")
NZ, NY, NX = 4, 8, 4
ROWS = 4
HALF = NX * NY * ROWS
D = 4096
HID = 256
FEATS = 512
STEPS = D // FEATS
PIECE = 2 * NY * ROWS


def contract(a, b, ca, cb):
    return lax.dot_general(a, b, (((ca,), (cb,)), ((), ())), preferred_element_type=F32)


def swap(value, axis):
    return lax.ppermute(value, axis, [(0, 1), (1, 0)])


def shift(value, axis, k):
    n = lax.axis_size(axis)
    return lax.ppermute(value, axis, [(i, (i + k) % n) for i in range(n)])


def neighbours(value):
    at = lambda zh, c, zl: ((zh % NZ) * 2 + c) * 2 + zl
    pairs = []
    for zh in range(NZ):
        pairs += [(at(zh, 0, 0), at(zh, 0, 1)), (at(zh, 0, 1), at(zh, 0, 0))]
        pairs += [(at(zh, 1, 1), at(zh + 1, 1, 0)), (at(zh + 1, 1, 0), at(zh, 1, 1))]
    return lax.ppermute(value, ("zh", "c", "zl"), pairs)


def pinned(*values):
    return [pltpu.with_memory_space_constraint(v, pltpu.MemorySpace.HBM) for v in values]


def flip(a, b):
    return a + b - 2 * a * b


def forward_body(where, pick, r0, r1, r2a, r2b, r3, gw, uw, mw, ow, dn, df, exch, dd, tok, cot, acc, dacc):
    step = pl.program_id(0)
    zh, far = step // 2, step % 2

    @pl.when(step == 0)
    def _():
        acc[...] = jnp.zeros_like(acc)
        dacc[...] = jnp.zeros_like(dacc)

    n = NY * ROWS
    r2 = jnp.concatenate([r2a[...], r2b[...]], axis=0)
    for i, piece in enumerate((r0[...], r1[...], r2, r3[...])):
        rows = contract(pick[...], piece, 1, 0).astype(BF16)
        tok[i * n : (i + 1) * n] = rows[:n]
        cot[i * n : (i + 1) * n] = rows[n:]
    t = tok[...]
    for i, w in enumerate((gw, uw, mw, ow)):
        acc[:, i * HID : (i + 1) * HID] += contract(t, w[...], 1, 0)
    exch[zh, far] = cot[...]

    @pl.when(far == 0)
    def _():
        dacc[...] += contract(cot[...], dn[0], 1, 1)

    @pl.when(far == 1)
    def _():
        dacc[...] += contract(cot[...], df[0], 1, 1)

    @pl.when(step == STEPS - 1)
    def _():
        first, low = where[0] == 0, where[1] == 0
        pm, po = acc[:, 2 * HID : 3 * HID], acc[:, 3 * HID :]
        dl, dh = dacc[:, :HID], dacc[:, HID:]
        sides = (
            (acc[:, :HID], acc[:, HID : 2 * HID], jnp.where(low, dl, dh)),
            (jnp.where(first, pm, po), jnp.where(first, po, pm), jnp.where(low, dh, dl)),
        )
        for i, (gate, up, d_hidden) in enumerate(sides):
            sigma = jax.nn.sigmoid(gate)
            silu = gate * sigma
            hidden = (silu * up).astype(BF16)
            for z in range(NZ):
                exch[z, 2, :, i * HID : (i + 1) * HID] = hidden
            d_up = d_hidden * silu
            d_gate = d_hidden * up * sigma * (1.0 + gate * (1.0 - sigma))
            if i == 1:
                d_gate, d_up = jnp.where(first, d_gate, d_up), jnp.where(first, d_up, d_gate)
            dd[:, 2 * i * HID : (2 * i + 1) * HID] = d_gate.astype(BF16)
            dd[:, (2 * i + 1) * HID : (2 * i + 2) * HID] = d_up.astype(BF16)


def forward(where, pieces, gw, uw, mw, ow, dn, df):
    def column(j, s):
        return (j // 2) * 2 + flip(j % 2, s[0])

    whole = lambda *shape: pl.BlockSpec(shape, lambda j, s: (0,) * len(shape))
    piece = pl.BlockSpec((PIECE, FEATS), lambda j, s: (0, column(j, s)))
    part = pl.BlockSpec((PIECE // 2, FEATS), lambda j, s: (0, column(j, s)))
    weight = pl.BlockSpec((FEATS, HID), lambda j, s: (column(j, s), 0))
    plane = pl.BlockSpec((1, 2 * HID, FEATS), lambda j, s: (j // 2, 0, 0))
    return pl.pallas_call(
        forward_body,
        grid_spec=pltpu.PrefetchScalarGridSpec(
            num_scalar_prefetch=1,
            grid=(STEPS,),
            in_specs=[whole(PIECE, PIECE), piece, piece, part, part, piece] + [weight] * 4 + [plane] * 2,
            out_specs=[whole(NZ, 3, HALF, FEATS), whole(HALF, 4 * HID)],
            scratch_shapes=[
                pltpu.VMEM((HALF, FEATS), BF16),
                pltpu.VMEM((HALF, FEATS), BF16),
                pltpu.VMEM((HALF, 4 * HID), F32),
                pltpu.VMEM((HALF, 2 * HID), F32),
            ],
        ),
        out_shape=[
            jax.ShapeDtypeStruct((NZ, 3, HALF, FEATS), BF16),
            jax.ShapeDtypeStruct((HALF, 4 * HID), BF16),
        ],
        compiler_params=pltpu.CompilerParams(vmem_limit_bytes=32 * 2**20),
        name="forward",
    )(where, selection((NY, 2, ROWS), (1, 0, 2)), *pieces, *pinned(gw, uw, mw), ow, *pinned(dn), df)


def term_body(pick, dd, *refs):
    weights, outs = refs[:-NX], refs[-NX:]
    halves = []
    for h in range(2):
        total = None
        for i, w in enumerate(weights[h::2]):
            part = contract(dd[:, i * HID : (i + 1) * HID], w[...], 1, 1)
            total = part if total is None else total + part
        halves.append(total.astype(BF16))
    rows = contract(pick[...], jnp.concatenate(halves, axis=0), 1, 0).astype(BF16)
    for i, out in enumerate(outs):
        out[...] = rows[i * PIECE : (i + 1) * PIECE]


def term(dd, gw, uw, mw, ow):
    low = pl.BlockSpec((FEATS, HID), lambda j: (j, 0))
    high = pl.BlockSpec((FEATS, HID), lambda j: (j + NZ, 0))
    gw, uw, mw = pinned(gw, uw, mw)
    return pl.pallas_call(
        term_body,
        grid=(STEPS // 2,),
        in_specs=[
            pl.BlockSpec((2 * HALF, 2 * HALF), lambda j: (0, 0)),
            pl.BlockSpec((HALF, 4 * HID), lambda j: (0, 0)),
        ]
        + [low, high] * 4,
        out_specs=[pl.BlockSpec((PIECE, FEATS), lambda j: (0, j))] * NX,
        out_shape=[jax.ShapeDtypeStruct((PIECE, D // 2), BF16)] * NX,
        compiler_params=pltpu.CompilerParams(vmem_limit_bytes=32 * 2**20),
        name="term",
    )(merge(), dd, gw, gw, uw, uw, mw, mw, ow, ow)


def grads_body(exch, *outs):
    for far in range(2):
        total = None
        for z in range(NZ):
            part = contract(exch[z, 2], exch[z, far], 0, 0)
            total = part if total is None else total + part
        for side, out in enumerate(outs[far::2]):
            out[...] = total[side * HID : (side + 1) * HID].astype(out.dtype)


def grads(exch):
    vmem = pl.BlockSpec(memory_space=pltpu.MemorySpace.VMEM)
    return pl.pallas_call(
        grads_body,
        in_specs=[vmem],
        out_specs=[vmem] * 4,
        out_shape=[jax.ShapeDtypeStruct((HID, FEATS), F32)] + [jax.ShapeDtypeStruct((HID, FEATS), BF16)] * 3,
        compiler_params=pltpu.CompilerParams(vmem_limit_bytes=32 * 2**20),
        name="grads",
    )(exch)


def selection(shape, order):
    source = np.arange(np.prod(shape)).reshape(shape).transpose(order).reshape(-1)
    return jnp.asarray(np.eye(source.size, dtype=np.float32)[source], BF16)


def merge():
    return selection((2, NX, NY, ROWS), (1, 2, 0, 3))


def spread(block, axis):
    n = lax.axis_size(axis)
    return lax.all_to_all(jnp.broadcast_to(block[None], (n, *block.shape)), axis, 0, 0)


def on_device(tokens, cotangent, gate_weight, up_weight, down_weight):
    core = lax.axis_index("c")
    where = jnp.stack([core, lax.axis_index("zl")]).astype(jnp.int32)

    picked = jnp.where(core == 0, gate_weight, up_weight)
    picked, tokens = lax.optimization_barrier((picked, tokens))
    mine = neighbours(picked)
    down_near = lax.all_gather(down_weight, ("zh", "zl"), axis=0).reshape(NZ, 2 * HID, FEATS)

    block = spread(jnp.concatenate([tokens, cotangent], axis=0), "y").reshape(PIECE, D)
    left, right = shift(block, "x", 1), shift(block, "x", -1)
    n = PIECE // 2
    far = shift(left[:n], "x", 1), shift(right[n:], "x", -1)
    far, mine, down_near = lax.optimization_barrier((far, mine, down_near))
    other, down_far = swap(mine, "c"), swap(down_near, "c")
    pieces = (block, left, *far, right)
    exch, dd = forward(where, pieces, gate_weight, up_weight, mine, other, down_near, down_far)

    exch = lax.all_to_all(exch, "zh", 0, 0)
    parts = term(dd, gate_weight, up_weight, mine, other)
    total = parts[0].astype(F32)
    for k in (1, 2, 3):
        total = total + shift(parts[k], "x", -k).astype(F32)
    total, exch = lax.optimization_barrier((total.astype(BF16), exch))
    parts = lax.all_to_all(total.reshape(NY, 2 * ROWS, D // 2), "y", 0, 0)
    total = jnp.sum(parts.astype(F32), axis=0).astype(BF16)
    input_grad = jnp.concatenate([total[:ROWS], total[ROWS:]], axis=1)

    keep, core_part, zl_part, both_part = grads(exch)
    down_grad = (
        keep
        + swap(core_part, "c").astype(F32)
        + swap(zl_part, "zl").astype(F32)
        + lax.ppermute(both_part, ("c", "zl"), [(0, 3), (3, 0), (1, 2), (2, 1)]).astype(F32)
    )
    return (input_grad, down_grad)


def solution(mesh):
    fine = Mesh(mesh.devices.reshape(NZ, 2, 2, NY, NX), ("zh", "c", "zl", "y", "x"))
    placed = (
        P((*DP, *TENSOR), None),
        P((*DP, *TENSOR), None),
        P(None, TENSOR),
        P(None, TENSOR),
        P(TENSOR, DP),
    )
    return jax.shard_map(
        on_device,
        mesh=fine,
        in_specs=placed,
        out_specs=(P((*DP, *TENSOR), None), P(TENSOR, DP)),
        check_vma=False,
    )
```

```python
import functools

import jax
import jax.numpy as jnp
import numpy as np
from jax import lax
from jax.experimental import pallas as pl
from jax.experimental.pallas import tpu as pltpu
from jax.sharding import Mesh, PartitionSpec as P

BF16 = jnp.bfloat16
F32 = jnp.float32
DP = ("zh", "c")
TENSOR = ("zl", "y", "x")
NZ, NY, NX = 4, 8, 4
ROWS = 4
HALF = NX * NY * ROWS
D = 4096
HID = 256
FEATS = 512
STEPS = D // FEATS
PIECE = 2 * NY * ROWS


def contract(a, b, ca, cb):
    return lax.dot_general(a, b, (((ca,), (cb,)), ((), ())), preferred_element_type=F32)


def swap(value, axis):
    return lax.ppermute(value, axis, [(0, 1), (1, 0)])


def shift(value, axis, k):
    n = lax.axis_size(axis)
    return lax.ppermute(value, axis, [(i, (i + k) % n) for i in range(n)])


def neighbours(value):
    at = lambda zh, c, zl: ((zh % NZ) * 2 + c) * 2 + zl
    pairs = []
    for zh in range(NZ):
        pairs += [(at(zh, 0, 0), at(zh, 0, 1)), (at(zh, 0, 1), at(zh, 0, 0))]
        pairs += [(at(zh, 1, 1), at(zh + 1, 1, 0)), (at(zh + 1, 1, 0), at(zh, 1, 1))]
    return lax.ppermute(value, ("zh", "c", "zl"), pairs)


def split_body(where, pick, r0, r1, r2a, r2b, r3, tok, cot):
    n = NY * ROWS
    r2 = jnp.concatenate([r2a[...], r2b[...]], axis=0)
    for i, piece in enumerate((r0[...], r1[...], r2, r3[...])):
        rows = contract(pick[...], piece, 1, 0).astype(BF16)
        tok[i * n : (i + 1) * n] = rows[:n]
        cot[0, 0, i * n : (i + 1) * n] = rows[n:]


def split(where, pieces):
    piece = pl.BlockSpec((PIECE, FEATS), lambda j, s: (0, j))
    part = pl.BlockSpec((PIECE // 2, FEATS), lambda j, s: (0, j))
    return pl.pallas_call(
        split_body,
        grid_spec=pltpu.PrefetchScalarGridSpec(
            num_scalar_prefetch=1,
            grid=(STEPS,),
            in_specs=[pl.BlockSpec((PIECE, PIECE), lambda j, s: (0, 0)), piece, piece, part, part, piece],
            out_specs=[
                pl.BlockSpec((HALF, FEATS), lambda j, s: (0, j)),
                pl.BlockSpec((1, 1, HALF, FEATS), lambda j, s: (j // 2, flip(j % 2, s[0]), 0, 0)),
            ],
        ),
        out_shape=[
            hbm((HALF, D), BF16),
            hbm((NZ, 2, HALF, FEATS), BF16),
        ],
        compiler_params=pltpu.CompilerParams(vmem_limit_bytes=32 * 2**20),
        name="split",
    )(where, selection((NY, 2, ROWS), (1, 0, 2)), *pieces)


def hbm(shape, dtype):
    return pltpu.MemorySpace.HBM(shape, dtype)


def pinned(*values):
    return [pltpu.with_memory_space_constraint(v, pltpu.MemorySpace.HBM) for v in values]


def flip(a, b):
    return a + b - 2 * a * b


def gates_body(where, tok, gw, uw, mw, ow, hid, fac, acc):
    step = pl.program_id(0)

    @pl.when(step == 0)
    def _():
        acc[...] = jnp.zeros_like(acc)

    t = tok[...]
    for i, w in enumerate((gw, uw, mw, ow)):
        acc[:, i * HID : (i + 1) * HID] += contract(t, w[...], 1, 0)

    @pl.when(step == STEPS - 1)
    def _():
        first = where[0] == 0
        pm, po = acc[:, 2 * HID : 3 * HID], acc[:, 3 * HID :]
        sides = (
            (acc[:, :HID], acc[:, HID : 2 * HID]),
            (jnp.where(first, pm, po), jnp.where(first, po, pm)),
        )
        for i, (gate, up) in enumerate(sides):
            sigma = jax.nn.sigmoid(gate)
            silu = gate * sigma
            hid[:, i * HID : (i + 1) * HID] = (silu * up).astype(BF16)
            slope = up * sigma * (1.0 + gate * (1.0 - sigma))
            if i == 1:
                slope, silu = jnp.where(first, slope, silu), jnp.where(first, silu, slope)
            fac[:, 2 * i * HID : (2 * i + 1) * HID] = slope
            fac[:, (2 * i + 1) * HID : (2 * i + 2) * HID] = silu


def gates(where, tok, gw, uw, mw, ow):
    weight = pl.BlockSpec((FEATS, HID), lambda j, s: (j, 0))
    return pl.pallas_call(
        gates_body,
        grid_spec=pltpu.PrefetchScalarGridSpec(
            num_scalar_prefetch=1,
            grid=(STEPS,),
            in_specs=[pl.BlockSpec((HALF, FEATS), lambda j, s: (0, j))] + [weight] * 4,
            out_specs=[
                pl.BlockSpec((HALF, 2 * HID), lambda j, s: (0, 0)),
                pl.BlockSpec((HALF, 4 * HID), lambda j, s: (0, 0)),
            ],
            scratch_shapes=[pltpu.VMEM((HALF, 4 * HID), F32)],
        ),
        out_shape=[
            jax.ShapeDtypeStruct((HALF, 2 * HID), BF16),
            jax.ShapeDtypeStruct((HALF, 4 * HID), F32),
        ],
        compiler_params=pltpu.CompilerParams(vmem_limit_bytes=32 * 2**20),
        name="gates",
    )(where, *pinned(tok, gw, uw, mw), ow)


def down_body(where, cot, dn, df, fac, dd, acc):
    step = pl.program_id(0)

    @pl.when(step == 0)
    def _():
        acc[...] = jnp.zeros_like(acc)

    acc[...] += contract(cot[0, 0], dn[0], 1, 1) + contract(cot[0, 1], df[0], 1, 1)

    @pl.when(step == NZ - 1)
    def _():
        low = where[1] == 0
        dl, dh = acc[:, :HID], acc[:, HID:]
        for i, d_hidden in enumerate((jnp.where(low, dl, dh), jnp.where(low, dh, dl))):
            for k in (2 * i, 2 * i + 1):
                dd[:, k * HID : (k + 1) * HID] = (d_hidden * fac[:, k * HID : (k + 1) * HID]).astype(BF16)


def down(where, cot, dn, df, fac):
    plane = pl.BlockSpec((1, 2 * HID, FEATS), lambda j, s: (j, 0, 0))
    block = pl.BlockSpec((HALF, 4 * HID), lambda j, s: (0, 0))
    return pl.pallas_call(
        down_body,
        grid_spec=pltpu.PrefetchScalarGridSpec(
            num_scalar_prefetch=1,
            grid=(NZ,),
            in_specs=[pl.BlockSpec((1, 2, HALF, FEATS), lambda j, s: (j, 0, 0, 0)), plane, plane, block],
            out_specs=block,
            scratch_shapes=[pltpu.VMEM((HALF, 2 * HID), F32)],
        ),
        out_shape=jax.ShapeDtypeStruct((HALF, 4 * HID), BF16),
        compiler_params=pltpu.CompilerParams(vmem_limit_bytes=32 * 2**20),
        name="down",
    )(where, *pinned(cot, dn), df, fac)


def term_body(where, pick, dd, *refs):
    weights, out = refs[:-1], refs[-1]
    halves = []
    for h in range(2):
        total = None
        for i, w in enumerate(weights[h::2]):
            part = contract(dd[:, i * HID : (i + 1) * HID], w[...], 1, 1)
            total = part if total is None else total + part
        halves.append(total.astype(BF16))
    rows = contract(pick[...], jnp.concatenate(halves, axis=0), 1, 0).astype(BF16)
    for i in range(NX):
        out[(where[2] + NX - i) % NX] = rows[i * PIECE : (i + 1) * PIECE]


def term(where, dd, gw, uw, mw, ow):
    low = pl.BlockSpec((FEATS, HID), lambda j, s: (j, 0))
    high = pl.BlockSpec((FEATS, HID), lambda j, s: (j + NZ, 0))
    gw, uw, mw = pinned(gw, uw, mw)
    return pl.pallas_call(
        term_body,
        grid_spec=pltpu.PrefetchScalarGridSpec(
            num_scalar_prefetch=1,
            grid=(STEPS // 2,),
            in_specs=[
                pl.BlockSpec((2 * HALF, 2 * HALF), lambda j, s: (0, 0)),
                pl.BlockSpec((HALF, 4 * HID), lambda j, s: (0, 0)),
            ]
            + [low, high] * 4,
            out_specs=pl.BlockSpec((NX, PIECE, FEATS), lambda j, s: (0, 0, j)),
        ),
        out_shape=hbm((NX, PIECE, D // 2), BF16),
        compiler_params=pltpu.CompilerParams(vmem_limit_bytes=32 * 2**20),
        name="term",
    )(where, merge(), dd, gw, gw, uw, uw, mw, mw, ow, ow)


def grads_body(where, h, cn, cf, keep, send):
    total = None
    for z in range(NZ):
        part = contract(h[z, 0], cn[z, 0], 0, 0) + contract(h[z, 1], cf[z], 0, 0)
        total = part if total is None else total + part
    keep[...] = total[:HID]
    send[...] = total[HID:].astype(BF16)


def grads(where, hidden, cot_near, cot_far):
    vmem = pl.BlockSpec(memory_space=pltpu.MemorySpace.VMEM)
    return pl.pallas_call(
        grads_body,
        in_specs=[pl.BlockSpec(memory_space=pltpu.MemorySpace.SMEM)] + [vmem] * 3,
        out_specs=[vmem] * 2,
        out_shape=[
            jax.ShapeDtypeStruct((HID, FEATS), F32),
            jax.ShapeDtypeStruct((HID, FEATS), BF16),
        ],
        compiler_params=pltpu.CompilerParams(vmem_limit_bytes=32 * 2**20),
        name="grads",
    )(where, hidden, cot_near, cot_far)


def selection(shape, order):
    source = np.arange(np.prod(shape)).reshape(shape).transpose(order).reshape(-1)
    return jnp.asarray(np.eye(source.size, dtype=np.float32)[source], BF16)


def merge():
    return selection((2, NX, NY, ROWS), (1, 2, 0, 3))


def spread(block, axis):
    n = lax.axis_size(axis)
    return lax.all_to_all(jnp.broadcast_to(block[None], (n, *block.shape)), axis, 0, 0)


def on_device(tokens, cotangent, gate_weight, up_weight, down_weight):
    core = lax.axis_index("c")
    where = jnp.stack([core, lax.axis_index("zl"), lax.axis_index("x")]).astype(jnp.int32)

    picked = jnp.where(core == 0, gate_weight, up_weight)
    picked, tokens = lax.optimization_barrier((picked, tokens))
    mine = neighbours(picked)
    down_near = lax.all_gather(down_weight, ("zh", "zl"), axis=0).reshape(NZ, 2 * HID, FEATS)

    block = spread(jnp.concatenate([tokens, cotangent], axis=0), "y").reshape(PIECE, D)
    left, right = shift(block, "x", 1), shift(block, "x", -1)
    n = PIECE // 2
    pieces = (block, left, shift(left[:n], "x", 1), shift(right[n:], "x", -1), right)

    tok, cot = split(where, pieces)
    cot_near = lax.all_to_all(cot, "zh", 0, 0)
    cot_far = swap(cot_near[:, 1], "c")
    tok, mine, down_near = lax.optimization_barrier((tok, mine, down_near))
    other, down_far = swap(mine, "c"), swap(down_near, "c")
    hidden, factors = gates(where, tok, gate_weight, up_weight, mine, other)
    hidden = lax.all_gather(jnp.stack([hidden, swap(hidden, "c")]), "zh", axis=0)
    dd = down(where, cot, down_near, down_far, factors)

    parts = term(where, dd, gate_weight, up_weight, mine, other)
    parts = lax.all_to_all(parts.reshape(NX * NY, 2 * ROWS, D // 2), ("x", "y"), 0, 0)
    total = jnp.sum(parts.astype(F32), axis=0).astype(BF16)
    input_grad = jnp.concatenate([total[:ROWS], total[ROWS:]], axis=1)

    keep, send = grads(where, hidden, cot_near, cot_far)
    down_grad = keep + swap(send, "zl").astype(F32)
    return (input_grad, down_grad)


def solution(mesh):
    fine = Mesh(mesh.devices.reshape(NZ, 2, 2, NY, NX), ("zh", "c", "zl", "y", "x"))
    placed = (
        P((*DP, *TENSOR), None),
        P((*DP, *TENSOR), None),
        P(None, TENSOR),
        P(None, TENSOR),
        P(TENSOR, DP),
    )
    return jax.shard_map(
        on_device,
        mesh=fine,
        in_specs=placed,
        out_specs=(P((*DP, *TENSOR), None), P(TENSOR, DP)),
        check_vma=False,
    )
```

```python
import functools

import jax
import jax.numpy as jnp
import numpy as np
from jax import lax
from jax.experimental import pallas as pl
from jax.experimental.pallas import tpu as pltpu
from jax.sharding import Mesh, PartitionSpec as P

BF16 = jnp.bfloat16
F32 = jnp.float32
DP = ("zh", "c")
TENSOR = ("zl", "y", "x")
NZ, NY, NX = 4, 8, 4
ROWS = 4
HALF = NX * NY * ROWS
D = 4096
HID = 256
FEATS = 512
STEPS = D // FEATS
PIECE = 2 * NY * ROWS


def contract(a, b, ca, cb):
    return lax.dot_general(a, b, (((ca,), (cb,)), ((), ())), preferred_element_type=F32)


def swap(value, axis):
    return lax.ppermute(value, axis, [(0, 1), (1, 0)])


def shift(value, axis, k):
    n = lax.axis_size(axis)
    return lax.ppermute(value, axis, [(i, (i + k) % n) for i in range(n)])


def neighbours(value):
    at = lambda zh, c, zl: ((zh % NZ) * 2 + c) * 2 + zl
    pairs = []
    for zh in range(NZ):
        pairs += [(at(zh, 0, 0), at(zh, 0, 1)), (at(zh, 0, 1), at(zh, 0, 0))]
        pairs += [(at(zh, 1, 1), at(zh + 1, 1, 0)), (at(zh + 1, 1, 0), at(zh, 1, 1))]
    return lax.ppermute(value, ("zh", "c", "zl"), pairs)


def split_body(where, pick, r0, r1, r2a, r2b, r3, tok, cot):
    n = NY * ROWS
    r2 = jnp.concatenate([r2a[...], r2b[...]], axis=0)
    for i, piece in enumerate((r0[...], r1[...], r2, r3[...])):
        rows = contract(pick[...], piece, 1, 0).astype(BF16)
        tok[i * n : (i + 1) * n] = rows[:n]
        cot[0, 0, i * n : (i + 1) * n] = rows[n:]


def split(where, pieces):
    piece = pl.BlockSpec((PIECE, FEATS), lambda j, s: (0, j))
    part = pl.BlockSpec((PIECE // 2, FEATS), lambda j, s: (0, j))
    return pl.pallas_call(
        split_body,
        grid_spec=pltpu.PrefetchScalarGridSpec(
            num_scalar_prefetch=1,
            grid=(STEPS,),
            in_specs=[pl.BlockSpec((PIECE, PIECE), lambda j, s: (0, 0)), piece, piece, part, part, piece],
            out_specs=[
                pl.BlockSpec((HALF, FEATS), lambda j, s: (0, j)),
                pl.BlockSpec((1, 1, HALF, FEATS), lambda j, s: (j // 2, flip(j % 2, s[0]), 0, 0)),
            ],
        ),
        out_shape=[
            hbm((HALF, D), BF16),
            hbm((NZ, 2, HALF, FEATS), BF16),
        ],
        compiler_params=pltpu.CompilerParams(vmem_limit_bytes=32 * 2**20),
        name="split",
    )(where, selection((NY, 2, ROWS), (1, 0, 2)), *pieces)


def hbm(shape, dtype):
    return pltpu.MemorySpace.HBM(shape, dtype)


def pinned(*values):
    return [pltpu.with_memory_space_constraint(v, pltpu.MemorySpace.HBM) for v in values]


def flip(a, b):
    return a + b - 2 * a * b


def gates_body(where, tok, gw, uw, mw, ow, hid, fac, acc):
    step = pl.program_id(0)

    @pl.when(step == 0)
    def _():
        acc[...] = jnp.zeros_like(acc)

    t = tok[...]
    for i, w in enumerate((gw, uw, mw, ow)):
        acc[:, i * HID : (i + 1) * HID] += contract(t, w[...], 1, 0)

    @pl.when(step == STEPS - 1)
    def _():
        first = where[0] == 0
        pm, po = acc[:, 2 * HID : 3 * HID], acc[:, 3 * HID :]
        sides = (
            (acc[:, :HID], acc[:, HID : 2 * HID]),
            (jnp.where(first, pm, po), jnp.where(first, po, pm)),
        )
        for i, (gate, up) in enumerate(sides):
            sigma = jax.nn.sigmoid(gate)
            silu = gate * sigma
            hid[:, i * HID : (i + 1) * HID] = (silu * up).astype(BF16)
            slope = up * sigma * (1.0 + gate * (1.0 - sigma))
            if i == 1:
                slope, silu = jnp.where(first, slope, silu), jnp.where(first, silu, slope)
            fac[:, 2 * i * HID : (2 * i + 1) * HID] = slope
            fac[:, (2 * i + 1) * HID : (2 * i + 2) * HID] = silu


def gates(where, tok, gw, uw, mw, ow):
    weight = pl.BlockSpec((FEATS, HID), lambda j, s: (j, 0))
    return pl.pallas_call(
        gates_body,
        grid_spec=pltpu.PrefetchScalarGridSpec(
            num_scalar_prefetch=1,
            grid=(STEPS,),
            in_specs=[pl.BlockSpec((HALF, FEATS), lambda j, s: (0, j))] + [weight] * 4,
            out_specs=[
                pl.BlockSpec((HALF, 2 * HID), lambda j, s: (0, 0)),
                pl.BlockSpec((HALF, 4 * HID), lambda j, s: (0, 0)),
            ],
            scratch_shapes=[pltpu.VMEM((HALF, 4 * HID), F32)],
        ),
        out_shape=[
            jax.ShapeDtypeStruct((HALF, 2 * HID), BF16),
            jax.ShapeDtypeStruct((HALF, 4 * HID), F32),
        ],
        compiler_params=pltpu.CompilerParams(vmem_limit_bytes=32 * 2**20),
        name="gates",
    )(where, *pinned(tok, gw, uw, mw), ow)


def down_body(where, cot, dn, df, fac, dd, acc):
    step = pl.program_id(0)

    @pl.when(step == 0)
    def _():
        acc[...] = jnp.zeros_like(acc)

    acc[...] += contract(cot[0, 0], dn[0], 1, 1) + contract(cot[0, 1], df[0], 1, 1)

    @pl.when(step == NZ - 1)
    def _():
        low = where[1] == 0
        dl, dh = acc[:, :HID], acc[:, HID:]
        for i, d_hidden in enumerate((jnp.where(low, dl, dh), jnp.where(low, dh, dl))):
            for k in (2 * i, 2 * i + 1):
                dd[:, k * HID : (k + 1) * HID] = (d_hidden * fac[:, k * HID : (k + 1) * HID]).astype(BF16)


def down(where, cot, dn, df, fac):
    plane = pl.BlockSpec((1, 2 * HID, FEATS), lambda j, s: (j, 0, 0))
    block = pl.BlockSpec((HALF, 4 * HID), lambda j, s: (0, 0))
    return pl.pallas_call(
        down_body,
        grid_spec=pltpu.PrefetchScalarGridSpec(
            num_scalar_prefetch=1,
            grid=(NZ,),
            in_specs=[pl.BlockSpec((1, 2, HALF, FEATS), lambda j, s: (j, 0, 0, 0)), plane, plane, block],
            out_specs=block,
            scratch_shapes=[pltpu.VMEM((HALF, 2 * HID), F32)],
        ),
        out_shape=jax.ShapeDtypeStruct((HALF, 4 * HID), BF16),
        compiler_params=pltpu.CompilerParams(vmem_limit_bytes=32 * 2**20),
        name="down",
    )(where, *pinned(cot, dn), df, fac)


def term_body(where, pick, dd, *refs):
    weights, out = refs[:-1], refs[-1]
    halves = []
    for h in range(2):
        total = None
        for i, w in enumerate(weights[h::2]):
            part = contract(dd[:, i * HID : (i + 1) * HID], w[...], 1, 1)
            total = part if total is None else total + part
        halves.append(total.astype(BF16))
    rows = contract(pick[...], jnp.concatenate(halves, axis=0), 1, 0).astype(BF16)
    for i in range(NX):
        out[(where[2] + NX - i) % NX] = rows[i * PIECE : (i + 1) * PIECE]


def term(where, dd, gw, uw, mw, ow):
    low = pl.BlockSpec((FEATS, HID), lambda j, s: (j, 0))
    high = pl.BlockSpec((FEATS, HID), lambda j, s: (j + NZ, 0))
    gw, uw, mw = pinned(gw, uw, mw)
    return pl.pallas_call(
        term_body,
        grid_spec=pltpu.PrefetchScalarGridSpec(
            num_scalar_prefetch=1,
            grid=(STEPS // 2,),
            in_specs=[
                pl.BlockSpec((2 * HALF, 2 * HALF), lambda j, s: (0, 0)),
                pl.BlockSpec((HALF, 4 * HID), lambda j, s: (0, 0)),
            ]
            + [low, high] * 4,
            out_specs=pl.BlockSpec((NX, PIECE, FEATS), lambda j, s: (0, 0, j)),
        ),
        out_shape=hbm((NX, PIECE, D // 2), BF16),
        compiler_params=pltpu.CompilerParams(vmem_limit_bytes=32 * 2**20),
        name="term",
    )(where, merge(), dd, gw, gw, uw, uw, mw, mw, ow, ow)


def grads_body(where, h, cn, cf, keep, send):
    total, core = None, where[0]
    for z in range(NZ):
        part = contract(h[z, core], cn[z, 0], 0, 0) + contract(h[z, 1 - core], cf[z], 0, 0)
        total = part if total is None else total + part
    keep[...] = total[:HID]
    send[...] = total[HID:].astype(BF16)


def grads(where, hidden, cot_near, cot_far):
    vmem = pl.BlockSpec(memory_space=pltpu.MemorySpace.VMEM)
    return pl.pallas_call(
        grads_body,
        in_specs=[pl.BlockSpec(memory_space=pltpu.MemorySpace.SMEM)] + [vmem] * 3,
        out_specs=[vmem] * 2,
        out_shape=[
            jax.ShapeDtypeStruct((HID, FEATS), F32),
            jax.ShapeDtypeStruct((HID, FEATS), BF16),
        ],
        compiler_params=pltpu.CompilerParams(vmem_limit_bytes=32 * 2**20),
        name="grads",
    )(where, hidden, cot_near, cot_far)


def selection(shape, order):
    source = np.arange(np.prod(shape)).reshape(shape).transpose(order).reshape(-1)
    return jnp.asarray(np.eye(source.size, dtype=np.float32)[source], BF16)


def merge():
    return selection((2, NX, NY, ROWS), (1, 2, 0, 3))


def spread(block, axis):
    n = lax.axis_size(axis)
    return lax.all_to_all(jnp.broadcast_to(block[None], (n, *block.shape)), axis, 0, 0)


def on_device(tokens, cotangent, gate_weight, up_weight, down_weight):
    core = lax.axis_index("c")
    where = jnp.stack([core, lax.axis_index("zl"), lax.axis_index("x")]).astype(jnp.int32)

    picked = jnp.where(core == 0, gate_weight, up_weight)
    picked, tokens = lax.optimization_barrier((picked, tokens))
    mine = neighbours(picked)
    down_near = lax.all_gather(down_weight, ("zh", "zl"), axis=0).reshape(NZ, 2 * HID, FEATS)

    block = spread(jnp.concatenate([tokens, cotangent], axis=0), "y").reshape(PIECE, D)
    left, right = shift(block, "x", 1), shift(block, "x", -1)
    n = PIECE // 2
    pieces = (block, left, shift(left[:n], "x", 1), shift(right[n:], "x", -1), right)

    tok, cot = split(where, pieces)
    cot_near = lax.all_to_all(cot, "zh", 0, 0)
    tok, mine, down_near = lax.optimization_barrier((tok, mine, down_near))
    other, down_far = swap(mine, "c"), swap(down_near, "c")
    hidden, factors = gates(where, tok, gate_weight, up_weight, mine, other)
    hidden = lax.all_gather(hidden, DP, axis=0).reshape(NZ, 2, HALF, 2 * HID)
    dd = down(where, cot, down_near, down_far, factors)

    parts = term(where, dd, gate_weight, up_weight, mine, other)
    parts = lax.all_to_all(parts.reshape(NX * NY, 2 * ROWS, D // 2), ("x", "y"), 0, 0)
    hidden, cot_near = lax.optimization_barrier((hidden, cot_near))
    keep, send = grads(where, hidden, cot_near, swap(cot_near[:, 1], "c"))
    parts, received = lax.optimization_barrier((parts, swap(send, "zl")))
    total = jnp.sum(parts.astype(F32), axis=0).astype(BF16)
    input_grad = jnp.concatenate([total[:ROWS], total[ROWS:]], axis=1)
    down_grad = keep + received.astype(F32)
    return (input_grad, down_grad)


def solution(mesh):
    fine = Mesh(mesh.devices.reshape(NZ, 2, 2, NY, NX), ("zh", "c", "zl", "y", "x"))
    placed = (
        P((*DP, *TENSOR), None),
        P((*DP, *TENSOR), None),
        P(None, TENSOR),
        P(None, TENSOR),
        P(TENSOR, DP),
    )
    return jax.shard_map(
        on_device,
        mesh=fine,
        in_specs=placed,
        out_specs=(P((*DP, *TENSOR), None), P(TENSOR, DP)),
        check_vma=False,
    )
```

```python
import functools

import jax
import jax.numpy as jnp
import numpy as np
from jax import lax
from jax.experimental import pallas as pl
from jax.experimental.pallas import tpu as pltpu
from jax.sharding import Mesh, PartitionSpec as P

BF16 = jnp.bfloat16
F32 = jnp.float32
DP = ("zh", "c")
TENSOR = ("zl", "y", "x")
NZ, NY, NX = 4, 8, 4
ROWS = 4
HALF = NX * NY * ROWS
D = 4096
HID = 256
FEATS = 512
STEPS = D // FEATS
PIECE = 2 * NY * ROWS


def contract(a, b, ca, cb):
    return lax.dot_general(a, b, (((ca,), (cb,)), ((), ())), preferred_element_type=F32)


def swap(value, axis):
    return lax.ppermute(value, axis, [(0, 1), (1, 0)])


def shift(value, axis, k):
    n = lax.axis_size(axis)
    return lax.ppermute(value, axis, [(i, (i + k) % n) for i in range(n)])


def neighbours(value):
    at = lambda zh, c, zl: ((zh % NZ) * 2 + c) * 2 + zl
    pairs = []
    for zh in range(NZ):
        pairs += [(at(zh, 0, 0), at(zh, 0, 1)), (at(zh, 0, 1), at(zh, 0, 0))]
        pairs += [(at(zh, 1, 1), at(zh + 1, 1, 0)), (at(zh + 1, 1, 0), at(zh, 1, 1))]
    return lax.ppermute(value, ("zh", "c", "zl"), pairs)


def split_body(where, pick, r0, r1, r2a, r2b, r3, gw, uw, tok, cot, pre, acc):
    step = pl.program_id(0)

    @pl.when(step == 0)
    def _():
        acc[...] = jnp.zeros_like(acc)

    n = NY * ROWS
    r2 = jnp.concatenate([r2a[...], r2b[...]], axis=0)
    for i, piece in enumerate((r0[...], r1[...], r2, r3[...])):
        rows = contract(pick[...], piece, 1, 0).astype(BF16)
        tok[i * n : (i + 1) * n] = rows[:n]
        cot[0, 0, i * n : (i + 1) * n] = rows[n:]
    t = tok[...]
    acc[:, :HID] += contract(t, gw[...], 1, 0)
    acc[:, HID:] += contract(t, uw[...], 1, 0)

    @pl.when(step == STEPS - 1)
    def _():
        pre[...] = acc[...]


def split(where, pieces, gw, uw):
    weight = pl.BlockSpec((FEATS, HID), lambda j, s: (j, 0))
    piece = pl.BlockSpec((PIECE, FEATS), lambda j, s: (0, j))
    part = pl.BlockSpec((PIECE // 2, FEATS), lambda j, s: (0, j))
    return pl.pallas_call(
        split_body,
        grid_spec=pltpu.PrefetchScalarGridSpec(
            num_scalar_prefetch=1,
            grid=(STEPS,),
            in_specs=[pl.BlockSpec((PIECE, PIECE), lambda j, s: (0, 0)), piece, piece, part, part, piece]
            + [weight] * 2,
            out_specs=[
                pl.BlockSpec((HALF, FEATS), lambda j, s: (0, j)),
                pl.BlockSpec((1, 1, HALF, FEATS), lambda j, s: (j // 2, flip(j % 2, s[0]), 0, 0)),
                pl.BlockSpec((HALF, 2 * HID), lambda j, s: (0, 0)),
            ],
            scratch_shapes=[pltpu.VMEM((HALF, 2 * HID), F32)],
        ),
        out_shape=[
            hbm((HALF, D), BF16),
            hbm((NZ, 2, HALF, FEATS), BF16),
            hbm((HALF, 2 * HID), F32),
        ],
        compiler_params=pltpu.CompilerParams(vmem_limit_bytes=32 * 2**20),
        name="split",
    )(where, selection((NY, 2, ROWS), (1, 0, 2)), *pieces, *pinned(gw, uw))


def hbm(shape, dtype):
    return pltpu.MemorySpace.HBM(shape, dtype)


def pinned(*values):
    return [pltpu.with_memory_space_constraint(v, pltpu.MemorySpace.HBM) for v in values]


def flip(a, b):
    return a + b - 2 * a * b


def gates_body(where, tok, mw, ow, pre, hid, fac, acc):
    step = pl.program_id(0)

    @pl.when(step == 0)
    def _():
        acc[...] = jnp.zeros_like(acc)

    t = tok[...]
    for i, w in enumerate((mw, ow)):
        acc[:, i * HID : (i + 1) * HID] += contract(t, w[...], 1, 0)

    @pl.when(step == STEPS - 1)
    def _():
        first = where[0] == 0
        pm, po = acc[:, :HID], acc[:, HID:]
        sides = (
            (pre[:, :HID], pre[:, HID:]),
            (jnp.where(first, pm, po), jnp.where(first, po, pm)),
        )
        for i, (gate, up) in enumerate(sides):
            sigma = jax.nn.sigmoid(gate)
            silu = gate * sigma
            hid[:, i * HID : (i + 1) * HID] = (silu * up).astype(BF16)
            slope = up * sigma * (1.0 + gate * (1.0 - sigma))
            if i == 1:
                slope, silu = jnp.where(first, slope, silu), jnp.where(first, silu, slope)
            fac[:, 2 * i * HID : (2 * i + 1) * HID] = slope
            fac[:, (2 * i + 1) * HID : (2 * i + 2) * HID] = silu


def gates(where, tok, mw, ow, pre):
    weight = pl.BlockSpec((FEATS, HID), lambda j, s: (j, 0))
    return pl.pallas_call(
        gates_body,
        grid_spec=pltpu.PrefetchScalarGridSpec(
            num_scalar_prefetch=1,
            grid=(STEPS,),
            in_specs=[pl.BlockSpec((HALF, FEATS), lambda j, s: (0, j))] + [weight] * 2
            + [pl.BlockSpec((HALF, 2 * HID), lambda j, s: (0, 0))],
            out_specs=[
                pl.BlockSpec((HALF, 2 * HID), lambda j, s: (0, 0)),
                pl.BlockSpec((HALF, 4 * HID), lambda j, s: (0, 0)),
            ],
            scratch_shapes=[pltpu.VMEM((HALF, 2 * HID), F32)],
        ),
        out_shape=[
            jax.ShapeDtypeStruct((HALF, 2 * HID), BF16),
            hbm((HALF, 4 * HID), F32),
        ],
        compiler_params=pltpu.CompilerParams(vmem_limit_bytes=32 * 2**20),
        name="gates",
    )(where, *pinned(tok, mw), ow, *pinned(pre))


def down_body(where, cot, dn, df, fac, dd, acc):
    step = pl.program_id(0)

    @pl.when(step == 0)
    def _():
        acc[...] = jnp.zeros_like(acc)

    acc[...] += contract(cot[0, 0], dn[0], 1, 1) + contract(cot[0, 1], df[0], 1, 1)

    @pl.when(step == NZ - 1)
    def _():
        low = where[1] == 0
        dl, dh = acc[:, :HID], acc[:, HID:]
        for i, d_hidden in enumerate((jnp.where(low, dl, dh), jnp.where(low, dh, dl))):
            for k in (2 * i, 2 * i + 1):
                dd[:, k * HID : (k + 1) * HID] = (d_hidden * fac[:, k * HID : (k + 1) * HID]).astype(BF16)


def down(where, cot, dn, df, fac):
    plane = pl.BlockSpec((1, 2 * HID, FEATS), lambda j, s: (j, 0, 0))
    block = pl.BlockSpec((HALF, 4 * HID), lambda j, s: (0, 0))
    return pl.pallas_call(
        down_body,
        grid_spec=pltpu.PrefetchScalarGridSpec(
            num_scalar_prefetch=1,
            grid=(NZ,),
            in_specs=[pl.BlockSpec((1, 2, HALF, FEATS), lambda j, s: (j, 0, 0, 0)), plane, plane, block],
            out_specs=block,
            scratch_shapes=[pltpu.VMEM((HALF, 2 * HID), F32)],
        ),
        out_shape=jax.ShapeDtypeStruct((HALF, 4 * HID), BF16),
        compiler_params=pltpu.CompilerParams(vmem_limit_bytes=32 * 2**20),
        name="down",
    )(where, *pinned(cot, dn), df, *pinned(fac))


def term_body(where, pick, dd, *refs):
    weights, out = refs[:-1], refs[-1]
    halves = []
    for h in range(2):
        total = None
        for i, w in enumerate(weights[h::2]):
            part = contract(dd[:, i * HID : (i + 1) * HID], w[...], 1, 1)
            total = part if total is None else total + part
        halves.append(total.astype(BF16))
    rows = contract(pick[...], jnp.concatenate(halves, axis=0), 1, 0).astype(BF16)
    for i in range(NX):
        out[(where[2] + NX - i) % NX] = rows[i * PIECE : (i + 1) * PIECE]


def term(where, dd, gw, uw, mw, ow):
    low = pl.BlockSpec((2 * FEATS, HID), lambda j, s: (j, 0))
    high = pl.BlockSpec((2 * FEATS, HID), lambda j, s: (j + 2, 0))
    gw, uw, mw = pinned(gw, uw, mw)
    return pl.pallas_call(
        term_body,
        grid_spec=pltpu.PrefetchScalarGridSpec(
            num_scalar_prefetch=1,
            grid=(STEPS // 4,),
            in_specs=[
                pl.BlockSpec((2 * HALF, 2 * HALF), lambda j, s: (0, 0)),
                pl.BlockSpec((HALF, 4 * HID), lambda j, s: (0, 0)),
            ]
            + [low, high] * 4,
            out_specs=pl.BlockSpec((NX, PIECE, 2 * FEATS), lambda j, s: (0, 0, j)),
        ),
        out_shape=hbm((NX, PIECE, D // 2), BF16),
        compiler_params=pltpu.CompilerParams(vmem_limit_bytes=32 * 2**20),
        name="term",
    )(where, merge(), dd, gw, gw, uw, uw, mw, mw, ow, ow)


def grads_body(where, h, cn, cf, keep, send):
    total, core = None, where[0]
    for z in range(NZ):
        part = contract(h[z, core], cn[z, 0], 0, 0) + contract(h[z, 1 - core], cf[z], 0, 0)
        total = part if total is None else total + part
    keep[...] = total[:HID]
    send[...] = total[HID:].astype(BF16)


def grads(where, hidden, cot_near, cot_far):
    vmem = pl.BlockSpec(memory_space=pltpu.MemorySpace.VMEM)
    return pl.pallas_call(
        grads_body,
        in_specs=[pl.BlockSpec(memory_space=pltpu.MemorySpace.SMEM)] + [vmem] * 3,
        out_specs=[vmem] * 2,
        out_shape=[
            jax.ShapeDtypeStruct((HID, FEATS), F32),
            jax.ShapeDtypeStruct((HID, FEATS), BF16),
        ],
        compiler_params=pltpu.CompilerParams(vmem_limit_bytes=32 * 2**20),
        name="grads",
    )(where, hidden, cot_near, cot_far)


def selection(shape, order):
    source = np.arange(np.prod(shape)).reshape(shape).transpose(order).reshape(-1)
    return jnp.asarray(np.eye(source.size, dtype=np.float32)[source], BF16)


def merge():
    return selection((2, NX, NY, ROWS), (1, 2, 0, 3))


def spread(block, axis):
    n = lax.axis_size(axis)
    return lax.all_to_all(jnp.broadcast_to(block[None], (n, *block.shape)), axis, 0, 0)


def on_device(tokens, cotangent, gate_weight, up_weight, down_weight):
    core = lax.axis_index("c")
    where = jnp.stack([core, lax.axis_index("zl"), lax.axis_index("x")]).astype(jnp.int32)

    picked = jnp.where(core == 0, gate_weight, up_weight)
    picked, tokens = lax.optimization_barrier((picked, tokens))
    mine = neighbours(picked)
    down_near = lax.all_gather(down_weight, ("zh", "zl"), axis=0).reshape(NZ, 2 * HID, FEATS)

    block = spread(jnp.concatenate([tokens, cotangent], axis=0), "y").reshape(PIECE, D)
    left, right = shift(block, "x", 1), shift(block, "x", -1)
    n = PIECE // 2
    pieces = (block, left, shift(left[:n], "x", 1), shift(right[n:], "x", -1), right)

    tok, cot, pre = split(where, pieces, gate_weight, up_weight)
    cot_near = lax.all_to_all(cot, "zh", 0, 0)
    tok, mine, down_near = lax.optimization_barrier((tok, mine, down_near))
    other, down_far = swap(mine, "c"), swap(down_near, "c")
    hidden, factors = gates(where, tok, mine, other, pre)
    hidden = lax.all_gather(hidden, DP, axis=0).reshape(NZ, 2, HALF, 2 * HID)
    dd = down(where, cot, down_near, down_far, factors)

    parts = term(where, dd, gate_weight, up_weight, mine, other)
    parts = lax.all_to_all(parts.reshape(NX * NY, 2 * ROWS, D // 2), ("x", "y"), 0, 0)
    hidden, cot_near = lax.optimization_barrier((hidden, cot_near))
    keep, send = grads(where, hidden, cot_near, swap(cot_near[:, 1], "c"))
    parts, received = lax.optimization_barrier((parts, swap(send, "zl")))
    total = jnp.sum(parts.astype(F32), axis=0).astype(BF16)
    input_grad = jnp.concatenate([total[:ROWS], total[ROWS:]], axis=1)
    down_grad = keep + received.astype(F32)
    return (input_grad, down_grad)


def solution(mesh):
    fine = Mesh(mesh.devices.reshape(NZ, 2, 2, NY, NX), ("zh", "c", "zl", "y", "x"))
    placed = (
        P((*DP, *TENSOR), None),
        P((*DP, *TENSOR), None),
        P(None, TENSOR),
        P(None, TENSOR),
        P(TENSOR, DP),
    )
    return jax.shard_map(
        on_device,
        mesh=fine,
        in_specs=placed,
        out_specs=(P((*DP, *TENSOR), None), P(TENSOR, DP)),
        check_vma=False,
    )
```

```python
import functools

import jax
import jax.numpy as jnp
import numpy as np
from jax import lax
from jax.experimental import pallas as pl
from jax.experimental.pallas import tpu as pltpu
from jax.sharding import Mesh, PartitionSpec as P

BF16 = jnp.bfloat16
F32 = jnp.float32
DP = ("zh", "c")
TENSOR = ("zl", "y", "x")
NZ, NY, NX = 4, 8, 4
ROWS = 4
HALF = NX * NY * ROWS
D = 4096
HID = 256
FEATS = 512
STEPS = D // FEATS
PIECE = 2 * NY * ROWS


def contract(a, b, ca, cb):
    return lax.dot_general(a, b, (((ca,), (cb,)), ((), ())), preferred_element_type=F32)


def swap(value, axis):
    return lax.ppermute(value, axis, [(0, 1), (1, 0)])


def shift(value, axis, k):
    n = lax.axis_size(axis)
    return lax.ppermute(value, axis, [(i, (i + k) % n) for i in range(n)])


def neighbours(value):
    at = lambda zh, c, zl: ((zh % NZ) * 2 + c) * 2 + zl
    pairs = []
    for zh in range(NZ):
        pairs += [(at(zh, 0, 0), at(zh, 0, 1)), (at(zh, 0, 1), at(zh, 0, 0))]
        pairs += [(at(zh, 1, 1), at(zh + 1, 1, 0)), (at(zh + 1, 1, 0), at(zh, 1, 1))]
    return lax.ppermute(value, ("zh", "c", "zl"), pairs)


def split_body(where, pick, r0, r1, r2a, r2b, r3, tok, cot):
    n = NY * ROWS
    r2 = jnp.concatenate([r2a[...], r2b[...]], axis=0)
    for i, piece in enumerate((r0[...], r1[...], r2, r3[...])):
        rows = contract(pick[...], piece, 1, 0).astype(BF16)
        tok[i * n : (i + 1) * n] = rows[:n]
        cot[0, 0, i * n : (i + 1) * n] = rows[n:]


def split(where, pieces):
    piece = pl.BlockSpec((PIECE, FEATS), lambda j, s: (0, j))
    part = pl.BlockSpec((PIECE // 2, FEATS), lambda j, s: (0, j))
    return pl.pallas_call(
        split_body,
        grid_spec=pltpu.PrefetchScalarGridSpec(
            num_scalar_prefetch=1,
            grid=(STEPS,),
            in_specs=[pl.BlockSpec((PIECE, PIECE), lambda j, s: (0, 0)), piece, piece, part, part, piece],
            out_specs=[
                pl.BlockSpec((HALF, FEATS), lambda j, s: (0, j)),
                pl.BlockSpec((1, 1, HALF, FEATS), lambda j, s: (j // 2, flip(j % 2, s[0]), 0, 0)),
            ],
        ),
        out_shape=[
            hbm((HALF, D), BF16),
            hbm((NZ, 2, HALF, FEATS), BF16),
        ],
        compiler_params=pltpu.CompilerParams(vmem_limit_bytes=32 * 2**20),
        name="split",
    )(where, selection((NY, 2, ROWS), (1, 0, 2)), *pieces)


def hbm(shape, dtype):
    return pltpu.MemorySpace.HBM(shape, dtype)


def pinned(*values):
    return [pltpu.with_memory_space_constraint(v, pltpu.MemorySpace.HBM) for v in values]


def flip(a, b):
    return a + b - 2 * a * b


def gates_body(where, tok, gw, uw, mw, ow, hid, fac, acc):
    step = pl.program_id(0)

    @pl.when(step == 0)
    def _():
        acc[...] = jnp.zeros_like(acc)

    t = tok[...]
    for i, w in enumerate((gw, uw, mw, ow)):
        acc[:, i * HID : (i + 1) * HID] += contract(t, w[...], 1, 0)

    @pl.when(step == STEPS // 2 - 1)
    def _():
        first = where[0] == 0
        pm, po = acc[:, 2 * HID : 3 * HID], acc[:, 3 * HID :]
        sides = (
            (acc[:, :HID], acc[:, HID : 2 * HID]),
            (jnp.where(first, pm, po), jnp.where(first, po, pm)),
        )
        for i, (gate, up) in enumerate(sides):
            sigma = jax.nn.sigmoid(gate)
            silu = gate * sigma
            hid[:, i * HID : (i + 1) * HID] = (silu * up).astype(BF16)
            slope = up * sigma * (1.0 + gate * (1.0 - sigma))
            if i == 1:
                slope, silu = jnp.where(first, slope, silu), jnp.where(first, silu, slope)
            fac[:, 2 * i * HID : (2 * i + 1) * HID] = slope
            fac[:, (2 * i + 1) * HID : (2 * i + 2) * HID] = silu


def gates(where, tok, gw, uw, mw, ow):
    weight = pl.BlockSpec((2 * FEATS, HID), lambda j, s: (j, 0))
    return pl.pallas_call(
        gates_body,
        grid_spec=pltpu.PrefetchScalarGridSpec(
            num_scalar_prefetch=1,
            grid=(STEPS // 2,),
            in_specs=[pl.BlockSpec((HALF, 2 * FEATS), lambda j, s: (0, j))] + [weight] * 4,
            out_specs=[
                pl.BlockSpec((HALF, 2 * HID), lambda j, s: (0, 0)),
                pl.BlockSpec((HALF, 4 * HID), lambda j, s: (0, 0)),
            ],
            scratch_shapes=[pltpu.VMEM((HALF, 4 * HID), F32)],
        ),
        out_shape=[
            jax.ShapeDtypeStruct((HALF, 2 * HID), BF16),
            hbm((HALF, 4 * HID), F32),
        ],
        compiler_params=pltpu.CompilerParams(vmem_limit_bytes=32 * 2**20),
        name="gates",
    )(where, *pinned(tok, gw, uw, mw), ow)


def down_body(where, cot, dn, df, fac, dd, acc):
    step = pl.program_id(0)

    @pl.when(step == 0)
    def _():
        acc[...] = jnp.zeros_like(acc)

    for z in range(2):
        acc[...] += contract(cot[z, 0], dn[z], 1, 1) + contract(cot[z, 1], df[z], 1, 1)

    @pl.when(step == NZ // 2 - 1)
    def _():
        low = where[1] == 0
        dl, dh = acc[:, :HID], acc[:, HID:]
        for i, d_hidden in enumerate((jnp.where(low, dl, dh), jnp.where(low, dh, dl))):
            for k in (2 * i, 2 * i + 1):
                dd[:, k * HID : (k + 1) * HID] = (d_hidden * fac[:, k * HID : (k + 1) * HID]).astype(BF16)


def down(where, cot, dn, df, fac):
    plane = pl.BlockSpec((2, 2 * HID, FEATS), lambda j, s: (j, 0, 0))
    block = pl.BlockSpec((HALF, 4 * HID), lambda j, s: (0, 0))
    return pl.pallas_call(
        down_body,
        grid_spec=pltpu.PrefetchScalarGridSpec(
            num_scalar_prefetch=1,
            grid=(NZ // 2,),
            in_specs=[pl.BlockSpec((2, 2, HALF, FEATS), lambda j, s: (j, 0, 0, 0)), plane, plane, block],
            out_specs=block,
            scratch_shapes=[pltpu.VMEM((HALF, 2 * HID), F32)],
        ),
        out_shape=jax.ShapeDtypeStruct((HALF, 4 * HID), BF16),
        compiler_params=pltpu.CompilerParams(vmem_limit_bytes=32 * 2**20),
        name="down",
    )(where, *pinned(cot, dn), df, *pinned(fac))


def term_body(where, pick, dd, *refs):
    weights, out = refs[:-1], refs[-1]
    halves = []
    for h in range(2):
        total = None
        for i, w in enumerate(weights[h::2]):
            part = contract(dd[:, i * HID : (i + 1) * HID], w[...], 1, 1)
            total = part if total is None else total + part
        halves.append(total.astype(BF16))
    rows = contract(pick[...], jnp.concatenate(halves, axis=0), 1, 0).astype(BF16)
    for i in range(NX):
        out[(where[2] + NX - i) % NX] = rows[i * PIECE : (i + 1) * PIECE]


def term(where, dd, gw, uw, mw, ow):
    low = pl.BlockSpec((2 * FEATS, HID), lambda j, s: (j, 0))
    high = pl.BlockSpec((2 * FEATS, HID), lambda j, s: (j + 2, 0))
    gw, uw, mw = pinned(gw, uw, mw)
    return pl.pallas_call(
        term_body,
        grid_spec=pltpu.PrefetchScalarGridSpec(
            num_scalar_prefetch=1,
            grid=(STEPS // 4,),
            in_specs=[
                pl.BlockSpec((2 * HALF, 2 * HALF), lambda j, s: (0, 0)),
                pl.BlockSpec((HALF, 4 * HID), lambda j, s: (0, 0)),
            ]
            + [low, high] * 4,
            out_specs=pl.BlockSpec((NX, PIECE, 2 * FEATS), lambda j, s: (0, 0, j)),
        ),
        out_shape=hbm((NX, PIECE, D // 2), BF16),
        compiler_params=pltpu.CompilerParams(vmem_limit_bytes=32 * 2**20),
        name="term",
    )(where, merge(), dd, gw, gw, uw, uw, mw, mw, ow, ow)


def grads_body(where, h, cn, cf, keep, send):
    total, core = None, where[0]
    for z in range(NZ):
        part = contract(h[z, core], cn[z, 0], 0, 0) + contract(h[z, 1 - core], cf[z], 0, 0)
        total = part if total is None else total + part
    keep[...] = total[:HID]
    send[...] = total[HID:].astype(BF16)


def grads(where, hidden, cot_near, cot_far):
    vmem = pl.BlockSpec(memory_space=pltpu.MemorySpace.VMEM)
    return pl.pallas_call(
        grads_body,
        in_specs=[pl.BlockSpec(memory_space=pltpu.MemorySpace.SMEM)] + [vmem] * 3,
        out_specs=[vmem] * 2,
        out_shape=[
            jax.ShapeDtypeStruct((HID, FEATS), F32),
            jax.ShapeDtypeStruct((HID, FEATS), BF16),
        ],
        compiler_params=pltpu.CompilerParams(vmem_limit_bytes=32 * 2**20),
        name="grads",
    )(where, hidden, cot_near, cot_far)


def selection(shape, order):
    source = np.arange(np.prod(shape)).reshape(shape).transpose(order).reshape(-1)
    return jnp.asarray(np.eye(source.size, dtype=np.float32)[source], BF16)


def merge():
    return selection((2, NX, NY, ROWS), (1, 2, 0, 3))


def spread(block, axis):
    n = lax.axis_size(axis)
    return lax.all_to_all(jnp.broadcast_to(block[None], (n, *block.shape)), axis, 0, 0)


def on_device(tokens, cotangent, gate_weight, up_weight, down_weight):
    core = lax.axis_index("c")
    where = jnp.stack([core, lax.axis_index("zl"), lax.axis_index("x")]).astype(jnp.int32)

    picked = jnp.where(core == 0, gate_weight, up_weight)
    picked, tokens = lax.optimization_barrier((picked, tokens))
    mine = neighbours(picked)
    down_near = lax.all_gather(down_weight, ("zh", "zl"), axis=0).reshape(NZ, 2 * HID, FEATS)

    block = spread(jnp.concatenate([tokens, cotangent], axis=0), "y").reshape(PIECE, D)
    left, right = shift(block, "x", 1), shift(block, "x", -1)
    n = PIECE // 2
    pieces = (block, left, shift(left[:n], "x", 1), shift(right[n:], "x", -1), right)

    tok, cot = split(where, pieces)
    cot_near = lax.all_to_all(cot, "zh", 0, 0)
    tok, mine, down_near = lax.optimization_barrier((tok, mine, down_near))
    other, down_far = swap(mine, "c"), swap(down_near, "c")
    hidden, factors = gates(where, tok, gate_weight, up_weight, mine, other)
    hidden = lax.all_gather(hidden, DP, axis=0).reshape(NZ, 2, HALF, 2 * HID)
    dd = down(where, cot, down_near, down_far, factors)

    parts = term(where, dd, gate_weight, up_weight, mine, other)
    parts = lax.all_to_all(parts.reshape(NX * NY, 2 * ROWS, D // 2), ("x", "y"), 0, 0)
    hidden, cot_near = lax.optimization_barrier((hidden, cot_near))
    keep, send = grads(where, hidden, cot_near, swap(cot_near[:, 1], "c"))
    parts, received = lax.optimization_barrier((parts, swap(send, "zl")))
    total = jnp.sum(parts.astype(F32), axis=0).astype(BF16)
    input_grad = jnp.concatenate([total[:ROWS], total[ROWS:]], axis=1)
    down_grad = keep + received.astype(F32)
    return (input_grad, down_grad)


def solution(mesh):
    fine = Mesh(mesh.devices.reshape(NZ, 2, 2, NY, NX), ("zh", "c", "zl", "y", "x"))
    placed = (
        P((*DP, *TENSOR), None),
        P((*DP, *TENSOR), None),
        P(None, TENSOR),
        P(None, TENSOR),
        P(TENSOR, DP),
    )
    return jax.shard_map(
        on_device,
        mesh=fine,
        in_specs=placed,
        out_specs=(P((*DP, *TENSOR), None), P(TENSOR, DP)),
        check_vma=False,
    )
```

```python
import functools

import jax
import jax.numpy as jnp
import numpy as np
from jax import lax
from jax.experimental import pallas as pl
from jax.experimental.pallas import tpu as pltpu
from jax.sharding import Mesh, PartitionSpec as P

BF16 = jnp.bfloat16
F32 = jnp.float32
DP = ("zh", "c")
TENSOR = ("zl", "y", "x")
NZ, NY, NX = 4, 8, 4
ROWS = 4
HALF = NX * NY * ROWS
D = 4096
HID = 256
FEATS = 512
STEPS = D // FEATS
PIECE = 2 * NY * ROWS


def contract(a, b, ca, cb):
    return lax.dot_general(a, b, (((ca,), (cb,)), ((), ())), preferred_element_type=F32)


def swap(value, axis):
    return lax.ppermute(value, axis, [(0, 1), (1, 0)])


def shift(value, axis, k):
    n = lax.axis_size(axis)
    return lax.ppermute(value, axis, [(i, (i + k) % n) for i in range(n)])


def neighbours(value):
    at = lambda zh, c, zl: ((zh % NZ) * 2 + c) * 2 + zl
    pairs = []
    for zh in range(NZ):
        pairs += [(at(zh, 0, 0), at(zh, 0, 1)), (at(zh, 0, 1), at(zh, 0, 0))]
        pairs += [(at(zh, 1, 1), at(zh + 1, 1, 0)), (at(zh + 1, 1, 0), at(zh, 1, 1))]
    return lax.ppermute(value, ("zh", "c", "zl"), pairs)


def split_body(where, pick, r0, r1, r2a, r2b, r3, tok, cot):
    n = NY * ROWS
    r2 = jnp.concatenate([r2a[...], r2b[...]], axis=0)
    for i, piece in enumerate((r0[...], r1[...], r2, r3[...])):
        rows = contract(pick[...], piece, 1, 0).astype(BF16)
        tok[i * n : (i + 1) * n] = rows[:n]
        cot[0, 0, i * n : (i + 1) * n] = rows[n:]


def split(where, pieces):
    piece = pl.BlockSpec((PIECE, FEATS), lambda j, s: (0, j))
    part = pl.BlockSpec((PIECE // 2, FEATS), lambda j, s: (0, j))
    return pl.pallas_call(
        split_body,
        grid_spec=pltpu.PrefetchScalarGridSpec(
            num_scalar_prefetch=1,
            grid=(STEPS,),
            in_specs=[pl.BlockSpec((PIECE, PIECE), lambda j, s: (0, 0)), piece, piece, part, part, piece],
            out_specs=[
                pl.BlockSpec((HALF, FEATS), lambda j, s: (0, j)),
                pl.BlockSpec((1, 1, HALF, FEATS), lambda j, s: (j // 2, flip(j % 2, s[0]), 0, 0)),
            ],
        ),
        out_shape=[
            hbm((HALF, D), BF16),
            hbm((NZ, 2, HALF, FEATS), BF16),
        ],
        compiler_params=pltpu.CompilerParams(vmem_limit_bytes=32 * 2**20),
        name="split",
    )(where, selection((NY, 2, ROWS), (1, 0, 2)), *pieces)


def hbm(shape, dtype):
    return pltpu.MemorySpace.HBM(shape, dtype)


def pinned(*values):
    return [pltpu.with_memory_space_constraint(v, pltpu.MemorySpace.HBM) for v in values]


def flip(a, b):
    return a + b - 2 * a * b


def gates_body(where, tok, gw, uw, mw, ow, hid, fac, acc):
    step = pl.program_id(0)

    @pl.when(step == 0)
    def _():
        acc[...] = jnp.zeros_like(acc)

    t = tok[...]
    for i, w in enumerate((gw, uw, mw, ow)):
        acc[:, i * HID : (i + 1) * HID] += contract(t, w[...], 1, 0)

    @pl.when(step == STEPS // 2 - 1)
    def _():
        first = where[0] == 0
        pm, po = acc[:, 2 * HID : 3 * HID], acc[:, 3 * HID :]
        sides = (
            (acc[:, :HID], acc[:, HID : 2 * HID]),
            (jnp.where(first, pm, po), jnp.where(first, po, pm)),
        )
        for i, (gate, up) in enumerate(sides):
            sigma = jax.nn.sigmoid(gate)
            silu = gate * sigma
            hid[:, i * HID : (i + 1) * HID] = (silu * up).astype(BF16)
            slope = up * sigma * (1.0 + gate * (1.0 - sigma))
            if i == 1:
                slope, silu = jnp.where(first, slope, silu), jnp.where(first, silu, slope)
            fac[:, 2 * i * HID : (2 * i + 1) * HID] = slope
            fac[:, (2 * i + 1) * HID : (2 * i + 2) * HID] = silu


def gates(where, tok, gw, uw, mw, ow):
    weight = pl.BlockSpec((2 * FEATS, HID), lambda j, s: (j, 0))
    return pl.pallas_call(
        gates_body,
        grid_spec=pltpu.PrefetchScalarGridSpec(
            num_scalar_prefetch=1,
            grid=(STEPS // 2,),
            in_specs=[pl.BlockSpec((HALF, 2 * FEATS), lambda j, s: (0, j))] + [weight] * 4,
            out_specs=[
                pl.BlockSpec((HALF, 2 * HID), lambda j, s: (0, 0)),
                pl.BlockSpec((HALF, 4 * HID), lambda j, s: (0, 0)),
            ],
            scratch_shapes=[pltpu.VMEM((HALF, 4 * HID), F32)],
        ),
        out_shape=[
            jax.ShapeDtypeStruct((HALF, 2 * HID), BF16),
            hbm((HALF, 4 * HID), F32),
        ],
        compiler_params=pltpu.CompilerParams(vmem_limit_bytes=32 * 2**20),
        name="gates",
    )(where, *pinned(tok, gw, uw, mw), ow)


def down_body(where, cot, dn, df, fac, dd, acc):
    step = pl.program_id(0)

    @pl.when(step == 0)
    def _():
        acc[...] = jnp.zeros_like(acc)

    for z in range(2):
        acc[...] += contract(cot[z, 0], dn[z], 1, 1) + contract(cot[z, 1], df[z], 1, 1)

    @pl.when(step == NZ // 2 - 1)
    def _():
        low = where[1] == 0
        dl, dh = acc[:, :HID], acc[:, HID:]
        for i, d_hidden in enumerate((jnp.where(low, dl, dh), jnp.where(low, dh, dl))):
            for k in (2 * i, 2 * i + 1):
                dd[:, k * HID : (k + 1) * HID] = (d_hidden * fac[:, k * HID : (k + 1) * HID]).astype(BF16)


def down(where, cot, dn, df, fac):
    plane = pl.BlockSpec((2, 2 * HID, FEATS), lambda j, s: (j, 0, 0))
    block = pl.BlockSpec((HALF, 4 * HID), lambda j, s: (0, 0))
    return pl.pallas_call(
        down_body,
        grid_spec=pltpu.PrefetchScalarGridSpec(
            num_scalar_prefetch=1,
            grid=(NZ // 2,),
            in_specs=[pl.BlockSpec((2, 2, HALF, FEATS), lambda j, s: (j, 0, 0, 0)), plane, plane, block],
            out_specs=block,
            scratch_shapes=[pltpu.VMEM((HALF, 2 * HID), F32)],
        ),
        out_shape=jax.ShapeDtypeStruct((HALF, 4 * HID), BF16),
        compiler_params=pltpu.CompilerParams(vmem_limit_bytes=32 * 2**20),
        name="down",
    )(where, *pinned(cot, dn), df, *pinned(fac))


def term_body(where, pick, dd, *refs):
    weights, out = refs[:-1], refs[-1]
    halves = []
    for h in range(2):
        total = None
        for i, w in enumerate(weights[h::2]):
            part = contract(dd[:, i * HID : (i + 1) * HID], w[...], 1, 1)
            total = part if total is None else total + part
        halves.append(total.astype(BF16))
    rows = contract(pick[...], jnp.concatenate(halves, axis=0), 1, 0).astype(BF16)
    for i in range(NX):
        out[(where[2] + NX - i) % NX] = rows[i * PIECE : (i + 1) * PIECE]


def term(where, dd, gw, uw, mw, ow):
    low = pl.BlockSpec((2 * FEATS, HID), lambda j, s: (j, 0))
    high = pl.BlockSpec((2 * FEATS, HID), lambda j, s: (j + 2, 0))
    gw, uw, mw = pinned(gw, uw, mw)
    return pl.pallas_call(
        term_body,
        grid_spec=pltpu.PrefetchScalarGridSpec(
            num_scalar_prefetch=1,
            grid=(STEPS // 4,),
            in_specs=[
                pl.BlockSpec((2 * HALF, 2 * HALF), lambda j, s: (0, 0)),
                pl.BlockSpec((HALF, 4 * HID), lambda j, s: (0, 0)),
            ]
            + [low, high] * 4,
            out_specs=pl.BlockSpec((NX, PIECE, 2 * FEATS), lambda j, s: (0, 0, j)),
        ),
        out_shape=hbm((NX, PIECE, D // 2), BF16),
        compiler_params=pltpu.CompilerParams(vmem_limit_bytes=32 * 2**20),
        name="term",
    )(where, merge(), dd, gw, gw, uw, uw, mw, mw, ow, ow)


def grads_body(where, h, cn, cf, keep, send):
    total, core = None, where[0]
    for z in range(NZ):
        part = contract(h[z, core], cn[z, 0], 0, 0) + contract(h[z, 1 - core], cf[z], 0, 0)
        total = part if total is None else total + part
    keep[...] = total[:HID]
    send[...] = total[HID:].astype(BF16)


def grads(where, hidden, cot_near, cot_far):
    vmem = pl.BlockSpec(memory_space=pltpu.MemorySpace.VMEM)
    return pl.pallas_call(
        grads_body,
        in_specs=[pl.BlockSpec(memory_space=pltpu.MemorySpace.SMEM)] + [vmem] * 3,
        out_specs=[vmem] * 2,
        out_shape=[
            jax.ShapeDtypeStruct((HID, FEATS), F32),
            jax.ShapeDtypeStruct((HID, FEATS), BF16),
        ],
        compiler_params=pltpu.CompilerParams(vmem_limit_bytes=32 * 2**20),
        name="grads",
    )(where, hidden, cot_near, cot_far)


def selection(shape, order):
    source = np.arange(np.prod(shape)).reshape(shape).transpose(order).reshape(-1)
    return jnp.asarray(np.eye(source.size, dtype=np.float32)[source], BF16)


def merge():
    return selection((2, NX, NY, ROWS), (1, 2, 0, 3))


def spread(block, axis):
    n = lax.axis_size(axis)
    return lax.all_to_all(jnp.broadcast_to(block[None], (n, *block.shape)), axis, 0, 0)


def on_device(tokens, cotangent, gate_weight, up_weight, down_weight):
    core = lax.axis_index("c")
    where = jnp.stack([core, lax.axis_index("zl"), lax.axis_index("x")]).astype(jnp.int32)

    block = jnp.concatenate([tokens, cotangent], axis=0)
    block = jnp.broadcast_to(block[None], (NY, 2 * ROWS, D))
    block, core = lax.optimization_barrier((block, core))
    picked = jnp.where(core == 0, gate_weight, up_weight)
    down_near = lax.all_gather(down_weight, ("zh", "zl"), axis=0).reshape(NZ, 2 * HID, FEATS)

    block = lax.all_to_all(block, "y", 0, 0).reshape(PIECE, D)
    block, picked = lax.optimization_barrier((block, picked))
    mine = neighbours(picked)
    left, right = shift(block, "x", 1), shift(block, "x", -1)
    n = PIECE // 2
    pieces = (block, left, shift(left[:n], "x", 1), shift(right[n:], "x", -1), right)

    tok, cot = split(where, pieces)
    cot_near = lax.all_to_all(cot, "zh", 0, 0)
    tok, mine, down_near = lax.optimization_barrier((tok, mine, down_near))
    other, down_far = swap(mine, "c"), swap(down_near, "c")
    hidden, factors = gates(where, tok, gate_weight, up_weight, mine, other)
    hidden = lax.all_gather(hidden, DP, axis=0).reshape(NZ, 2, HALF, 2 * HID)
    dd = down(where, cot, down_near, down_far, factors)

    parts = term(where, dd, gate_weight, up_weight, mine, other)
    parts = lax.all_to_all(parts.reshape(NX * NY, 2 * ROWS, D // 2), ("x", "y"), 0, 0)
    hidden, cot_near = lax.optimization_barrier((hidden, cot_near))
    keep, send = grads(where, hidden, cot_near, swap(cot_near[:, 1], "c"))
    parts, received = lax.optimization_barrier((parts, swap(send, "zl")))
    total = jnp.sum(parts.astype(F32), axis=0).astype(BF16)
    input_grad = jnp.concatenate([total[:ROWS], total[ROWS:]], axis=1)
    down_grad = keep + received.astype(F32)
    return (input_grad, down_grad)


def solution(mesh):
    fine = Mesh(mesh.devices.reshape(NZ, 2, 2, NY, NX), ("zh", "c", "zl", "y", "x"))
    placed = (
        P((*DP, *TENSOR), None),
        P((*DP, *TENSOR), None),
        P(None, TENSOR),
        P(None, TENSOR),
        P(TENSOR, DP),
    )
    return jax.shard_map(
        on_device,
        mesh=fine,
        in_specs=placed,
        out_specs=(P((*DP, *TENSOR), None), P(TENSOR, DP)),
        check_vma=False,
    )
```

```python
import functools

import jax
import jax.numpy as jnp
import numpy as np
from jax import lax
from jax.experimental import pallas as pl
from jax.experimental.pallas import tpu as pltpu
from jax.sharding import Mesh, PartitionSpec as P

BF16 = jnp.bfloat16
F32 = jnp.float32
DP = ("zh", "c")
TENSOR = ("zl", "y", "x")
NZ, NY, NX = 4, 8, 4
ROWS = 4
HALF = NX * NY * ROWS
D = 4096
HID = 256
FEATS = 512
STEPS = D // FEATS
PIECE = 2 * NY * ROWS


def contract(a, b, ca, cb):
    return lax.dot_general(a, b, (((ca,), (cb,)), ((), ())), preferred_element_type=F32)


def swap(value, axis):
    return lax.ppermute(value, axis, [(0, 1), (1, 0)])


def shift(value, axis, k):
    n = lax.axis_size(axis)
    return lax.ppermute(value, axis, [(i, (i + k) % n) for i in range(n)])


def neighbours(value):
    at = lambda zh, c, zl: ((zh % NZ) * 2 + c) * 2 + zl
    pairs = []
    for zh in range(NZ):
        pairs += [(at(zh, 0, 0), at(zh, 0, 1)), (at(zh, 0, 1), at(zh, 0, 0))]
        pairs += [(at(zh, 1, 1), at(zh + 1, 1, 0)), (at(zh + 1, 1, 0), at(zh, 1, 1))]
    return lax.ppermute(value, ("zh", "c", "zl"), pairs)


def split_body(where, pick, r0, r1, r2a, r2b, r3, tok, cot):
    n = NY * ROWS
    r2 = jnp.concatenate([r2a[...], r2b[...]], axis=0)
    for i, piece in enumerate((r0[...], r1[...], r2, r3[...])):
        rows = contract(pick[...], piece, 1, 0).astype(BF16)
        tok[i * n : (i + 1) * n] = rows[:n]
        for k in range(2):
            cot[0, flip(k, where[0]), i * n : (i + 1) * n] = rows[n:, k * FEATS : (k + 1) * FEATS]


def split(where, pieces):
    piece = pl.BlockSpec((PIECE, 2 * FEATS), lambda j, s: (0, j))
    part = pl.BlockSpec((PIECE // 2, 2 * FEATS), lambda j, s: (0, j))
    return pl.pallas_call(
        split_body,
        grid_spec=pltpu.PrefetchScalarGridSpec(
            num_scalar_prefetch=1,
            grid=(NZ,),
            in_specs=[pl.BlockSpec((PIECE, PIECE), lambda j, s: (0, 0)), piece, piece, part, part, piece],
            out_specs=[
                pl.BlockSpec((HALF, 2 * FEATS), lambda j, s: (0, j)),
                pl.BlockSpec((1, 2, HALF, FEATS), lambda j, s: (j, 0, 0, 0)),
            ],
        ),
        out_shape=[
            hbm((HALF, D), BF16),
            hbm((NZ, 2, HALF, FEATS), BF16),
        ],
        compiler_params=pltpu.CompilerParams(vmem_limit_bytes=32 * 2**20),
        name="split",
    )(where, selection((NY, 2, ROWS), (1, 0, 2)), *pieces)


def hbm(shape, dtype):
    return pltpu.MemorySpace.HBM(shape, dtype)


def pinned(*values):
    return [pltpu.with_memory_space_constraint(v, pltpu.MemorySpace.HBM) for v in values]


def flip(a, b):
    return a + b - 2 * a * b


def gates_body(where, tok, gw, uw, mw, ow, hid, fac, acc):
    step = pl.program_id(0)

    @pl.when(step == 0)
    def _():
        acc[...] = jnp.zeros_like(acc)

    t = tok[...]
    for i, w in enumerate((gw, uw, mw, ow)):
        acc[:, i * HID : (i + 1) * HID] += contract(t, w[...], 1, 0)

    @pl.when(step == STEPS // 4 - 1)
    def _():
        first = where[0] == 0
        pm, po = acc[:, 2 * HID : 3 * HID], acc[:, 3 * HID :]
        sides = (
            (acc[:, :HID], acc[:, HID : 2 * HID]),
            (jnp.where(first, pm, po), jnp.where(first, po, pm)),
        )
        for i, (gate, up) in enumerate(sides):
            sigma = jax.nn.sigmoid(gate)
            silu = gate * sigma
            hid[:, i * HID : (i + 1) * HID] = (silu * up).astype(BF16)
            slope = up * sigma * (1.0 + gate * (1.0 - sigma))
            if i == 1:
                slope, silu = jnp.where(first, slope, silu), jnp.where(first, silu, slope)
            fac[:, 2 * i * HID : (2 * i + 1) * HID] = slope
            fac[:, (2 * i + 1) * HID : (2 * i + 2) * HID] = silu


def gates(where, tok, gw, uw, mw, ow):
    weight = pl.BlockSpec((4 * FEATS, HID), lambda j, s: (j, 0))
    return pl.pallas_call(
        gates_body,
        grid_spec=pltpu.PrefetchScalarGridSpec(
            num_scalar_prefetch=1,
            grid=(STEPS // 4,),
            in_specs=[pl.BlockSpec((HALF, 4 * FEATS), lambda j, s: (0, j))] + [weight] * 4,
            out_specs=[
                pl.BlockSpec((HALF, 2 * HID), lambda j, s: (0, 0)),
                pl.BlockSpec((HALF, 4 * HID), lambda j, s: (0, 0)),
            ],
            scratch_shapes=[pltpu.VMEM((HALF, 4 * HID), F32)],
        ),
        out_shape=[
            jax.ShapeDtypeStruct((HALF, 2 * HID), BF16),
            hbm((HALF, 4 * HID), F32),
        ],
        compiler_params=pltpu.CompilerParams(vmem_limit_bytes=32 * 2**20),
        name="gates",
    )(where, *pinned(tok, gw, uw, mw), ow)


def down_body(where, cot, dn, df, fac, dd, acc):
    step = pl.program_id(0)

    @pl.when(step == 0)
    def _():
        acc[...] = jnp.zeros_like(acc)

    for z in range(2):
        acc[...] += contract(cot[z, 0], dn[z], 1, 1) + contract(cot[z, 1], df[z], 1, 1)

    @pl.when(step == NZ // 2 - 1)
    def _():
        low = where[1] == 0
        dl, dh = acc[:, :HID], acc[:, HID:]
        for i, d_hidden in enumerate((jnp.where(low, dl, dh), jnp.where(low, dh, dl))):
            for k in (2 * i, 2 * i + 1):
                dd[:, k * HID : (k + 1) * HID] = (d_hidden * fac[:, k * HID : (k + 1) * HID]).astype(BF16)


def down(where, cot, dn, df, fac):
    plane = pl.BlockSpec((2, 2 * HID, FEATS), lambda j, s: (j, 0, 0))
    block = pl.BlockSpec((HALF, 4 * HID), lambda j, s: (0, 0))
    return pl.pallas_call(
        down_body,
        grid_spec=pltpu.PrefetchScalarGridSpec(
            num_scalar_prefetch=1,
            grid=(NZ // 2,),
            in_specs=[pl.BlockSpec((2, 2, HALF, FEATS), lambda j, s: (j, 0, 0, 0)), plane, plane, block],
            out_specs=block,
            scratch_shapes=[pltpu.VMEM((HALF, 2 * HID), F32)],
        ),
        out_shape=jax.ShapeDtypeStruct((HALF, 4 * HID), BF16),
        compiler_params=pltpu.CompilerParams(vmem_limit_bytes=32 * 2**20),
        name="down",
    )(where, *pinned(cot, dn), df, *pinned(fac))


def term_body(where, pick, dd, *refs):
    weights, out = refs[:-1], refs[-1]
    halves = []
    for h in range(2):
        total = None
        for i, w in enumerate(weights[h::2]):
            part = contract(dd[:, i * HID : (i + 1) * HID], w[...], 1, 1)
            total = part if total is None else total + part
        halves.append(total.astype(BF16))
    rows = contract(pick[...], jnp.concatenate(halves, axis=0), 1, 0).astype(BF16)
    for i in range(NX):
        out[(where[2] + NX - i) % NX] = rows[i * PIECE : (i + 1) * PIECE]


def term(where, dd, gw, uw, mw, ow):
    low = pl.BlockSpec((2 * FEATS, HID), lambda j, s: (j, 0))
    high = pl.BlockSpec((2 * FEATS, HID), lambda j, s: (j + 2, 0))
    gw, uw, mw = pinned(gw, uw, mw)
    return pl.pallas_call(
        term_body,
        grid_spec=pltpu.PrefetchScalarGridSpec(
            num_scalar_prefetch=1,
            grid=(STEPS // 4,),
            in_specs=[
                pl.BlockSpec((2 * HALF, 2 * HALF), lambda j, s: (0, 0)),
                pl.BlockSpec((HALF, 4 * HID), lambda j, s: (0, 0)),
            ]
            + [low, high] * 4,
            out_specs=pl.BlockSpec((NX, PIECE, 2 * FEATS), lambda j, s: (0, 0, j)),
        ),
        out_shape=hbm((NX, PIECE, D // 2), BF16),
        compiler_params=pltpu.CompilerParams(vmem_limit_bytes=32 * 2**20),
        name="term",
    )(where, merge(), dd, gw, gw, uw, uw, mw, mw, ow, ow)


def grads_body(where, h, cn, cf, keep, send):
    total, core = None, where[0]
    for z in range(NZ):
        part = contract(h[z, core], cn[z, 0], 0, 0) + contract(h[z, 1 - core], cf[z], 0, 0)
        total = part if total is None else total + part
    keep[...] = total[:HID]
    send[...] = total[HID:].astype(BF16)


def grads(where, hidden, cot_near, cot_far):
    vmem = pl.BlockSpec(memory_space=pltpu.MemorySpace.VMEM)
    return pl.pallas_call(
        grads_body,
        in_specs=[pl.BlockSpec(memory_space=pltpu.MemorySpace.SMEM)] + [vmem] * 3,
        out_specs=[vmem] * 2,
        out_shape=[
            jax.ShapeDtypeStruct((HID, FEATS), F32),
            jax.ShapeDtypeStruct((HID, FEATS), BF16),
        ],
        compiler_params=pltpu.CompilerParams(vmem_limit_bytes=32 * 2**20),
        name="grads",
    )(where, hidden, cot_near, cot_far)


def selection(shape, order):
    source = np.arange(np.prod(shape)).reshape(shape).transpose(order).reshape(-1)
    return jnp.asarray(np.eye(source.size, dtype=np.float32)[source], BF16)


def merge():
    return selection((2, NX, NY, ROWS), (1, 2, 0, 3))


def spread(block, axis):
    n = lax.axis_size(axis)
    return lax.all_to_all(jnp.broadcast_to(block[None], (n, *block.shape)), axis, 0, 0)


def on_device(tokens, cotangent, gate_weight, up_weight, down_weight):
    core = lax.axis_index("c")
    where = jnp.stack([core, lax.axis_index("zl"), lax.axis_index("x")]).astype(jnp.int32)

    picked = jnp.where(core == 0, gate_weight, up_weight)
    picked, tokens = lax.optimization_barrier((picked, tokens))
    mine = neighbours(picked)
    down_near = lax.all_gather(down_weight, ("zh", "zl"), axis=0).reshape(NZ, 2 * HID, FEATS)

    block = spread(jnp.concatenate([tokens, cotangent], axis=0), "y").reshape(PIECE, D)
    left, right = shift(block, "x", 1), shift(block, "x", -1)
    n = PIECE // 2
    pieces = (block, left, shift(left[:n], "x", 1), shift(right[n:], "x", -1), right)

    tok, cot = split(where, pieces)
    cot_near = lax.all_to_all(cot, "zh", 0, 0)
    tok, mine, down_near = lax.optimization_barrier((tok, mine, down_near))
    other, down_far = swap(mine, "c"), swap(down_near, "c")
    hidden, factors = gates(where, tok, gate_weight, up_weight, mine, other)
    hidden = lax.all_gather(hidden, DP, axis=0).reshape(NZ, 2, HALF, 2 * HID)
    dd = down(where, cot, down_near, down_far, factors)

    parts = term(where, dd, gate_weight, up_weight, mine, other)
    parts = lax.all_to_all(parts.reshape(NX * NY, 2 * ROWS, D // 2), ("x", "y"), 0, 0)
    hidden, cot_near = lax.optimization_barrier((hidden, cot_near))
    keep, send = grads(where, hidden, cot_near, swap(cot_near[:, 1], "c"))
    parts, received = lax.optimization_barrier((parts, swap(send, "zl")))
    total = jnp.sum(parts.astype(F32), axis=0).astype(BF16)
    input_grad = jnp.concatenate([total[:ROWS], total[ROWS:]], axis=1)
    down_grad = keep + received.astype(F32)
    return (input_grad, down_grad)


def solution(mesh):
    fine = Mesh(mesh.devices.reshape(NZ, 2, 2, NY, NX), ("zh", "c", "zl", "y", "x"))
    placed = (
        P((*DP, *TENSOR), None),
        P((*DP, *TENSOR), None),
        P(None, TENSOR),
        P(None, TENSOR),
        P(TENSOR, DP),
    )
    return jax.shard_map(
        on_device,
        mesh=fine,
        in_specs=placed,
        out_specs=(P((*DP, *TENSOR), None), P(TENSOR, DP)),
        check_vma=False,
    )
```

```python
import functools

import jax
import jax.numpy as jnp
import numpy as np
from jax import lax
from jax.experimental import pallas as pl
from jax.experimental.pallas import tpu as pltpu
from jax.sharding import Mesh, PartitionSpec as P

BF16 = jnp.bfloat16
F32 = jnp.float32
DP = ("zh", "c")
TENSOR = ("zl", "y", "x")
NZ, NY, NX = 4, 8, 4
ROWS = 4
HALF = NX * NY * ROWS
D = 4096
HID = 256
FEATS = 512
STEPS = D // FEATS
PIECE = 2 * NY * ROWS


def contract(a, b, ca, cb):
    return lax.dot_general(a, b, (((ca,), (cb,)), ((), ())), preferred_element_type=F32)


def swap(value, axis):
    return lax.ppermute(value, axis, [(0, 1), (1, 0)])


def shift(value, axis, k):
    n = lax.axis_size(axis)
    return lax.ppermute(value, axis, [(i, (i + k) % n) for i in range(n)])


def neighbours(value):
    at = lambda zh, c, zl: ((zh % NZ) * 2 + c) * 2 + zl
    pairs = []
    for zh in range(NZ):
        pairs += [(at(zh, 0, 0), at(zh, 0, 1)), (at(zh, 0, 1), at(zh, 0, 0))]
        pairs += [(at(zh, 1, 1), at(zh + 1, 1, 0)), (at(zh + 1, 1, 0), at(zh, 1, 1))]
    return lax.ppermute(value, ("zh", "c", "zl"), pairs)


def split_body(where, pick, r0, r1, r2a, r2b, r3, tok, cot):
    n = NY * ROWS
    r2 = jnp.concatenate([r2a[...], r2b[...]], axis=0)
    for i, piece in enumerate((r0[...], r1[...], r2, r3[...])):
        rows = contract(pick[...], piece, 1, 0).astype(BF16)
        tok[i * n : (i + 1) * n] = rows[:n]
        for k in range(4):
            cot[k // 2, flip(k % 2, where[0]), i * n : (i + 1) * n] = rows[n:, k * FEATS : (k + 1) * FEATS]


def split(where, pieces):
    piece = pl.BlockSpec((PIECE, 4 * FEATS), lambda j, s: (0, j))
    part = pl.BlockSpec((PIECE // 2, 4 * FEATS), lambda j, s: (0, j))
    return pl.pallas_call(
        split_body,
        grid_spec=pltpu.PrefetchScalarGridSpec(
            num_scalar_prefetch=1,
            grid=(NZ // 2,),
            in_specs=[pl.BlockSpec((PIECE, PIECE), lambda j, s: (0, 0)), piece, piece, part, part, piece],
            out_specs=[
                pl.BlockSpec((HALF, 4 * FEATS), lambda j, s: (0, j)),
                pl.BlockSpec((2, 2, HALF, FEATS), lambda j, s: (j, 0, 0, 0)),
            ],
        ),
        out_shape=[
            hbm((HALF, D), BF16),
            hbm((NZ, 2, HALF, FEATS), BF16),
        ],
        compiler_params=pltpu.CompilerParams(vmem_limit_bytes=32 * 2**20),
        name="split",
    )(where, selection((NY, 2, ROWS), (1, 0, 2)), *pieces)


def hbm(shape, dtype):
    return pltpu.MemorySpace.HBM(shape, dtype)


def pinned(*values):
    return [pltpu.with_memory_space_constraint(v, pltpu.MemorySpace.HBM) for v in values]


def flip(a, b):
    return a + b - 2 * a * b


def gates_body(where, tok, gw, uw, mw, ow, hid, fac, acc):
    step = pl.program_id(0)

    @pl.when(step == 0)
    def _():
        acc[...] = jnp.zeros_like(acc)

    t = tok[...]
    for i, w in enumerate((gw, uw, mw, ow)):
        acc[:, i * HID : (i + 1) * HID] += contract(t, w[...], 1, 0)

    @pl.when(step == STEPS // 4 - 1)
    def _():
        first = where[0] == 0
        pm, po = acc[:, 2 * HID : 3 * HID], acc[:, 3 * HID :]
        sides = (
            (acc[:, :HID], acc[:, HID : 2 * HID]),
            (jnp.where(first, pm, po), jnp.where(first, po, pm)),
        )
        for i, (gate, up) in enumerate(sides):
            sigma = jax.nn.sigmoid(gate)
            silu = gate * sigma
            hid[:, i * HID : (i + 1) * HID] = (silu * up).astype(BF16)
            slope = up * sigma * (1.0 + gate * (1.0 - sigma))
            if i == 1:
                slope, silu = jnp.where(first, slope, silu), jnp.where(first, silu, slope)
            fac[:, 2 * i * HID : (2 * i + 1) * HID] = slope
            fac[:, (2 * i + 1) * HID : (2 * i + 2) * HID] = silu


def gates(where, tok, gw, uw, mw, ow):
    weight = pl.BlockSpec((4 * FEATS, HID), lambda j, s: (j, 0))
    return pl.pallas_call(
        gates_body,
        grid_spec=pltpu.PrefetchScalarGridSpec(
            num_scalar_prefetch=1,
            grid=(STEPS // 4,),
            in_specs=[pl.BlockSpec((HALF, 4 * FEATS), lambda j, s: (0, j))] + [weight] * 4,
            out_specs=[
                pl.BlockSpec((HALF, 2 * HID), lambda j, s: (0, 0)),
                pl.BlockSpec((HALF, 4 * HID), lambda j, s: (0, 0)),
            ],
            scratch_shapes=[pltpu.VMEM((HALF, 4 * HID), F32)],
        ),
        out_shape=[
            jax.ShapeDtypeStruct((HALF, 2 * HID), BF16),
            hbm((HALF, 4 * HID), F32),
        ],
        compiler_params=pltpu.CompilerParams(vmem_limit_bytes=32 * 2**20),
        name="gates",
    )(where, *pinned(tok, gw, uw, mw), ow)


def down_body(where, cot, dn, df, fac, dd, acc):
    step = pl.program_id(0)

    @pl.when(step == 0)
    def _():
        acc[...] = jnp.zeros_like(acc)

    for z in range(2):
        acc[...] += contract(cot[z, 0], dn[z], 1, 1) + contract(cot[z, 1], df[z], 1, 1)

    @pl.when(step == NZ // 2 - 1)
    def _():
        low = where[1] == 0
        dl, dh = acc[:, :HID], acc[:, HID:]
        for i, d_hidden in enumerate((jnp.where(low, dl, dh), jnp.where(low, dh, dl))):
            for k in (2 * i, 2 * i + 1):
                dd[:, k * HID : (k + 1) * HID] = (d_hidden * fac[:, k * HID : (k + 1) * HID]).astype(BF16)


def down(where, cot, dn, df, fac):
    plane = pl.BlockSpec((2, 2 * HID, FEATS), lambda j, s: (j, 0, 0))
    block = pl.BlockSpec((HALF, 4 * HID), lambda j, s: (0, 0))
    return pl.pallas_call(
        down_body,
        grid_spec=pltpu.PrefetchScalarGridSpec(
            num_scalar_prefetch=1,
            grid=(NZ // 2,),
            in_specs=[pl.BlockSpec((2, 2, HALF, FEATS), lambda j, s: (j, 0, 0, 0)), plane, plane, block],
            out_specs=block,
            scratch_shapes=[pltpu.VMEM((HALF, 2 * HID), F32)],
        ),
        out_shape=jax.ShapeDtypeStruct((HALF, 4 * HID), BF16),
        compiler_params=pltpu.CompilerParams(vmem_limit_bytes=32 * 2**20),
        name="down",
    )(where, *pinned(cot, dn), df, *pinned(fac))


def term_body(where, pick, dd, *refs):
    weights, out = refs[:-1], refs[-1]
    halves = []
    for h in range(2):
        total = None
        for i, w in enumerate(weights[h::2]):
            part = contract(dd[:, i * HID : (i + 1) * HID], w[...], 1, 1)
            total = part if total is None else total + part
        halves.append(total.astype(BF16))
    rows = contract(pick[...], jnp.concatenate(halves, axis=0), 1, 0).astype(BF16)
    for i in range(NX):
        out[(where[2] + NX - i) % NX] = rows[i * PIECE : (i + 1) * PIECE]


def term(where, dd, gw, uw, mw, ow):
    low = pl.BlockSpec((2 * FEATS, HID), lambda j, s: (j, 0))
    high = pl.BlockSpec((2 * FEATS, HID), lambda j, s: (j + 2, 0))
    gw, uw, mw = pinned(gw, uw, mw)
    return pl.pallas_call(
        term_body,
        grid_spec=pltpu.PrefetchScalarGridSpec(
            num_scalar_prefetch=1,
            grid=(STEPS // 4,),
            in_specs=[
                pl.BlockSpec((2 * HALF, 2 * HALF), lambda j, s: (0, 0)),
                pl.BlockSpec((HALF, 4 * HID), lambda j, s: (0, 0)),
            ]
            + [low, high] * 4,
            out_specs=pl.BlockSpec((NX, PIECE, 2 * FEATS), lambda j, s: (0, 0, j)),
        ),
        out_shape=hbm((NX, PIECE, D // 2), BF16),
        compiler_params=pltpu.CompilerParams(vmem_limit_bytes=32 * 2**20),
        name="term",
    )(where, merge(), dd, gw, gw, uw, uw, mw, mw, ow, ow)


def grads_body(where, h, cn, cf, keep, send):
    total, core = None, where[0]
    for z in range(NZ):
        part = contract(h[z, core], cn[z, 0], 0, 0) + contract(h[z, 1 - core], cf[z], 0, 0)
        total = part if total is None else total + part
    keep[...] = total[:HID]
    send[...] = total[HID:].astype(BF16)


def grads(where, hidden, cot_near, cot_far):
    vmem = pl.BlockSpec(memory_space=pltpu.MemorySpace.VMEM)
    return pl.pallas_call(
        grads_body,
        in_specs=[pl.BlockSpec(memory_space=pltpu.MemorySpace.SMEM)] + [vmem] * 3,
        out_specs=[vmem] * 2,
        out_shape=[
            jax.ShapeDtypeStruct((HID, FEATS), F32),
            jax.ShapeDtypeStruct((HID, FEATS), BF16),
        ],
        compiler_params=pltpu.CompilerParams(vmem_limit_bytes=32 * 2**20),
        name="grads",
    )(where, hidden, cot_near, cot_far)


def selection(shape, order):
    source = np.arange(np.prod(shape)).reshape(shape).transpose(order).reshape(-1)
    return jnp.asarray(np.eye(source.size, dtype=np.float32)[source], BF16)


def merge():
    return selection((2, NX, NY, ROWS), (1, 2, 0, 3))


def spread(block, axis):
    n = lax.axis_size(axis)
    return lax.all_to_all(jnp.broadcast_to(block[None], (n, *block.shape)), axis, 0, 0)


def on_device(tokens, cotangent, gate_weight, up_weight, down_weight):
    core = lax.axis_index("c")
    where = jnp.stack([core, lax.axis_index("zl"), lax.axis_index("x")]).astype(jnp.int32)

    picked = jnp.where(core == 0, gate_weight, up_weight)
    picked, tokens = lax.optimization_barrier((picked, tokens))
    mine = neighbours(picked)
    down_near = lax.all_gather(down_weight, ("zh", "zl"), axis=0).reshape(NZ, 2 * HID, FEATS)

    block = spread(jnp.concatenate([tokens, cotangent], axis=0), "y").reshape(PIECE, D)
    left, right = shift(block, "x", 1), shift(block, "x", -1)
    n = PIECE // 2
    pieces = (block, left, shift(left[:n], "x", 1), shift(right[n:], "x", -1), right)

    tok, cot = split(where, pieces)
    cot_near = lax.all_to_all(cot, "zh", 0, 0)
    tok, mine, down_near = lax.optimization_barrier((tok, mine, down_near))
    other, down_far = swap(mine, "c"), swap(down_near, "c")
    hidden, factors = gates(where, tok, gate_weight, up_weight, mine, other)
    hidden = lax.all_gather(hidden, DP, axis=0).reshape(NZ, 2, HALF, 2 * HID)
    dd = down(where, cot, down_near, down_far, factors)

    parts = term(where, dd, gate_weight, up_weight, mine, other)
    parts = lax.all_to_all(parts.reshape(NX * NY, 2 * ROWS, D // 2), ("x", "y"), 0, 0)
    hidden, cot_near = lax.optimization_barrier((hidden, cot_near))
    keep, send = grads(where, hidden, cot_near, swap(cot_near[:, 1], "c"))
    parts, received = lax.optimization_barrier((parts, swap(send, "zl")))
    total = jnp.sum(parts.astype(F32), axis=0).astype(BF16)
    input_grad = jnp.concatenate([total[:ROWS], total[ROWS:]], axis=1)
    down_grad = keep + received.astype(F32)
    return (input_grad, down_grad)


def solution(mesh):
    fine = Mesh(mesh.devices.reshape(NZ, 2, 2, NY, NX), ("zh", "c", "zl", "y", "x"))
    placed = (
        P((*DP, *TENSOR), None),
        P((*DP, *TENSOR), None),
        P(None, TENSOR),
        P(None, TENSOR),
        P(TENSOR, DP),
    )
    return jax.shard_map(
        on_device,
        mesh=fine,
        in_specs=placed,
        out_specs=(P((*DP, *TENSOR), None), P(TENSOR, DP)),
        check_vma=False,
    )
```
